32 devices in a mesh: dp: 8 (over y, x, core), mp: 4 (over z).
Axes of the slice: x: 2, y: 2, z: 4, core: 2. Of those that a mesh axis runs over, the one named last changes fastest.
Arguments:
- activations: bfloat16 [128, 288, 768], P(('dp', 'mp')), may hold values from -2.5 to 2.5
- cotangent: bfloat16 [128, 288, 768], P(('dp', 'mp')), may hold values from -2.5 to 2.5
- segments: int32 [128, 288], P('dp'), may hold values from 0 to 2, never falling along the last dimension, each value on 1 to 160 neighbouring positions
- triple_weight: bfloat16 [3, 768, 768], P(None, None, 'mp'), may hold values from -0.21875 to 0.21875
- query_value_bias: bfloat16 [2, 12, 64], P(None, 'mp'), may hold values from -1.5 to 1.5
- output_weight: bfloat16 [768, 768], P('mp'), may hold values from -0.875 to 0.875
- expand_weight: bfloat16 [768, 3072], P(None, 'mp'), may hold values from -0.21875 to 0.21875
- expand_bias: bfloat16 [48, 64], P('mp'), may hold values from -1.5 to 1.5
- shrink_weight: bfloat16 [3072, 768], P('mp'), may hold values from -0.109375 to 0.109375
- vector_params: bfloat16 [6, 768], replicated
- triple_master: float32 [3, 768, 768], P(None, 'dp', 'mp'), may hold values from -0.21875 to 0.21875
- triple_first: float32 [3, 768, 768], P(None, 'dp', 'mp'), may hold values from -144 to 144
- triple_second: float32 [3, 768, 768], P(None, 'dp', 'mp'), may hold values from 2211.84 to 8847.36
- query_value_master: float32 [2, 12, 64], P(None, 'mp', 'dp'), may hold values from -1.5 to 1.5
- query_value_first: float32 [2, 12, 64], P(None, 'mp', 'dp'), may hold values from -192 to 192
- query_value_second: float32 [2, 12, 64], P(None, 'mp', 'dp'), may hold values from 3944.448 to 15851.52
- output_master: float32 [768, 768], P('mp', 'dp'), may hold values from -0.875 to 0.875
- output_first: float32 [768, 768], P('mp', 'dp'), may hold values from -57.6 to 57.6
- output_second: float32 [768, 768], P('mp', 'dp'), may hold values from 353.8944 to 1400.832
- expand_master: float32 [768, 3072], P('dp', 'mp'), may hold values from -0.21875 to 0.21875
- expand_first: float32 [768, 3072], P('dp', 'mp'), may hold values from -96 to 96
- expand_second: float32 [768, 3072], P('dp', 'mp'), may hold values from 995.328 to 3944.448
- expand_bias_master: float32 [48, 64], P('mp', 'dp'), may hold values from -1.5 to 1.5
- expand_bias_first: float32 [48, 64], P('mp', 'dp'), may hold values from -96 to 96
- expand_bias_second: float32 [48, 64], P('mp', 'dp'), may hold values from 995.328 to 3944.448
- shrink_master: float32 [3072, 768], P('mp', 'dp'), may hold values from -0.109375 to 0.109375
- shrink_first: float32 [3072, 768], P('mp', 'dp'), may hold values from -192 to 192
- shrink_second: float32 [3072, 768], P('mp', 'dp'), may hold values from 3944.448 to 15851.52
- vector_master: float32 [6, 768], P(None, ('dp', 'mp'))
- vector_first: float32 [6, 768], P(None, ('dp', 'mp')), may hold values from -384 to 384
- vector_second: float32 [6, 768], P(None, ('dp', 'mp')), may hold values from 15851.52 to 62668.8
Outputs:
- block_output: bfloat16 [128, 288, 768], P(('dp', 'mp'))
- input_grad: float32 [128, 288, 768], P(('dp', 'mp'))
- triple_master_new: float32 [3, 768, 768], P(None, 'dp', 'mp')
- triple_first_new: float32 [3, 768, 768], P(None, 'dp', 'mp')
- triple_second_new: float32 [3, 768, 768], P(None, 'dp', 'mp')
- triple_copy: bfloat16 [3, 768, 768], P(None, 'dp', 'mp')
- query_value_master_new: float32 [2, 12, 64], P(None, 'mp', 'dp')
- query_value_first_new: float32 [2, 12, 64], P(None, 'mp', 'dp')
- query_value_second_new: float32 [2, 12, 64], P(None, 'mp', 'dp')
- query_value_copy: bfloat16 [2, 12, 64], P(None, 'mp', 'dp')
- output_master_new: float32 [768, 768], P('mp', 'dp')
- output_first_new: float32 [768, 768], P('mp', 'dp')
- output_second_new: float32 [768, 768], P('mp', 'dp')
- output_copy: bfloat16 [768, 768], P('mp', 'dp')
- expand_master_new: float32 [768, 3072], P('dp', 'mp')
- expand_first_new: float32 [768, 3072], P('dp', 'mp')
- expand_second_new: float32 [768, 3072], P('dp', 'mp')
- expand_copy: bfloat16 [768, 3072], P('dp', 'mp')
- expand_bias_master_new: float32 [48, 64], P('mp', 'dp')
- expand_bias_first_new: float32 [48, 64], P('mp', 'dp')
- expand_bias_second_new: float32 [48, 64], P('mp', 'dp')
- expand_bias_copy: bfloat16 [48, 64], P('mp', 'dp')
- shrink_master_new: float32 [3072, 768], P('mp', 'dp')
- shrink_first_new: float32 [3072, 768], P('mp', 'dp')
- shrink_second_new: float32 [3072, 768], P('mp', 'dp')
- shrink_copy: bfloat16 [3072, 768], P('mp', 'dp')
- vector_master_new: float32 [6, 768], P(None, ('dp', 'mp'))
- vector_first_new: float32 [6, 768], P(None, ('dp', 'mp'))
- vector_second_new: float32 [6, 768], P(None, ('dp', 'mp'))
- vector_copy: bfloat16 [6, 768], P(None, ('dp', 'mp'))
The draws below stay inside these ranges and needn't reach their ends.
Inputs may be any that keep to these rules, and one draw needn't show every extreme that they name: `segments`: along a row the pair numbers never fall; each pair has 1 to 160 tokens, and each row has one pair of exactly 160.
All inputs are finite; a program needn't handle non-finite values.
Results may differ from the reference program's by a relative error of at most 0.018.
Values may be sent and summed in bfloat16 or wider, within the bound.
A program may use at most 256 MiB of HBM per device.

```python
import math
import jax
import jax.numpy as jnp
import numpy as np
from jax import lax

D = 768
HEADS = 12
HEAD = 64
FF = 3072
L = 288
SEGS = 3
SEG_MOST = 160
STEP = 10
ROWS = 128


def vector_rows(key):
    gains = 1.0 + 0.15 * jax.random.normal(jax.random.fold_in(key, 1), (2, D), jnp.float32)
    gains = jnp.clip(gains, 0.5, 1.5)
    shifts = 0.3 * jax.random.normal(jax.random.fold_in(key, 2), (4, D), jnp.float32)
    shifts = jnp.clip(shifts, -1.5, 1.5)
    return jnp.stack([gains[0], shifts[0], shifts[1], gains[1], shifts[2], shifts[3]])


def draw_vector_params(key, part):
    return vector_rows(jax.random.fold_in(key, 11)).astype(jnp.bfloat16)


def draw_vector_master(key, part):
    return vector_rows(jax.random.fold_in(key, 23))


def block_levels(own_key, dims, shards, least, largest):
    def one(position, shards_of):
        steps = jax.random.uniform(jax.random.fold_in(jax.random.fold_in(own_key, 6), position), (shards_of,), jnp.float32, least / len(shards), largest / len(shards))
        return jnp.repeat(jnp.exp(steps), dims[position] // shards_of).reshape((-1,) + (1,) * (len(dims) - position - 1))

    loudness = one(*shards[0])
    for cut in shards[1:]:
        loudness = loudness * one(*cut)
    return loudness


def profile(number_of, total, bound, slope):
    weights = [(1 << 20) // math.isqrt(rank ** slope) + 1 for rank in range(2, number_of + 1)]
    spare, counts = total - bound - (number_of - 1), [1] * (number_of - 1)
    while spare > 0:
        movable = [i for i in range(number_of - 1) if counts[i] < bound]
        whole, budget = sum([weights[i] for i in movable]), spare
        for i in movable:
            addition = min(bound - counts[i], max(1, budget * weights[i] // whole), spare)
            counts[i] = counts[i] + addition
            spare = spare - addition
    return np.array([bound] + counts)


def ragged(own_key, number_of, total, most, slope):
    if number_of == 2:
        one = jax.random.randint(own_key, (), max(1, total - most), min(most, total - 1) + 1)
        return jnp.stack([one, total - one])
    lengths = jnp.asarray(profile(number_of, total, most, slope), jnp.int32)
    pairs = (number_of - 1) // 2
    donor, sink = lengths[1:1 + 2 * pairs:2], lengths[2:2 + 2 * pairs:2]
    room = jnp.minimum(donor - 1, most - sink)
    moved = jax.random.randint(jax.random.fold_in(own_key, 1), (pairs,), 0, 1 << 20) % (room + 1)
    lengths = lengths.at[1:1 + 2 * pairs:2].set(donor - moved).at[2:2 + 2 * pairs:2].set(sink + moved)
    return lengths[jax.random.permutation(jax.random.fold_in(own_key, 2), number_of)]


def bell_draw(own_key, extent, deviation, reach, split=(), dtype=jnp.bfloat16):
    drawn = jax.random.normal(own_key, extent, jnp.float32) * deviation
    if len(split) > 0:
        drawn = block_levels(own_key, extent, split, -0.22, 0.18) * drawn
    return jnp.clip(drawn, min=-reach, max=reach).astype(dtype)


def setup_inputs(seed: int = 0) -> dict:
    key_of = jax.random.split(jax.random.key(seed), 32)
    return {
        "activations": bell_draw(key_of[0], (ROWS, L, D), 1.0, 2.5, ((0, 32),)),
        "cotangent": bell_draw(key_of[1], (ROWS, L, D), 1.0, 2.5, ((0, 32),)),
        "segments": jax.vmap(lambda own: jnp.searchsorted(jnp.cumsum(ragged(own, SEGS, L, SEG_MOST, 0)), jnp.arange(L), side="right"))(jax.random.split(key_of[2], ROWS)).reshape((ROWS, L)).astype(jnp.int32),
        "triple_weight": bell_draw(key_of[3], (3, D, D), D ** -0.5, 0.21875, ((2, 4),)),
        "query_value_bias": bell_draw(key_of[4], (2, HEADS, HEAD), 0.5, 1.5, ((1, 4),)),
        "output_weight": bell_draw(key_of[5], (D, D), (D // 16) ** -0.5, 0.875, ((0, 4),)),
        "expand_weight": bell_draw(key_of[6], (D, FF), D ** -0.5, 0.21875, ((1, 4),)),
        "expand_bias": bell_draw(key_of[7], (FF // HEAD, HEAD), 0.5, 1.5, ((0, 4),)),
        "shrink_weight": bell_draw(key_of[8], (FF, D), FF ** -0.5, 0.109375, ((0, 4),)),
        "vector_params": draw_vector_params(jax.random.fold_in(key_of[31], 71), 0),
        "triple_master": bell_draw(key_of[10], (3, D, D), D ** -0.5, 0.21875, ((1, 8), (2, 4)), jnp.float32),
        "triple_first": bell_draw(key_of[11], (3, D, D), (0.3 * (ROWS * L) ** 0.5), 144.0, ((1, 8), (2, 4)), jnp.float32),
        "triple_second": jnp.clip(jnp.exp(math.log(8847.36) - 1.3862944 * jax.random.uniform(key_of[12], (3, D, D), jnp.float32) ** block_levels(key_of[12], (3, D, D), ((1, 8), (2, 4)), -0.2, 0.2)), 2211.84, 8847.36),
        "query_value_master": bell_draw(key_of[13], (2, HEADS, HEAD), 0.5, 1.5, ((1, 4), (2, 8)), jnp.float32),
        "query_value_first": bell_draw(key_of[14], (2, HEADS, HEAD), (0.4 * (ROWS * L) ** 0.5), 192.0, ((1, 4), (2, 8)), jnp.float32),
        "query_value_second": jnp.clip(jnp.exp(math.log(15851.52) - 1.39095635 * jax.random.uniform(key_of[15], (2, HEADS, HEAD), jnp.float32) ** block_levels(key_of[15], (2, HEADS, HEAD), ((1, 4), (2, 8)), -0.2, 0.2)), 3944.448, 15851.52),
        "output_master": bell_draw(key_of[16], (D, D), (D // 16) ** -0.5, 0.875, ((0, 4), (1, 8)), jnp.float32),
        "output_first": bell_draw(key_of[17], (D, D), (0.12 * (ROWS * L) ** 0.5), 57.6, ((0, 4), (1, 8)), jnp.float32),
        "output_second": jnp.clip(jnp.exp(math.log(1400.832) - 1.375823 * jax.random.uniform(key_of[18], (D, D), jnp.float32) ** block_levels(key_of[18], (D, D), ((0, 4), (1, 8)), -0.2, 0.2)), 353.8944, 1400.832),
        "expand_master": bell_draw(key_of[19], (D, FF), D ** -0.5, 0.21875, ((0, 8), (1, 4)), jnp.float32),
        "expand_first": bell_draw(key_of[20], (D, FF), (0.2 * (ROWS * L) ** 0.5), 96.0, ((0, 8), (1, 4)), jnp.float32),
        "expand_second": jnp.clip(jnp.exp(math.log(3944.448) - 1.376992 * jax.random.uniform(key_of[21], (D, FF), jnp.float32) ** block_levels(key_of[21], (D, FF), ((0, 8), (1, 4)), -0.2, 0.2)), 995.328, 3944.448),
        "expand_bias_master": bell_draw(key_of[22], (FF // HEAD, HEAD), 0.5, 1.5, ((0, 4), (1, 8)), jnp.float32),
        "expand_bias_first": bell_draw(key_of[23], (FF // HEAD, HEAD), (0.2 * (ROWS * L) ** 0.5), 96.0, ((0, 4), (1, 8)), jnp.float32),
        "expand_bias_second": jnp.clip(jnp.exp(math.log(3944.448) - 1.376992 * jax.random.uniform(key_of[24], (FF // HEAD, HEAD), jnp.float32) ** block_levels(key_of[24], (FF // HEAD, HEAD), ((0, 4), (1, 8)), -0.2, 0.2)), 995.328, 3944.448),
        "shrink_master": bell_draw(key_of[25], (FF, D), FF ** -0.5, 0.109375, ((0, 4), (1, 8)), jnp.float32),
        "shrink_first": bell_draw(key_of[26], (FF, D), (0.4 * (ROWS * L) ** 0.5), 192.0, ((0, 4), (1, 8)), jnp.float32),
        "shrink_second": jnp.clip(jnp.exp(math.log(15851.52) - 1.39095635 * jax.random.uniform(key_of[27], (FF, D), jnp.float32) ** block_levels(key_of[27], (FF, D), ((0, 4), (1, 8)), -0.2, 0.2)), 3944.448, 15851.52),
        "vector_master": draw_vector_master(jax.random.fold_in(key_of[31], 71), 0),
        "vector_first": bell_draw(key_of[29], (6, D), (0.8 * (ROWS * L) ** 0.5), 384.0, ((1, 32),), jnp.float32),
        "vector_second": jnp.clip(jnp.exp(math.log(62668.8) - 1.3745984 * jax.random.uniform(key_of[30], (6, D), jnp.float32) ** block_levels(key_of[30], (6, D), ((1, 32),), -0.2, 0.2)), 15851.52, 62668.8),
    }


NORM_EPS = 1e-05
BETA_ONE = 0.5
BETA_TWO = 0.6
ADAM_EPS = 1e-08
WEIGHT_DECAY = 0.01
MASKED = -1e+30
SQRT_HALF = 0.7071067811865476
highest = lax.Precision.HIGHEST

@jax.custom_vjp
def low(v):
    return lax.optimization_barrier(v.astype(jnp.bfloat16)).astype(jnp.float32)

@jax.custom_vjp
def low_back(v):
    return v

def low_keep(v):
    return (low(v), None)

def low_pass(kept, grad):
    return (grad,)

def back_keep(v):
    return (v, None)

def back_low(kept, grad):
    return (low(grad),)
low.defvjp(low_keep, low_pass)
low_back.defvjp(back_keep, back_low)

def gelu(inputs):
    return 0.5 * inputs * (1.0 + jax.scipy.special.erf(inputs * SQRT_HALF))

def layer_norm(summed, gain, shift):
    centre = summed - lax.optimization_barrier(jnp.mean(summed, axis=-1, keepdims=True))
    variance = lax.optimization_barrier(jnp.mean(centre * centre, axis=-1, keepdims=True))
    return gain * (centre * lax.rsqrt(variance + NORM_EPS)) + shift

def forward(inputs, seg_rows, triple, query_value, output, expand, expand_shift, shrink, vectors):
    group_rows, length = (inputs.shape[0], inputs.shape[1])
    biases = query_value.reshape(2, D)

    def project(which):
        return jnp.einsum('gld,de->gle', inputs, triple[which], precision=highest)

    def shaped(tensor_in):
        return tensor_in.reshape(group_rows, length, HEADS, HEAD)
    queries = low(low_back(project(0) + biases[0]))
    key_rows = low(low_back(project(1)))
    values = low(low_back(project(2) + biases[1]))
    scores = jnp.einsum('gqhc,gkhc->ghqk', shaped(queries), shaped(key_rows), precision=highest) * HEAD ** (-0.5)
    scores = low_back(scores)
    allowed = seg_rows[:, :, None] == seg_rows[:, None, :]
    scores = jnp.where(allowed[:, None], scores, MASKED)
    row_max = lax.optimization_barrier(jnp.max(scores, axis=-1, keepdims=True))
    weights = jnp.exp(scores - row_max)
    probabilities = low(weights / lax.optimization_barrier(jnp.sum(weights, axis=-1, keepdims=True)))
    context = jnp.einsum('ghqk,gkhc->gqhc', probabilities, shaped(values), precision=highest)
    context = low(low_back(context.reshape(group_rows, length, D)))
    attended = jnp.einsum('gle,ed->gld', context, output, precision=highest)
    mixed = inputs + low_back(attended) + vectors[2]
    hidden = layer_norm(mixed, vectors[0], vectors[1])
    expanded = jnp.einsum('gld,df->glf', low(hidden), expand, precision=highest) + expand_shift.reshape(FF)
    active = low(gelu(low_back(expanded)))
    shrunk = jnp.einsum('glf,fd->gld', active, shrink, precision=highest)
    summed = hidden + low_back(shrunk) + vectors[5]
    return layer_norm(summed, vectors[3], vectors[4])

def adam_update(master, first, second, gradient, rate):
    first_new = BETA_ONE * first + (1.0 - BETA_ONE) * gradient
    second_new = BETA_TWO * second + (1.0 - BETA_TWO) * gradient * gradient
    corrected = first_new / (1.0 - BETA_ONE ** STEP)
    spread = jnp.sqrt(second_new / (1.0 - BETA_TWO ** STEP))
    master_new = master - rate * (corrected / (spread + ADAM_EPS) + WEIGHT_DECAY * master)
    return (master_new, first_new, second_new, master_new.astype(jnp.bfloat16))

def reference(activations, cotangent, segments, triple_weight, query_value_bias, output_weight, expand_weight, expand_bias, shrink_weight, vector_params, triple_master, triple_first, triple_second, query_value_master, query_value_first, query_value_second, output_master, output_first, output_second, expand_master, expand_first, expand_second, expand_bias_master, expand_bias_first, expand_bias_second, shrink_master, shrink_first, shrink_second, vector_master, vector_first, vector_second):
    params = tuple((weight_in.astype(jnp.float32) for weight_in in (triple_weight, query_value_bias, output_weight, expand_weight, expand_bias, shrink_weight, vector_params)))
    block_rows = 8
    block_count = activations.shape[0] // block_rows
    inputs = activations.astype(jnp.float32).reshape(block_count, block_rows, L, D)
    backs = cotangent.astype(jnp.float32).reshape(block_count, block_rows, L, D)
    seg_blocks = segments.reshape(block_count, block_rows, L)

    def one_block(totals, block_item):
        inputs_block, back_block, seg_block = block_item

        def run_forward(inputs_here, *parameters):
            return forward(inputs_here, seg_block, *parameters)
        result, pull_back = jax.vjp(run_forward, inputs_block, *params)
        pulled = pull_back(back_block)
        totals = tuple((total + grad_part for total, grad_part in zip(totals, pulled[1:])))
        return (totals, (result.astype(jnp.bfloat16), pulled[0]))
    zeros = tuple((jnp.zeros_like(param_in) for param_in in params))
    totals, (results, input_grads) = lax.scan(one_block, zeros, (inputs, backs, seg_blocks))
    block_output = results.reshape(ROWS, L, D)
    input_grad = input_grads.reshape(ROWS, L, D)
    triple_master_new, triple_first_new, triple_second_new, triple_copy = adam_update(triple_master, triple_first, triple_second, totals[0], D ** (-0.5))
    query_value_master_new, query_value_first_new, query_value_second_new, query_value_copy = adam_update(query_value_master, query_value_first, query_value_second, totals[1], 0.5)
    output_master_new, output_first_new, output_second_new, output_copy = adam_update(output_master, output_first, output_second, totals[2], (D // 16) ** (-0.5))
    expand_master_new, expand_first_new, expand_second_new, expand_copy = adam_update(expand_master, expand_first, expand_second, totals[3], D ** (-0.5))
    expand_bias_master_new, expand_bias_first_new, expand_bias_second_new, expand_bias_copy = adam_update(expand_bias_master, expand_bias_first, expand_bias_second, totals[4], 0.5)
    shrink_master_new, shrink_first_new, shrink_second_new, shrink_copy = adam_update(shrink_master, shrink_first, shrink_second, totals[5], FF ** (-0.5))
    vector_master_new, vector_first_new, vector_second_new, vector_copy = adam_update(vector_master, vector_first, vector_second, totals[6], 0.3)
    return (block_output, input_grad, triple_master_new, triple_first_new, triple_second_new, triple_copy, query_value_master_new, query_value_first_new, query_value_second_new, query_value_copy, output_master_new, output_first_new, output_second_new, output_copy, expand_master_new, expand_first_new, expand_second_new, expand_copy, expand_bias_master_new, expand_bias_first_new, expand_bias_second_new, expand_bias_copy, shrink_master_new, shrink_first_new, shrink_second_new, shrink_copy, vector_master_new, vector_first_new, vector_second_new, vector_copy)
```

```python
import jax
import jax.numpy as jnp
from jax import lax
from jax.sharding import PartitionSpec as P

D = 768
HEAD = 64
FF = 3072
STEP = 10


NORM_EPS = 1e-05
BETA_ONE = 0.5
BETA_TWO = 0.6
ADAM_EPS = 1e-08
WEIGHT_DECAY = 0.01
MASKED = -1e30
SQRT_HALF = 0.7071067811865476
INV_ROOT_TAU = 0.3989422804014327


def norm_forward(summed, gain, shift):
    centre = summed - jnp.mean(summed, axis=-1, keepdims=True)
    scale = lax.rsqrt(jnp.mean(centre * centre, axis=-1, keepdims=True) + NORM_EPS)
    normed = centre * scale
    return (gain * normed + shift, normed, scale)


def norm_backward(gradient, gain, normed, scale):
    scaled = gradient * gain
    centred = scaled - jnp.mean(scaled, axis=-1, keepdims=True)
    return scale * (centred - normed * jnp.mean(scaled * normed, axis=-1, keepdims=True))


def adam_update(master, first, second, gradient, rate):
    first_new = BETA_ONE * first + (1.0 - BETA_ONE) * gradient
    second_new = BETA_TWO * second + (1.0 - BETA_TWO) * gradient * gradient
    corrected = first_new / (1.0 - BETA_ONE**STEP)
    spread = jnp.sqrt(second_new / (1.0 - BETA_TWO**STEP))
    master_new = master - rate * (corrected / (spread + ADAM_EPS) + WEIGHT_DECAY * master)
    return (master_new, first_new, second_new, master_new.astype(jnp.bfloat16))


def gather_weight(shard, rows_axis):
    count = lax.axis_size("dp")
    piece = shard.shape[rows_axis] // count
    own = lax.dynamic_slice_in_dim(shard, lax.axis_index("dp") * piece, piece, rows_axis)
    return own


def mm(a, b, dims):
    return lax.dot_general(a, b, (dims, ((), ())), preferred_element_type=jnp.float32)


def per_device(
    activations,
    cotangent,
    segments,
    triple_weight,
    query_value_bias,
    output_weight,
    expand_weight,
    expand_bias,
    shrink_weight,
    vector_params,
    *state,
):
    rows, length, _ = activations.shape
    tokens = rows * length
    triple = gather_weight(triple_weight, 1)
    triple = lax.all_gather(lax.all_gather(triple, "mp", axis=2, tiled=True), "dp", axis=1, tiled=True)
    output = gather_weight(output_weight, 1)
    output = lax.all_gather(lax.all_gather(output, "mp", axis=0, tiled=True), "dp", axis=1, tiled=True)
    expand = gather_weight(expand_weight, 0)
    expand = lax.all_gather(lax.all_gather(expand, "mp", axis=1, tiled=True), "dp", axis=0, tiled=True)
    shrink = gather_weight(shrink_weight, 1)
    shrink = lax.all_gather(lax.all_gather(shrink, "mp", axis=0, tiled=True), "dp", axis=1, tiled=True)
    biases = lax.all_gather(query_value_bias, "mp", axis=1, tiled=True).reshape(2, D).astype(jnp.float32)
    expand_shift = lax.all_gather(expand_bias, "mp", axis=0, tiled=True).reshape(-1).astype(jnp.float32)
    gains = vector_params.astype(jnp.float32)
    heads = D // HEAD
    seg = lax.dynamic_slice_in_dim(segments, lax.axis_index("mp") * rows, rows, 0)
    allowed = (seg[:, :, None] == seg[:, None, :])[:, None]
    x = activations.reshape(tokens, D)
    back = cotangent.reshape(tokens, D).astype(jnp.float32)

    def split(t):
        return t.reshape(rows, length, heads, HEAD)

    query = (mm(x, triple[0], ((1,), (0,))) + biases[0]).astype(jnp.bfloat16)
    key = mm(x, triple[1], ((1,), (0,))).astype(jnp.bfloat16)
    value = (mm(x, triple[2], ((1,), (0,))) + biases[1]).astype(jnp.bfloat16)
    q4, k4, v4 = split(query), split(key), split(value)
    scores = jnp.einsum("rqhc,rkhc->rhqk", q4, k4, preferred_element_type=jnp.float32) * HEAD ** (-0.5)
    scores = jnp.where(allowed, scores, MASKED)
    row_max = jnp.max(scores, axis=-1, keepdims=True)
    weights = jnp.exp(scores - row_max)
    probs = weights / jnp.sum(weights, axis=-1, keepdims=True)
    probs_low = probs.astype(jnp.bfloat16)
    context = jnp.einsum("rhqk,rkhc->rqhc", probs_low, v4, preferred_element_type=jnp.float32)
    context = context.astype(jnp.bfloat16).reshape(tokens, D)
    attended = mm(context, output, ((1,), (0,)))
    mixed = x.astype(jnp.float32) + attended + gains[2]
    hidden, normed_one, scale_one = norm_forward(mixed, gains[0], gains[1])
    hidden_low = hidden.astype(jnp.bfloat16)
    expanded = mm(hidden_low, expand, ((1,), (0,))) + expand_shift
    cumulative = 0.5 * (1.0 + jax.scipy.special.erf(expanded * SQRT_HALF))
    active = (expanded * cumulative).astype(jnp.bfloat16)
    slope = (cumulative + expanded * jnp.exp(-0.5 * expanded * expanded) * INV_ROOT_TAU).astype(jnp.bfloat16)
    shrunk = mm(active, shrink, ((1,), (0,)))
    summed = hidden + shrunk + gains[5]
    result, normed_two, scale_two = norm_forward(summed, gains[3], gains[4])
    dsummed = norm_backward(back, gains[3], normed_two, scale_two)
    dsummed_low = dsummed.astype(jnp.bfloat16)

    def reduce_grad(part):
        part = part.astype(jnp.bfloat16)
        part = lax.psum_scatter(part, "dp", scatter_dimension=part.ndim - 2, tiled=True)
        return lax.psum_scatter(part, "mp", scatter_dimension=part.ndim - 1, tiled=True).astype(jnp.float32)

    shrink_grad = reduce_grad(mm(dsummed_low, active, ((0,), (0,))))
    dactive = mm(dsummed_low, shrink, ((1,), (1,)))
    dexpanded = (dactive * slope).astype(jnp.bfloat16)
    expand_grad = reduce_grad(mm(hidden_low, dexpanded, ((0,), (0,))))
    dhidden = dsummed + mm(dexpanded, expand, ((1,), (1,)))
    dmixed = norm_backward(dhidden, gains[0], normed_one, scale_one)
    dmixed_low = dmixed.astype(jnp.bfloat16)
    output_grad = reduce_grad(mm(dmixed_low, context, ((0,), (0,))))
    dcontext = split(mm(dmixed_low, output, ((1,), (1,))).astype(jnp.bfloat16))
    dvalue = jnp.einsum("rhqk,rqhc->rkhc", probs_low, dcontext, preferred_element_type=jnp.float32)
    dprobs = jnp.einsum("rqhc,rkhc->rhqk", dcontext, v4, preferred_element_type=jnp.float32)
    inner = jnp.sum(probs * dprobs, axis=-1, keepdims=True)
    dscores = (probs * (dprobs - inner)).astype(jnp.bfloat16)
    dquery = jnp.einsum("rhqk,rkhc->rqhc", dscores, k4, preferred_element_type=jnp.float32) * HEAD ** (-0.5)
    dkey = jnp.einsum("rhqk,rqhc->rkhc", dscores, q4, preferred_element_type=jnp.float32) * HEAD ** (-0.5)
    dthree = [t.astype(jnp.bfloat16).reshape(tokens, D) for t in (dquery, dkey, dvalue)]
    triple_grad = reduce_grad(jnp.stack([mm(x, t, ((0,), (0,))) for t in dthree]))
    input_grad = dmixed
    for j in range(3):
        input_grad = input_grad + mm(dthree[j], triple[j], ((1,), (1,)))

    def total(t):
        return jnp.sum(t.astype(jnp.float32), axis=0)

    vector_grad = jnp.stack([
        total(dhidden * normed_one), total(dhidden), total(dmixed),
        total(back * normed_two), total(back), total(dsummed),
        total(dthree[0]), total(dthree[2]),
    ])
    vector_grad = lax.psum(jnp.concatenate([vector_grad, total(dexpanded).reshape(4, D)]), ("dp", "mp"))
    dp, mp = lax.axis_index("dp"), lax.axis_index("mp")
    groups, parts = lax.axis_size("mp"), lax.axis_size("dp")
    width = D // (groups * parts)
    vec = lax.dynamic_slice_in_dim(vector_grad[:6], (dp * groups + mp) * width, width, 1)
    qv = vector_grad[6:8].reshape(2, heads, HEAD)
    qv = lax.dynamic_slice_in_dim(qv, mp * (heads // groups), heads // groups, 1)
    qv = lax.dynamic_slice_in_dim(qv, dp * (HEAD // parts), HEAD // parts, 2)
    eb = vector_grad[8:].reshape(FF // HEAD, HEAD)
    eb = lax.dynamic_slice_in_dim(eb, mp * (FF // HEAD // groups), FF // HEAD // groups, 0)
    eb = lax.dynamic_slice_in_dim(eb, dp * (HEAD // parts), HEAD // parts, 1)
    grads = (triple_grad, qv, output_grad.T, expand_grad, eb, shrink_grad.T, vec)
    rates = (D ** (-0.5), 0.5, (D // 16) ** (-0.5), D ** (-0.5), 0.5, FF ** (-0.5), 0.3)
    outs = (result.astype(jnp.bfloat16).reshape(activations.shape), input_grad.reshape(activations.shape))
    for i in range(7):
        outs = outs + adam_update(state[3 * i], state[3 * i + 1], state[3 * i + 2], grads[i], rates[i])
    return outs


STATE_SPECS = (
    P(None, "dp", "mp"),
    P(None, "mp", "dp"),
    P("mp", "dp"),
    P("dp", "mp"),
    P("mp", "dp"),
    P("mp", "dp"),
    P(None, ("dp", "mp")),
)


def solution(mesh):
    rows = P(("dp", "mp"), None, None)
    placed = (
        rows,
        rows,
        P("dp", None),
        P(None, None, "mp"),
        P(None, "mp", None),
        P("mp", None),
        P(None, "mp"),
        P("mp", None),
        P("mp", None),
        P(),
    )
    for spec in STATE_SPECS:
        placed = placed + (spec,) * 3
    out_specs = (rows, rows)
    for spec in STATE_SPECS:
        out_specs = out_specs + (spec,) * 4
    return jax.shard_map(per_device, mesh=mesh, in_specs=placed, out_specs=out_specs, check_vma=False)
```

```python
import jax
import jax.numpy as jnp
from jax import lax
from jax.experimental import pallas as pl
from jax.experimental.pallas import tpu as pltpu
from jax.sharding import PartitionSpec as P

D = 768
HEAD = 64
FF = 3072
STEP = 10


NORM_EPS = 1e-05
BETA_ONE = 0.5
BETA_TWO = 0.6
ADAM_EPS = 1e-08
WEIGHT_DECAY = 0.01
MASKED = -1e30
SQRT_HALF = 0.7071067811865476
INV_ROOT_TAU = 0.3989422804014327


def norm_forward(summed, gain, shift):
    centre = summed - jnp.mean(summed, axis=-1, keepdims=True)
    scale = lax.rsqrt(jnp.mean(centre * centre, axis=-1, keepdims=True) + NORM_EPS)
    normed = centre * scale
    return (gain * normed + shift, normed, scale)


def norm_backward(gradient, gain, normed, scale):
    scaled = gradient * gain
    centred = scaled - jnp.mean(scaled, axis=-1, keepdims=True)
    return scale * (centred - normed * jnp.mean(scaled * normed, axis=-1, keepdims=True))


def adam_update(master, first, second, gradient, rate):
    first_new = BETA_ONE * first + (1.0 - BETA_ONE) * gradient
    second_new = BETA_TWO * second + (1.0 - BETA_TWO) * gradient * gradient
    corrected = first_new / (1.0 - BETA_ONE**STEP)
    spread = jnp.sqrt(second_new / (1.0 - BETA_TWO**STEP))
    master_new = master - rate * (corrected / (spread + ADAM_EPS) + WEIGHT_DECAY * master)
    return (master_new, first_new, second_new, master_new.astype(jnp.bfloat16))


MESH = pl.DeviceIdType.MESH
BF = jnp.bfloat16
F32 = jnp.float32
HALF = 48
SLICE = 96
SMALL = 16


def place():
    p, z = lax.axis_index("dp"), lax.axis_index("mp")
    core, xy = p % 2, p // 2
    x, y = xy % 2, xy // 2
    return p, z, core, xy, p + 1 - 2 * core, p + 2 - 4 * x, p + 4 - 8 * y, xy + 1 - 2 * x, xy + 2 - 4 * y


def remote(src, dst, send_sem, recv_sem, p, z):
    return pltpu.make_async_remote_copy(
        src_ref=src, dst_ref=dst, send_sem=send_sem, recv_sem=recv_sem, device_id=(p, z), device_id_type=MESH
    )


def greet(p, z, pc, px, py):
    barrier = pltpu.get_barrier_semaphore()
    for peer in ((pc, z), (px, z), (py, z), (p, (z + 1) % 4), (p, (z + 2) % 4), (p, (z + 3) % 4)):
        pl.semaphore_signal(barrier, inc=1, device_id=peer, device_id_type=MESH)
    pl.semaphore_wait(barrier, 6)


class Gather:
    steps = [(m, d) for m in range(3) for d in (1, 3, 2)]
    sems = [(3,)] + [(3, 3)] * 12 + [(3,)] * 2

    def __init__(self, mats, whole, bias, biases, sems):
        self.mats, self.whole, self.bias, self.biases = mats, whole, bias, biases
        (self.ls, self.zs, self.zr, self.xs, self.xr, self.ys, self.yr, self.as_, self.ar, self.bs, self.br, self.cs,
         self.cr, self.ss, self.sr) = sems
        self.where = place()

    def local(self, m):
        z = self.where[1]
        return pltpu.make_async_copy(self.mats[m], self.whole.at[m, z], self.ls.at[m])

    def small(self, d):
        p, z = self.where[:2]
        return remote(self.bias, self.biases.at[z], self.ss.at[d - 1], self.sr.at[d - 1], p, (z + d) % 4)

    def along_z(self, m, d):
        p, z, core, xy = self.where[:4]
        return remote(self.mats[m].at[xy, core], self.whole.at[m, z, xy, core], self.zs.at[m, d - 1],
                      self.zr.at[m, d - 1], p, (z + d) % 4)

    def plane(self, m, d, block, rows, send_sem, recv_sem, peer):
        z = self.where[1]
        part = self.whole.at[m, (z + 4 - d) % 4, block, self.where[2], rows]
        return remote(part, part, send_sem.at[m, d - 1], recv_sem.at[m, d - 1], peer, z)

    def to_x(self, m, d):
        return self.plane(m, d, self.where[3], slice(None), self.xs, self.xr, self.where[5])

    def to_y(self, m, d):
        return self.plane(m, d, self.where[3], slice(None), self.ys, self.yr, self.where[6])

    def on_to_y(self, m, d):
        return self.plane(m, d, self.where[7], pl.ds(0, HALF), self.as_, self.ar, self.where[6])

    def on_to_x(self, m, d):
        return self.plane(m, d, self.where[8], pl.ds(HALF, HALF), self.bs, self.br, self.where[5])

    def to_core(self, m, d):
        z = self.where[1]
        part = self.whole.at[m, (z + 4 - d) % 4, :, self.where[2]]
        return remote(part, part, self.cs.at[m, d - 1], self.cr.at[m, d - 1], self.where[4], z)

    def begin(self):
        p, z, _, _, pc, px, py = self.where[:7]
        greet(p, z, pc, px, py)
        for d in (1, 3, 2):
            self.small(d).start()
            self.along_z(0, d).start()
        for m in range(3):
            self.local(m).start()
        own = pltpu.make_async_copy(self.bias, self.biases.at[z], self.ls.at[0])
        self.local(0).wait()
        own.start()
        own.wait()
        for d in (1, 2, 3):
            self.small(d).wait_recv()

    def stage(self, i):
        steps, n = self.steps, len(self.steps)
        if i < n:
            m, d = steps[i]
            self.along_z(m, d).wait_recv()
            self.to_x(m, d).start()
            self.to_y(m, d).start()
            if m < 2:
                self.along_z(m + 1, d).start()
        if 0 <= i - 1 < n:
            self.to_x(*steps[i - 1]).wait_recv()
            self.to_y(*steps[i - 1]).wait_recv()
            self.on_to_y(*steps[i - 1]).start()
            self.on_to_x(*steps[i - 1]).start()
        if 0 <= i - 2 < n:
            self.on_to_y(*steps[i - 2]).wait_recv()
            self.on_to_x(*steps[i - 2]).wait_recv()
            self.to_core(*steps[i - 2]).start()
        if 0 <= i - 3 < n:
            self.to_core(*steps[i - 3]).wait_recv()

    def finish(self):
        for m in (1, 2):
            self.local(m).wait()
        for d in (1, 2, 3):
            self.small(d).wait_send()
        for m, d in self.steps:
            for copy in (self.along_z, self.to_x, self.to_y, self.on_to_y, self.on_to_x, self.to_core):
                copy(m, d).wait_send()


def gather_kernel(p_ref, e_ref, s_ref, bias_ref, whole_ref, biases_ref, *sems):
    gather = Gather((p_ref, e_ref, s_ref), whole_ref, bias_ref, biases_ref, sems)
    gather.begin()
    for i in range(len(Gather.steps) + 3):
        gather.stage(i)
    gather.finish()


def gather_weights(mats, bias):
    if lax.axis_size("dp") != 8 or lax.axis_size("mp") != 4:
        whole = jnp.stack([lax.all_gather(m, "mp", axis=0) for m in mats])
        return whole, lax.all_gather(bias, "mp", axis=0)
    hbm = pl.BlockSpec(memory_space=pl.ANY)
    whole, biases = pl.pallas_call(
        gather_kernel,
        out_shape=(jax.ShapeDtypeStruct((3, 4, 4, 2, SLICE, D), BF), jax.ShapeDtypeStruct((4, SMALL, D), BF)),
        in_specs=[hbm] * 4,
        out_specs=(hbm, hbm),
        scratch_shapes=[pltpu.SemaphoreType.DMA(s) for s in Gather.sems],
        compiler_params=pltpu.CompilerParams(collective_id=0, has_side_effects=True),
        name="gather_weights",
    )(*[m.reshape(4, 2, SLICE, D) for m in mats], bias)
    return whole.reshape(3, 4, D, D), biases


class Scatter:
    steps = [(m, k) for m in range(3) for k in range(4)]
    buffers = [((12, 4, SLICE, D), BF)] + [((12, 2, HALF, D), BF)] * 2 + [((12, HALF, D), BF)] * 2 + [
        ((3, 3, SLICE, D), BF), ((3, 4, SLICE, D), BF), ((6, SMALL, D), F32), ((3, SMALL, D), F32)]
    sems = [(12,)] * 2 + [(12, 2)] * 4 + [(12,)] * 4 + [(3, 3)] * 2 + [(6,)] * 2

    def __init__(self, grads, buffers, sems):
        self.grads = grads
        self.sum, self.rx, self.ry, self.ra, self.rb, self.rz, self.plane, self.rv, self.sv = buffers
        (self.cs, self.cr, self.xs, self.xr, self.ys, self.yr, self.as_, self.ar, self.bs, self.br, self.zs, self.zr,
         self.ss, self.sr) = sems
        self.where = place()

    def to_core(self, i):
        m, k = self.steps[i]
        _, z, core, _, pc = self.where[:5]
        return remote(self.grads.at[m, k, :, 1 - core], self.sum.at[i], self.cs.at[i], self.cr.at[i], pc, z)

    def to_x(self, i, t):
        q = (self.where[7], 3 - self.where[3])[t]
        return remote(self.sum.at[i, q, pl.ds(0, HALF)], self.rx.at[i, t], self.xs.at[i, t], self.xr.at[i, t],
                      self.where[5], self.where[1])

    def to_y(self, i, t):
        q = (self.where[8], 3 - self.where[3])[t]
        return remote(self.sum.at[i, q, pl.ds(HALF, HALF)], self.ry.at[i, t], self.ys.at[i, t], self.yr.at[i, t],
                      self.where[6], self.where[1])

    def on_to_y(self, i):
        return remote(self.sum.at[i, self.where[8], pl.ds(0, HALF)], self.ra.at[i], self.as_.at[i], self.ar.at[i],
                      self.where[6], self.where[1])

    def on_to_x(self, i):
        return remote(self.sum.at[i, self.where[7], pl.ds(HALF, HALF)], self.rb.at[i], self.bs.at[i], self.br.at[i],
                      self.where[5], self.where[1])

    def along_z(self, m, d):
        p, z = self.where[:2]
        k = (z + d) % 4
        return remote(self.plane.at[m, k], self.rz.at[m, d - 1], self.zs.at[m, d - 1], self.zr.at[m, d - 1], p, k)

    def begin(self):
        p, z, _, _, pc, px, py = self.where[:7]
        greet(p, z, pc, px, py)

    def stage(self, i):
        n = len(self.steps)
        core, xy, xyx, xyy = self.where[2], self.where[3], self.where[7], self.where[8]
        low, high = slice(0, HALF), slice(HALF, SLICE)
        if i < n:
            self.to_core(i).start()
        j = i - 1
        if 0 <= j < n:
            self.to_core(j).wait_recv()
            m, k = self.steps[j]
            for q in range(4):
                self.sum[j, q] = (self.sum[j, q].astype(F32) + self.grads[m, k, q, core].astype(F32)).astype(BF)
            for t in (0, 1):
                self.to_x(j, t).start()
                self.to_y(j, t).start()
        j = i - 2
        if 0 <= j < n:
            for t in (0, 1):
                self.to_x(j, t).wait_recv()
                self.to_y(j, t).wait_recv()
            self.sum[j, xyy, low] = (self.sum[j, xyy, low].astype(F32) + self.rx[j, 1].astype(F32)).astype(BF)
            self.sum[j, xyx, high] = (self.sum[j, xyx, high].astype(F32) + self.ry[j, 1].astype(F32)).astype(BF)
            self.on_to_y(j).start()
            self.on_to_x(j).start()
        j = i - 3
        if 0 <= j < n:
            m, k = self.steps[j]
            self.on_to_y(j).wait_recv()
            self.on_to_x(j).wait_recv()
            self.plane[m, k, low] = (
                self.sum[j, xy, low].astype(F32) + self.rx[j, 0].astype(F32) + self.ra[j].astype(F32)
            ).astype(BF)
            self.plane[m, k, high] = (
                self.sum[j, xy, high].astype(F32) + self.ry[j, 0].astype(F32) + self.rb[j].astype(F32)
            ).astype(BF)
            if k == 3:
                for d in (1, 2, 3):
                    self.along_z(m, d).start()

    def total(self, m):
        for d in (1, 2, 3):
            self.along_z(m, d).wait_recv()
        own = self.plane[m, self.where[1]].astype(F32)
        return own + self.rz[m, 0].astype(F32) + self.rz[m, 1].astype(F32) + self.rz[m, 2].astype(F32)

    def small_to(self, s, src, p, z):
        return remote(src, self.rv.at[s], self.ss.at[s], self.sr.at[s], p, z)

    def small_copy(self, part, c):
        p, z, _, _, pc, px, py = self.where[:7]
        if c == 0:
            return self.small_to(0, part, pc, z)
        if c == 1:
            return self.small_to(1, self.sv.at[0], px, z)
        if c == 2:
            return self.small_to(2, self.sv.at[1], py, z)
        return self.small_to(c, self.sv.at[2], p, (z + c - 2) % 4)

    def small_stage(self, part, i):
        if i == 0:
            self.small_copy(part, 0).start()
        elif i < 4:
            self.small_copy(part, i - 1).wait_recv()
            before = part[...] if i == 1 else self.sv[i - 2]
            self.sv[i - 1] = before + self.rv[i - 1]
            for c in (i,) if i < 3 else (3, 4, 5):
                self.small_copy(part, c).start()
        else:
            for c in (3, 4, 5):
                self.small_copy(part, c).wait_recv()
            return self.sv[2] + self.rv[3] + self.rv[4] + self.rv[5]

    def finish(self, part):
        for c in range(6):
            self.small_copy(part, c).wait_send()
        for i in range(len(self.steps)):
            self.to_core(i).wait_send()
            self.on_to_y(i).wait_send()
            self.on_to_x(i).wait_send()
            for t in (0, 1):
                self.to_x(i, t).wait_send()
                self.to_y(i, t).wait_send()
        for m in range(3):
            for d in (1, 2, 3):
                self.along_z(m, d).wait_send()


def scatter_kernel(grads_ref, part_ref, out_ref, small_ref, held, load_sem, *rest):
    buffers, sems = rest[: len(Scatter.buffers)], rest[len(Scatter.buffers) :]
    scatter = Scatter(held, buffers, sems)
    n = len(Scatter.steps)

    def load(i):
        m, k = Scatter.steps[i]
        return pltpu.make_async_copy(grads_ref.at[m, k], held.at[m, k], load_sem.at[i])

    scatter.begin()
    for i in range(n):
        load(i).start()
    for i in range(n + 3):
        if i < n:
            load(i).wait()
        scatter.stage(i)
        if i in (0, 2, 4, 6, 8):
            total = scatter.small_stage(part_ref, i // 2)
            if i == 8:
                small_ref[...] = total
    for m in range(3):
        out_ref[m] = scatter.total(m)
    scatter.finish(part_ref)


def scatter_gradients(grads, part):
    if lax.axis_size("dp") != 8 or lax.axis_size("mp") != 4:
        grads = lax.psum_scatter(grads, "dp", scatter_dimension=2, tiled=True)
        grads = lax.psum_scatter(grads, "mp", scatter_dimension=1, tiled=True)
        return grads[:, 0].astype(F32), lax.psum(part, ("dp", "mp"))
    hbm, vmem = pl.BlockSpec(memory_space=pl.ANY), pl.BlockSpec(memory_space=pltpu.VMEM)
    return pl.pallas_call(
        scatter_kernel,
        out_shape=(jax.ShapeDtypeStruct((3, SLICE, D), F32), jax.ShapeDtypeStruct((SMALL, D), F32)),
        in_specs=[hbm, vmem],
        out_specs=(vmem, vmem),
        scratch_shapes=[pltpu.VMEM((3, 4, 4, 2, SLICE, D), BF), pltpu.SemaphoreType.DMA((12,))]
        + [pltpu.VMEM(s, t) for s, t in Scatter.buffers]
        + [pltpu.SemaphoreType.DMA(s) for s in Scatter.sems],
        compiler_params=pltpu.CompilerParams(collective_id=1, has_side_effects=True, vmem_limit_bytes=56 << 20),
        name="scatter_gradients",
    )(grads.reshape(3, 4, 4, 2, SLICE, D), part)


def mm(a, b, dims):
    return lax.dot_general(a, b, (dims, ((), ())), preferred_element_type=jnp.float32)


def pack_weights(triple_weight, output_weight, expand_weight, shrink_weight):
    width = triple_weight.shape[2]
    mixing = jnp.concatenate([triple_weight.transpose(1, 0, 2).reshape(D, 3 * width), output_weight.T], axis=1)
    return mixing, expand_weight, shrink_weight


def pack_biases(query_value_bias, expand_bias):
    pair = query_value_bias.reshape(2, -1)
    width = pair.shape[1]
    none = jnp.zeros((width,), BF)
    first = jnp.concatenate([pair[0], none, pair[1], none])
    return jnp.concatenate([first[None], expand_bias.reshape(1, -1), jnp.zeros((SMALL - 2, D), BF)])


def update_all(state, reduced, sums, activations_shape, outs):
    dp, mp = lax.axis_index("dp"), lax.axis_index("mp")
    groups, parts = lax.axis_size("mp"), lax.axis_size("dp")
    heads = D // HEAD
    width = D // (groups * parts)
    vec = lax.dynamic_slice_in_dim(sums[:6], (dp * groups + mp) * width, width, 1)
    qv = sums[6:8].reshape(2, heads, HEAD)
    qv = lax.dynamic_slice_in_dim(qv, mp * (heads // groups), heads // groups, 1)
    qv = lax.dynamic_slice_in_dim(qv, dp * (HEAD // parts), HEAD // parts, 2)
    eb = sums[8:12].reshape(FF // HEAD, HEAD)
    eb = lax.dynamic_slice_in_dim(eb, mp * (FF // HEAD // groups), FF // HEAD // groups, 0)
    eb = lax.dynamic_slice_in_dim(eb, dp * (HEAD // parts), HEAD // parts, 1)
    cut = 3 * D // groups
    rows = reduced.shape[1]
    triple_grad = reduced[0, :, :cut].reshape(rows, 3, D // groups).transpose(1, 0, 2)
    grads = (triple_grad, qv, reduced[0, :, cut:].T, reduced[1], eb, reduced[2].T, vec)
    rates = (D ** (-0.5), 0.5, (D // 16) ** (-0.5), D ** (-0.5), 0.5, FF ** (-0.5), 0.3)
    for i in range(7):
        outs = outs + adam_update(state[3 * i], state[3 * i + 1], state[3 * i + 2], grads[i], rates[i])
    return outs


def per_device(
    activations,
    cotangent,
    segments,
    triple_weight,
    query_value_bias,
    output_weight,
    expand_weight,
    expand_bias,
    shrink_weight,
    vector_params,
    *state,
):
    rows, length, _ = activations.shape
    tokens = rows * length
    groups = lax.axis_size("mp")
    heads = D // HEAD
    width = D // groups
    mats = pack_weights(triple_weight, output_weight, expand_weight, shrink_weight)
    whole, biases = gather_weights(mats, pack_biases(query_value_bias, expand_bias))
    biases = biases.astype(F32)
    gains = vector_params.astype(jnp.float32)
    seg = lax.dynamic_slice_in_dim(segments, lax.axis_index("mp") * rows, rows, 0)
    allowed = (seg[:, :, None] == seg[:, None, :])[:, None]
    x = activations.reshape(tokens, D)
    back = cotangent.reshape(tokens, D).astype(jnp.float32)
    mixing, expand, shrink = whole[0], whole[1], whole[2]
    triple = mixing[:, :, : 3 * width]
    output = mixing[:, :, 3 * width :]

    proj = jnp.einsum("td,zde->zte", x, triple, preferred_element_type=F32)
    proj = (proj + biases[:, None, 0, : 3 * width]).astype(BF)
    proj = proj.reshape(groups, rows, length, 3, heads // groups, HEAD)
    q4, k4, v4 = (proj[:, :, :, j] for j in range(3))
    scores = jnp.einsum("zrqhc,zrkhc->rzhqk", q4, k4, preferred_element_type=F32) * HEAD ** (-0.5)
    scores = jnp.where(allowed[:, None], scores, MASKED)
    row_max = jnp.max(scores, axis=-1, keepdims=True)
    weights = jnp.exp(scores - row_max)
    probs = weights / jnp.sum(weights, axis=-1, keepdims=True)
    probs_low = probs.astype(BF)
    context = jnp.einsum("rzhqk,zrkhc->zrqhc", probs_low, v4, preferred_element_type=F32)
    context = context.astype(BF).reshape(groups, tokens, width)
    attended = jnp.einsum("zte,zde->td", context, output, preferred_element_type=F32)
    mixed = x.astype(F32) + attended + gains[2]
    hidden, normed_one, scale_one = norm_forward(mixed, gains[0], gains[1])
    hidden_low = hidden.astype(BF)
    expanded = jnp.einsum("td,zdf->ztf", hidden_low, expand, preferred_element_type=F32) + biases[:, None, 1]
    cumulative = 0.5 * (1.0 + jax.scipy.special.erf(expanded * SQRT_HALF))
    active = (expanded * cumulative).astype(BF)
    slope = (cumulative + expanded * jnp.exp(-0.5 * expanded * expanded) * INV_ROOT_TAU).astype(BF)
    shrunk = jnp.einsum("ztf,zfd->td", active, shrink, preferred_element_type=F32)
    summed = hidden + shrunk + gains[5]
    result, normed_two, scale_two = norm_forward(summed, gains[3], gains[4])
    dsummed = norm_backward(back, gains[3], normed_two, scale_two)
    dsummed_low = dsummed.astype(BF)

    shrink_grad = jnp.einsum("td,ztf->zdf", dsummed_low, active, preferred_element_type=F32).astype(BF)
    dactive = jnp.einsum("td,zfd->ztf", dsummed_low, shrink, preferred_element_type=F32)
    dexpanded = (dactive * slope).astype(BF)
    expand_grad = jnp.einsum("td,ztf->zdf", hidden_low, dexpanded, preferred_element_type=F32).astype(BF)
    dhidden = dsummed + jnp.einsum("ztf,zdf->td", dexpanded, expand, preferred_element_type=F32)
    dmixed = norm_backward(dhidden, gains[0], normed_one, scale_one)
    dmixed_low = dmixed.astype(BF)
    output_grad = jnp.einsum("td,zte->zde", dmixed_low, context, preferred_element_type=F32).astype(BF)
    dcontext = jnp.einsum("td,zde->zte", dmixed_low, output, preferred_element_type=F32).astype(BF)
    dcontext = dcontext.reshape(groups, rows, length, heads // groups, HEAD)
    dvalue = jnp.einsum("rzhqk,zrqhc->zrkhc", probs_low, dcontext, preferred_element_type=F32)
    dprobs = jnp.einsum("zrqhc,zrkhc->rzhqk", dcontext, v4, preferred_element_type=F32)
    inner = jnp.sum(probs * dprobs, axis=-1, keepdims=True)
    dscores = (probs * (dprobs - inner)).astype(BF)
    dquery = jnp.einsum("rzhqk,zrkhc->zrqhc", dscores, k4, preferred_element_type=F32) * HEAD ** (-0.5)
    dkey = jnp.einsum("rzhqk,zrqhc->zrkhc", dscores, q4, preferred_element_type=F32) * HEAD ** (-0.5)
    dproj = jnp.stack([dquery, dkey, dvalue], axis=3).astype(BF).reshape(groups, tokens, 3 * width)
    triple_grad = jnp.einsum("td,zte->zde", x, dproj, preferred_element_type=F32).astype(BF)
    input_grad = dmixed + jnp.einsum("zte,zde->td", dproj, triple, preferred_element_type=F32)

    def total(t):
        return jnp.sum(t.astype(F32), axis=0)

    dsum = jnp.sum(dproj.astype(F32), axis=1)
    part = jnp.stack([
        total(dhidden * normed_one), total(dhidden), total(dmixed),
        total(back * normed_two), total(back), total(dsummed),
        dsum[:, :width].reshape(-1), dsum[:, 2 * width :].reshape(-1),
    ])
    part = jnp.concatenate([part, jnp.sum(dexpanded.astype(F32), axis=1), jnp.zeros((SMALL - 12, D), F32)])
    grads = jnp.stack([jnp.concatenate([triple_grad, output_grad], axis=2), expand_grad, shrink_grad])
    reduced, sums = scatter_gradients(grads, part)
    outs = (result.astype(BF).reshape(activations.shape), input_grad.reshape(activations.shape))
    return update_all(state, reduced, sums, activations.shape, outs)


STATE_SPECS = (
    P(None, "dp", "mp"),
    P(None, "mp", "dp"),
    P("mp", "dp"),
    P("dp", "mp"),
    P("mp", "dp"),
    P("mp", "dp"),
    P(None, ("dp", "mp")),
)


def solution(mesh):
    rows = P(("dp", "mp"), None, None)
    placed = (
        rows,
        rows,
        P("dp", None),
        P(None, None, "mp"),
        P(None, "mp", None),
        P("mp", None),
        P(None, "mp"),
        P("mp", None),
        P("mp", None),
        P(),
    )
    for spec in STATE_SPECS:
        placed = placed + (spec,) * 3
    out_specs = (rows, rows)
    for spec in STATE_SPECS:
        out_specs = out_specs + (spec,) * 4
    return jax.shard_map(per_device, mesh=mesh, in_specs=placed, out_specs=out_specs, check_vma=False)
```

```python
import functools

import jax
import jax.numpy as jnp
from jax import lax
from jax.experimental import pallas as pl
from jax.experimental.pallas import tpu as pltpu
from jax.sharding import PartitionSpec as P

D = 768
HEAD = 64
FF = 3072
STEP = 10


NORM_EPS = 1e-05
BETA_ONE = 0.5
BETA_TWO = 0.6
ADAM_EPS = 1e-08
WEIGHT_DECAY = 0.01
MASKED = -1e30
SQRT_HALF = 0.7071067811865476
INV_ROOT_TAU = 0.3989422804014327


def norm_forward(summed, gain, shift):
    centre = summed - jnp.mean(summed, axis=-1, keepdims=True)
    scale = lax.rsqrt(jnp.mean(centre * centre, axis=-1, keepdims=True) + NORM_EPS)
    normed = centre * scale
    return (gain * normed + shift, normed, scale)


def norm_backward(gradient, gain, normed, scale):
    scaled = gradient * gain
    centred = scaled - jnp.mean(scaled, axis=-1, keepdims=True)
    return scale * (centred - normed * jnp.mean(scaled * normed, axis=-1, keepdims=True))


def adam_update(master, first, second, gradient, rate):
    first_new = BETA_ONE * first + (1.0 - BETA_ONE) * gradient
    second_new = BETA_TWO * second + (1.0 - BETA_TWO) * gradient * gradient
    corrected = first_new / (1.0 - BETA_ONE**STEP)
    spread = jnp.sqrt(second_new / (1.0 - BETA_TWO**STEP))
    master_new = master - rate * (corrected / (spread + ADAM_EPS) + WEIGHT_DECAY * master)
    return (master_new, first_new, second_new, master_new.astype(jnp.bfloat16))


MESH = pl.DeviceIdType.MESH
BF = jnp.bfloat16
F32 = jnp.float32
HALF = 48
SLICE = 96
SMALL = 16


def place():
    p, z = lax.axis_index("dp"), lax.axis_index("mp")
    core, xy = p % 2, p // 2
    x, y = xy % 2, xy // 2
    return p, z, core, xy, p + 1 - 2 * core, p + 2 - 4 * x, p + 4 - 8 * y, xy + 1 - 2 * x, xy + 2 - 4 * y


def remote(src, dst, send_sem, recv_sem, p, z):
    return pltpu.make_async_remote_copy(
        src_ref=src, dst_ref=dst, send_sem=send_sem, recv_sem=recv_sem, device_id=(p, z), device_id_type=MESH
    )


def greet(p, z, pc, px, py):
    barrier = pltpu.get_barrier_semaphore()
    for peer in ((pc, z), (px, z), (py, z), (p, (z + 1) % 4), (p, (z + 2) % 4), (p, (z + 3) % 4)):
        pl.semaphore_signal(barrier, inc=1, device_id=peer, device_id_type=MESH)
    pl.semaphore_wait(barrier, 6)


class Gather:
    steps = [(0, 1), (0, 3), (0, 2), (1, 1), (2, 1), (1, 3), (2, 3), (1, 2), (2, 2)]
    sems = [(3,)] + [(3, 3)] * 12 + [(3,)] * 2

    def __init__(self, mats, whole, bias, biases, sems):
        self.mats, self.whole, self.bias, self.biases = mats, whole, bias, biases
        (self.ls, self.zs, self.zr, self.xs, self.xr, self.ys, self.yr, self.as_, self.ar, self.bs, self.br, self.cs,
         self.cr, self.ss, self.sr) = sems
        self.where = place()

    def local(self, m):
        z = self.where[1]
        return pltpu.make_async_copy(self.mats[m], self.whole.at[m, z], self.ls.at[m])

    def small(self, d):
        p, z = self.where[:2]
        return remote(self.bias, self.biases.at[z], self.ss.at[d - 1], self.sr.at[d - 1], p, (z + d) % 4)

    def along_z(self, m, d):
        p, z, core, xy = self.where[:4]
        return remote(self.mats[m].at[xy, core], self.whole.at[m, z, xy, core], self.zs.at[m, d - 1],
                      self.zr.at[m, d - 1], p, (z + d) % 4)

    def plane(self, m, d, block, rows, send_sem, recv_sem, peer):
        z = self.where[1]
        part = self.whole.at[m, (z + 4 - d) % 4, block, self.where[2], rows]
        return remote(part, part, send_sem.at[m, d - 1], recv_sem.at[m, d - 1], peer, z)

    def to_x(self, m, d):
        return self.plane(m, d, self.where[3], slice(None), self.xs, self.xr, self.where[5])

    def to_y(self, m, d):
        return self.plane(m, d, self.where[3], slice(None), self.ys, self.yr, self.where[6])

    def on_to_y(self, m, d):
        return self.plane(m, d, self.where[7], pl.ds(0, HALF), self.as_, self.ar, self.where[6])

    def on_to_x(self, m, d):
        return self.plane(m, d, self.where[8], pl.ds(HALF, HALF), self.bs, self.br, self.where[5])

    def to_core(self, m, d):
        z = self.where[1]
        part = self.whole.at[m, (z + 4 - d) % 4, :, self.where[2]]
        return remote(part, part, self.cs.at[m, d - 1], self.cr.at[m, d - 1], self.where[4], z)

    def begin(self):
        p, z, _, _, pc, px, py = self.where[:7]
        greet(p, z, pc, px, py)
        for d in (1, 3, 2):
            self.small(d).start()
            self.along_z(0, d).start()
        for m in range(3):
            self.local(m).start()
        own = pltpu.make_async_copy(self.bias, self.biases.at[z], self.ls.at[0])
        self.local(0).wait()
        own.start()
        own.wait()
        for d in (1, 2, 3):
            self.small(d).wait_recv()

    def stage(self, i):
        steps, n = self.steps, len(self.steps)
        if i < n:
            m, d = steps[i]
            self.along_z(m, d).wait_recv()
            self.to_x(m, d).start()
            self.to_y(m, d).start()
            if m < 2:
                self.along_z(m + 1, d).start()
        if 0 <= i - 1 < n:
            self.to_x(*steps[i - 1]).wait_recv()
            self.to_y(*steps[i - 1]).wait_recv()
            self.on_to_y(*steps[i - 1]).start()
            self.on_to_x(*steps[i - 1]).start()
        if 0 <= i - 2 < n:
            self.on_to_y(*steps[i - 2]).wait_recv()
            self.on_to_x(*steps[i - 2]).wait_recv()
            self.to_core(*steps[i - 2]).start()
        if 0 <= i - 3 < n:
            self.to_core(*steps[i - 3]).wait_recv()

    def finish(self):
        for d in (1, 2, 3):
            self.small(d).wait_send()
        for m, d in self.steps:
            for copy in (self.along_z, self.to_x, self.to_y, self.on_to_y, self.on_to_x, self.to_core):
                copy(m, d).wait_send()


class Scatter:
    steps = [(m, k) for k in range(4) for m in (2, 1)] + [(0, k) for k in range(4)]
    slots = [k + 4 * j for k in range(4) for j in (0, 1)] + list(range(4))
    buffers = [((12, 4, SLICE, D), BF)] + [((12, 2, HALF, D), BF)] * 2 + [((12, HALF, D), BF)] * 2 + [
        ((3, 3, SLICE, D), BF), ((3, 4, SLICE, D), BF), ((6, SMALL, D), F32), ((3, SMALL, D), F32)]
    sems = [(12,)] * 2 + [(12, 2)] * 4 + [(12,)] * 4 + [(3, 3)] * 2 + [(6,)] * 2

    def __init__(self, grads, buffers, sems):
        self.grads = grads
        self.sum, self.rx, self.ry, self.ra, self.rb, self.rz, self.plane, self.rv, self.sv = buffers
        (self.cs, self.cr, self.xs, self.xr, self.ys, self.yr, self.as_, self.ar, self.bs, self.br, self.zs, self.zr,
         self.ss, self.sr) = sems
        self.where = place()

    def to_core(self, i):
        _, z, core, _, pc = self.where[:5]
        return remote(self.grads.at[self.slots[i], :, 1 - core], self.sum.at[i], self.cs.at[i], self.cr.at[i], pc, z)

    def to_x(self, i, t):
        q = (self.where[7], 3 - self.where[3])[t]
        return remote(self.sum.at[i, q, pl.ds(0, HALF)], self.rx.at[i, t], self.xs.at[i, t], self.xr.at[i, t],
                      self.where[5], self.where[1])

    def to_y(self, i, t):
        q = (self.where[8], 3 - self.where[3])[t]
        return remote(self.sum.at[i, q, pl.ds(HALF, HALF)], self.ry.at[i, t], self.ys.at[i, t], self.yr.at[i, t],
                      self.where[6], self.where[1])

    def on_to_y(self, i):
        return remote(self.sum.at[i, self.where[8], pl.ds(0, HALF)], self.ra.at[i], self.as_.at[i], self.ar.at[i],
                      self.where[6], self.where[1])

    def on_to_x(self, i):
        return remote(self.sum.at[i, self.where[7], pl.ds(HALF, HALF)], self.rb.at[i], self.bs.at[i], self.br.at[i],
                      self.where[5], self.where[1])

    def along_z(self, m, d):
        p, z = self.where[:2]
        k = (z + d) % 4
        return remote(self.plane.at[m, k], self.rz.at[m, d - 1], self.zs.at[m, d - 1], self.zr.at[m, d - 1], p, k)

    def begin(self):
        p, z, _, _, pc, px, py = self.where[:7]
        greet(p, z, pc, px, py)

    def stage(self, i):
        n = len(self.steps)
        core, xy, xyx, xyy = self.where[2], self.where[3], self.where[7], self.where[8]
        low, high = slice(0, HALF), slice(HALF, SLICE)
        if i < n:
            self.to_core(i).start()
        j = i - 1
        if 0 <= j < n:
            self.to_core(j).wait_recv()
            for q in range(4):
                mine = self.grads[self.slots[j], q, core].astype(F32)
                self.sum[j, q] = (self.sum[j, q].astype(F32) + mine).astype(BF)
            for t in (0, 1):
                self.to_x(j, t).start()
                self.to_y(j, t).start()
        j = i - 2
        if 0 <= j < n:
            for t in (0, 1):
                self.to_x(j, t).wait_recv()
                self.to_y(j, t).wait_recv()
            self.sum[j, xyy, low] = (self.sum[j, xyy, low].astype(F32) + self.rx[j, 1].astype(F32)).astype(BF)
            self.sum[j, xyx, high] = (self.sum[j, xyx, high].astype(F32) + self.ry[j, 1].astype(F32)).astype(BF)
            self.on_to_y(j).start()
            self.on_to_x(j).start()
        j = i - 3
        if 0 <= j < n:
            m, k = self.steps[j]
            self.on_to_y(j).wait_recv()
            self.on_to_x(j).wait_recv()
            self.plane[m, k, low] = (
                self.sum[j, xy, low].astype(F32) + self.rx[j, 0].astype(F32) + self.ra[j].astype(F32)
            ).astype(BF)
            self.plane[m, k, high] = (
                self.sum[j, xy, high].astype(F32) + self.ry[j, 0].astype(F32) + self.rb[j].astype(F32)
            ).astype(BF)
            if k == 3:
                for d in (1, 2, 3):
                    self.along_z(m, d).start()

    def total(self, m):
        for d in (1, 2, 3):
            self.along_z(m, d).wait_recv()
        own = self.plane[m, self.where[1]].astype(F32)
        return own + self.rz[m, 0].astype(F32) + self.rz[m, 1].astype(F32) + self.rz[m, 2].astype(F32)

    def small_to(self, s, src, p, z):
        return remote(src, self.rv.at[s], self.ss.at[s], self.sr.at[s], p, z)

    def small_copy(self, part, c):
        p, z, _, _, pc, px, py = self.where[:7]
        if c == 0:
            return self.small_to(0, part, pc, z)
        if c == 1:
            return self.small_to(1, self.sv.at[0], px, z)
        if c == 2:
            return self.small_to(2, self.sv.at[1], py, z)
        return self.small_to(c, self.sv.at[2], p, (z + c - 2) % 4)

    def small_stage(self, part, i):
        if i == 0:
            self.small_copy(part, 0).start()
        elif i < 4:
            self.small_copy(part, i - 1).wait_recv()
            before = part[...] if i == 1 else self.sv[i - 2]
            self.sv[i - 1] = before + self.rv[i - 1]
            for c in (i,) if i < 3 else (3, 4, 5):
                self.small_copy(part, c).start()
        else:
            for c in (3, 4, 5):
                self.small_copy(part, c).wait_recv()
            return self.sv[2] + self.rv[3] + self.rv[4] + self.rv[5]

    def finish(self, part):
        for c in range(6):
            self.small_copy(part, c).wait_send()
        for i in range(len(self.steps)):
            if self.slots[i] not in self.slots[i + 1 :]:
                self.to_core(i).wait_send()
            self.on_to_y(i).wait_send()
            self.on_to_x(i).wait_send()
            for t in (0, 1):
                self.to_x(i, t).wait_send()
                self.to_y(i, t).wait_send()
        for m in range(3):
            for d in (1, 2, 3):
                self.along_z(m, d).wait_send()


def mm(a, b, dims):
    return lax.dot_general(a, b, (dims, ((), ())), preferred_element_type=jnp.float32)


def pack_weights(triple_weight, output_weight, expand_weight, shrink_weight):
    width = triple_weight.shape[2]
    mixing = jnp.concatenate([triple_weight.transpose(1, 0, 2).reshape(D, 3 * width), output_weight.T], axis=1)
    return mixing, expand_weight, shrink_weight


def pack_biases(query_value_bias, expand_bias):
    pair = query_value_bias.reshape(2, -1)
    width = pair.shape[1]
    none = jnp.zeros((width,), BF)
    first = jnp.concatenate([pair[0], none, pair[1], none])
    return jnp.concatenate([first[None], expand_bias.reshape(1, -1), jnp.zeros((SMALL - 2, D), BF)])


TN = ((0,), (0,))
NT = ((1,), (1,))
NN = ((1,), (0,))
CHUNK = 384
STRIP = 128
VMEM_MOST = 60 << 20
FEED_STAGES = {0: ((0, 7), (2, 8)), 1: ((1, 9), (2, 10)), 2: ((1, 11),)}


def square(ref):
    return ref[...].reshape(D, D)


def forward_kernel(fused, rows, length, *refs):
    n_sem = len(Gather.sems) if fused else 0
    n_in = 9 if fused else 7
    x_ref, cot_ref, segr_ref, segc_ref, vec_ref = refs[:5]
    ins = refs[5:n_in]
    n_out = 12
    outs = refs[n_in : n_in + n_out]
    (whole_out, qkv_out, ctx_out, prob_out, act_out, slope_out, normed_out, rstd_out, ds_out, turned_out, result_out,
     part_out) = outs
    rest = refs[n_in + n_out :]
    gather_sems, rest = rest[:n_sem], rest[n_sem:]
    (whole, biases, qkv, ctx, prob, act, slope, mixed, normed, rstd, low, turned, result, part,
     w_sem, qkv_sem, ctx_sem, prob_sem, act_sem, slope_sem, end_sem) = rest
    tokens = rows * length
    strips, chunks = tokens // STRIP, tokens // CHUNK
    z_own = lax.axis_index("mp")
    if fused:
        gather = Gather(ins[:3], whole, ins[3], biases, gather_sems)
        gather.begin()
        stage = gather.stage
        order = [z_own, (z_own + 3) % 4, (z_own + 1) % 4, (z_own + 2) % 4]
    else:
        copy = pltpu.make_async_copy(ins[0], whole, w_sem.at[0])
        copy.start()
        small = pltpu.make_async_copy(ins[1], biases, w_sem.at[1])
        small.start()
        copy.wait()
        small.wait()
        stage = lambda i: None
        order = [0, 1, 2, 3]

    def turn(source, slot):
        @pl.loop(0, strips)
        def _(s):
            at = pl.ds(pl.multiple_of(s * STRIP, STRIP), STRIP)
            turned[slot, :, at] = source[at, :].T

    def turned_copy(slot):
        return pltpu.make_async_copy(turned.at[slot], turned_out.at[slot], end_sem.at[slot])

    attended = mixed
    heads = D // HEAD // 4
    width = heads * HEAD
    for i, z in enumerate(order):
        slot = i % 2
        if i >= 2:
            pltpu.make_async_copy(qkv.at[slot], qkv_out.at[order[i - 2]], qkv_sem.at[slot]).wait()
            pltpu.make_async_copy(ctx.at[slot], ctx_out.at[order[i - 2]], ctx_sem.at[slot]).wait()
        weight = whole.at[0, z]
        bias = biases[z, 0:1, :].astype(F32)

        def project(r, i=i, slot=slot, weight=weight, bias=bias):
            at = pl.ds(pl.multiple_of(r * CHUNK, CHUNK), CHUNK)
            qkv[slot, at, :] = (mm(x_ref[at, :], square(weight), NN) + bias).astype(BF)

        pl.loop(0, chunks)(project)
        pltpu.make_async_copy(qkv.at[slot], qkv_out.at[z], qkv_sem.at[slot]).start()
        if i == 0:
            stage(0)

        def attend(r, i=i, slot=slot, z=z):
            at = pl.ds(pl.multiple_of(r * length, 32), length)
            if i >= 1:
                pltpu.make_async_copy(prob.at[r], prob_out.at[order[i - 1], r], prob_sem.at[r]).wait()
            mask = jnp.where(segc_ref[r] == segr_ref[r], 0.0, MASKED)
            done = []
            for h in range(heads):
                q = qkv[slot, at, h * HEAD : (h + 1) * HEAD] * jnp.asarray(HEAD ** (-0.5), BF)
                k = qkv[slot, at, width + h * HEAD : width + (h + 1) * HEAD]
                v = qkv[slot, at, 2 * width + h * HEAD : 2 * width + (h + 1) * HEAD]
                scores = mm(k, q, NT) + mask
                weights = jnp.exp(scores - jnp.max(scores, axis=0, keepdims=True))
                share = 1.0 / jnp.sum(weights, axis=0, keepdims=True)
                probs = (weights * share).astype(BF)
                prob[r, h] = probs
                done.append(mm(v, probs, TN).astype(BF).T)
            ctx[slot, at, :] = jnp.concatenate(done, axis=1)
            pltpu.make_async_copy(prob.at[r], prob_out.at[z, r], prob_sem.at[r]).start()

        if i == 0:
            for half in (0, 1):
                pl.loop(2 * half, 2 * half + 2)(attend)
                stage(1 + half)
            turn(x_ref, 0)
            turned_copy(0).start()
            stage(3)
        else:
            pl.loop(0, rows)(attend)
            if i < 3:
                stage(3 + i)
        pltpu.make_async_copy(ctx.at[slot], ctx_out.at[z], ctx_sem.at[slot]).start()

        def mix(r, i=i, slot=slot, weight=weight):
            at = pl.ds(pl.multiple_of(r * CHUNK, CHUNK), CHUNK)
            add = mm(ctx[slot, at, :], square(weight)[:, 3 * width :], NT)
            attended[at, :] = add if i == 0 else attended[at, :] + add

        pl.loop(0, chunks)(mix)
    stage(6)
    for m in (0, 1, 2) if fused else ():
        if m:
            gather.local(m).wait()

    @pl.loop(0, strips)
    def _(s):
        at = pl.ds(pl.multiple_of(s * STRIP, STRIP), STRIP)
        summed = x_ref[at, :].astype(F32) + mixed[at, :] + vec_ref[2:3, :]
        hidden, normal, scale = norm_forward(summed, vec_ref[0:1, :], vec_ref[1:2, :])
        normed[at, :] = normal
        rstd[at, :] = jnp.broadcast_to(scale, (STRIP, 128))
        hidden = hidden.astype(BF)
        low[at, :] = hidden
        turned[1, :, at] = hidden.T

    turned_copy(1).start()
    normed_copy = pltpu.make_async_copy(normed, normed_out, end_sem.at[3])
    normed_copy.start()
    rstd_copy = pltpu.make_async_copy(rstd, rstd_out, end_sem.at[4])
    rstd_copy.start()

    shrunk = mixed
    for i, z in enumerate(order):
        def feed(c, i=i, z=z):
            at = pl.ds(pl.multiple_of(c * CHUNK, CHUNK), CHUNK)
            if i >= 1:
                pltpu.make_async_copy(act.at[at, :], act_out.at[order[i - 1], at], act_sem.at[c]).wait()
                pltpu.make_async_copy(slope.at[at, :], slope_out.at[order[i - 1], at], slope_sem.at[c]).wait()
            u = mm(low[at, :], square(whole.at[1, z]), NN) + biases[z, 1:2, :].astype(F32)
            cumulative = 0.5 + 0.5 * lax.erf(u * SQRT_HALF)
            active = (u * cumulative).astype(BF)
            act[at, :] = active
            slope[at, :] = (cumulative + u * jnp.exp(-0.5 * u * u) * INV_ROOT_TAU).astype(BF)
            pltpu.make_async_copy(act.at[at, :], act_out.at[z, at], act_sem.at[c]).start()
            pltpu.make_async_copy(slope.at[at, :], slope_out.at[z, at], slope_sem.at[c]).start()
            add = mm(act[at, :], square(whole.at[2, z]), NN)
            shrunk[at, :] = add if i == 0 else shrunk[at, :] + add
            for after, number in FEED_STAGES.get(i, ()):
                pl.when(c == after)(functools.partial(stage, number))

        pl.loop(0, chunks)(feed)
    whole_copy = pltpu.make_async_copy(whole, whole_out, w_sem.at[0])
    whole_copy.start()

    normed_copy.wait()
    part[...] = jnp.zeros_like(part)

    @pl.loop(0, strips)
    def _(s):
        at = pl.ds(pl.multiple_of(s * STRIP, STRIP), STRIP)
        hidden = vec_ref[0:1, :] * normed[at, :] + vec_ref[1:2, :]
        summed = hidden + shrunk[at, :] + vec_ref[5:6, :]
        block, normal, scale = norm_forward(summed, vec_ref[3:4, :], vec_ref[4:5, :])
        result[at, :] = block.astype(BF)
        back = cot_ref[at, :].astype(F32)
        dsummed = norm_backward(back, vec_ref[3:4, :], normal, scale)
        normed[at, :] = dsummed
        turned[2, :, at] = dsummed.astype(BF).T
        part[3:4, :] += jnp.sum(back * normal, axis=0, keepdims=True)
        part[4:5, :] += jnp.sum(back, axis=0, keepdims=True)
        part[5:6, :] += jnp.sum(dsummed, axis=0, keepdims=True)

    last = [
        turned_copy(2),
        pltpu.make_async_copy(normed, ds_out, end_sem.at[5]),
        pltpu.make_async_copy(result, result_out, end_sem.at[6]),
        pltpu.make_async_copy(part, part_out, end_sem.at[7]),
    ]
    for copy in last:
        copy.start()
    for i in (2, 3):
        pltpu.make_async_copy(qkv.at[i % 2], qkv_out.at[order[i]], qkv_sem.at[i % 2]).wait()
        pltpu.make_async_copy(ctx.at[i % 2], ctx_out.at[order[i]], ctx_sem.at[i % 2]).wait()
    for r in range(rows):
        pltpu.make_async_copy(prob.at[r], prob_out.at[order[3], r], prob_sem.at[r]).wait()
    for c in range(chunks):
        at = pl.ds(c * CHUNK, CHUNK)
        pltpu.make_async_copy(act.at[at, :], act_out.at[order[3], at], act_sem.at[c]).wait()
        pltpu.make_async_copy(slope.at[at, :], slope_out.at[order[3], at], slope_sem.at[c]).wait()
    turned_copy(0).wait()
    turned_copy(1).wait()
    rstd_copy.wait()
    whole_copy.wait()
    for copy in last:
        copy.wait()
    if fused:
        gather.finish()


def run_forward(x, cot, seg, vectors, mats, bias):
    rows, length, _ = x.shape
    tokens = rows * length
    fused = lax.axis_size("dp") == 8 and lax.axis_size("mp") == 4
    hbm, vmem = pl.BlockSpec(memory_space=pl.ANY), pl.BlockSpec(memory_space=pltpu.VMEM)
    flat = (tokens, D)
    width = D // 4
    block = (4, 2, SLICE, D)
    dense = [x.reshape(flat), cot.reshape(flat), seg[:, None, :], seg[:, :, None], vectors]
    if fused:
        held = [m.reshape(block) for m in mats] + [bias]
    else:
        held = [jnp.stack([lax.all_gather(m, "mp", axis=0) for m in mats]).reshape((3, 4) + block)]
        held = held + [lax.all_gather(bias, "mp", axis=0)]
    probs = (rows, D // HEAD // 4, length, length)
    shape = jax.ShapeDtypeStruct
    dma = pltpu.SemaphoreType.DMA
    return pl.pallas_call(
        functools.partial(forward_kernel, fused, rows, length),
        out_shape=(
            shape((3, 4) + block, BF),
            shape((4,) + flat, BF),
            shape((4, tokens, width), BF),
            shape((4,) + probs, BF),
            shape((4,) + flat, BF),
            shape((4,) + flat, BF),
            shape(flat, F32),
            shape((tokens, 128), F32),
            shape(flat, F32),
            shape((3, D, tokens), BF),
            shape(flat, BF),
            shape((8, D), F32),
        ),
        in_specs=[vmem] * 5 + [hbm] * len(held),
        out_specs=(hbm,) * 12,
        scratch_shapes=([dma(s) for s in Gather.sems] if fused else [])
        + [
            pltpu.VMEM((3, 4) + block, BF),
            pltpu.VMEM((4, SMALL, D), BF),
            pltpu.VMEM((2,) + flat, BF),
            pltpu.VMEM((2, tokens, width), BF),
            pltpu.VMEM(probs, BF),
            pltpu.VMEM(flat, BF),
            pltpu.VMEM(flat, BF),
            pltpu.VMEM(flat, F32),
            pltpu.VMEM(flat, F32),
            pltpu.VMEM((tokens, 128), F32),
            pltpu.VMEM(flat, BF),
            pltpu.VMEM((3, D, tokens), BF),
            pltpu.VMEM(flat, BF),
            pltpu.VMEM((8, D), F32),
            dma((2,)),
            dma((2,)),
            dma((2,)),
            dma((rows,)),
            dma((tokens // CHUNK,)),
            dma((tokens // CHUNK,)),
            dma((8,)),
        ],
        compiler_params=pltpu.CompilerParams(
            collective_id=0 if fused else None, has_side_effects=True, vmem_limit_bytes=VMEM_MOST
        ),
        name="forward",
    )(*dense, *held)


def backward_kernel(fused, rows, length, *refs):
    n_sem = len(Scatter.sems) if fused else 0
    n_buf = len(Scatter.buffers) if fused else 0
    (vec_ref, part_in, whole, qkv_in, ctx_in, prob_in, act_in, slope_in, normed_in, rstd_in, ds_in, turned_in) = refs[:12]
    grad_out, small_out, input_out = refs[12:15]
    rest = refs[15:]
    buffers, sems, rest = rest[:n_buf], rest[n_buf : n_buf + n_sem], rest[n_buf + n_sem :]
    (grads, weights, wide, tall, thin, stream, normed, rstd, low, turned, prob, ctx, dctx, part,
     w_sem, wide_sem, tall_sem, prob_sem, ctx_sem, turned_sem, end_sem) = rest
    tokens = rows * length
    strips, chunks = tokens // STRIP, tokens // CHUNK
    heads = D // HEAD // 4
    width = heads * HEAD
    if fused:
        scatter = Scatter(grads, buffers, sems)
        scatter.begin()
        stage = scatter.stage
    else:
        stage = lambda i: None

    def weight_copy(m, z, slot):
        return pltpu.make_async_copy(whole.at[m, z], weights.at[slot], w_sem.at[slot])

    def wide_copy(source, z):
        return pltpu.make_async_copy(source.at[z], wide.at[z % 2], wide_sem.at[z % 2])

    def tall_copy(z):
        return pltpu.make_async_copy(slope_in.at[z], tall.at[z % 2], tall_sem.at[z % 2])

    def turned_copy(source, slot):
        return pltpu.make_async_copy(turned_in.at[source], turned.at[slot], turned_sem.at[slot])

    def prob_copy(g):
        return pltpu.make_async_copy(prob_in.at[g // rows, g % rows], prob.at[g % 2], prob_sem.at[g % 2])

    def ctx_copy(z):
        return pltpu.make_async_copy(ctx_in.at[z], ctx.at[z % 2], ctx_sem.at[z % 2])

    stream_copy = pltpu.make_async_copy(ds_in, stream, end_sem.at[0])
    normed_copy = pltpu.make_async_copy(normed_in, normed, end_sem.at[1])
    rstd_copy = pltpu.make_async_copy(rstd_in, rstd, end_sem.at[2])
    stream_copy.start()
    turned_copy(2, 0).start()
    wide_copy(act_in, 0).start()
    weight_copy(2, 0, 0).start()
    tall_copy(0).start()
    turned_copy(1, 1).start()
    weight_copy(1, 0, 1).start()
    wide_copy(act_in, 1).start()
    tall_copy(1).start()
    weight_copy(2, 1, 2).start()
    weight_copy(1, 1, 3).start()
    normed_copy.start()
    rstd_copy.start()
    part[...] = jnp.zeros_like(part)
    part[0:8, :] = part_in[...]
    stream_copy.wait()

    @pl.loop(0, strips)
    def _(s):
        at = pl.ds(pl.multiple_of(s * STRIP, STRIP), STRIP)
        low[at, :] = stream[at, :].astype(BF)

    def outer(slot, turned_slot, right, columns, offset):
        @pl.loop(0, 2)
        def _(j):
            rows_at = pl.ds(pl.multiple_of(j * CHUNK, CHUNK), CHUNK)
            product = mm(turned[turned_slot, rows_at, :], right[:, :columns], NN).astype(BF)
            grads[slot, pl.ds(2 * j, 2), :, :, offset : offset + columns] = product.reshape(2, 2, SLICE, columns)

    def emit(slot, m, z):
        if not fused:
            copy = pltpu.make_async_copy(grads.at[slot], grad_out.at[m, z], end_sem.at[3])
            copy.start()
            copy.wait()

    dexp = thin
    turned_copy(2, 0).wait()
    turned_copy(1, 1).wait()
    for z in range(4):
        slot = 2 * (z % 2)
        wide_copy(act_in, z).wait()
        outer(z, 0, wide.at[z % 2], D, 0)
        emit(z, 2, z)
        stage(2 * z)
        weight_copy(2, z, slot).wait()
        weight_copy(1, z, slot + 1).wait()
        tall_copy(z).wait()

        @pl.loop(0, chunks)
        def _(c, z=z, slot=slot):
            at = pl.ds(pl.multiple_of(c * CHUNK, CHUNK), CHUNK)
            dactive = mm(low[at, :], square(weights.at[slot]), NT)
            value = (dactive * tall[z % 2, at, :].astype(F32)).astype(BF)
            dexp[at, :] = value
            part[10 + z : 11 + z, :] += jnp.sum(value.astype(F32), axis=0, keepdims=True)
            stream[at, :] = stream[at, :] + mm(value, square(weights.at[slot + 1]), NT)

        outer(4 + z, 1, dexp, D, 0)
        emit(4 + z, 1, z)
        stage(2 * z + 1)
        if z < 2:
            wide_copy(act_in, z + 2).start()
            tall_copy(z + 2).start()
            weight_copy(2, z + 2, slot).start()
            weight_copy(1, z + 2, slot + 1).start()
        elif z == 2:
            wide_copy(qkv_in, 0).start()
            weight_copy(0, 0, 0).start()
            weight_copy(0, 1, 1).start()
            ctx_copy(0).start()
            ctx_copy(1).start()
            prob_copy(0).start()
        else:
            wide_copy(qkv_in, 1).start()
            weight_copy(0, 2, 2).start()
            weight_copy(0, 3, 3).start()
            turned_copy(0, 0).start()
    normed_copy.wait()
    rstd_copy.wait()

    @pl.loop(0, strips)
    def _(s):
        at = pl.ds(pl.multiple_of(s * STRIP, STRIP), STRIP)
        dhidden, normal = stream[at, :], normed[at, :]
        dmixed = norm_backward(dhidden, vec_ref[0:1, :], normal, rstd[at, 0:1])
        part[0:1, :] += jnp.sum(dhidden * normal, axis=0, keepdims=True)
        part[1:2, :] += jnp.sum(dhidden, axis=0, keepdims=True)
        part[2:3, :] += jnp.sum(dmixed, axis=0, keepdims=True)
        stream[at, :] = dmixed
        dmixed = dmixed.astype(BF)
        low[at, :] = dmixed
        turned[1, :, at] = dmixed.T

    turned_copy(0, 0).wait()
    dproj = thin
    for z in range(4):
        weight_copy(0, z, z).wait()
        wide_copy(qkv_in, z).wait()
        ctx_copy(z).wait()
        weight, qkv = weights.at[z], wide.at[z % 2]

        @pl.loop(0, chunks)
        def _(c, weight=weight):
            at = pl.ds(pl.multiple_of(c * CHUNK, CHUNK), CHUNK)
            dctx[at, :] = mm(low[at, :], square(weight)[:, 3 * width :], NN).astype(BF)

        @pl.loop(0, rows)
        def _(r, z=z, qkv=qkv):
            at = pl.ds(pl.multiple_of(r * length, 32), length)
            g = z * rows + r
            prob_copy(g).wait()
            pl.when(g + 1 < 4 * rows)(lambda: prob_copy(g + 1).start())
            dq, dk, dv = [], [], []
            scale = jnp.asarray(HEAD ** (-0.5), BF)
            for h in range(heads):
                q = qkv[at, h * HEAD : (h + 1) * HEAD] * scale
                k = qkv[at, width + h * HEAD : width + (h + 1) * HEAD]
                v = qkv[at, 2 * width + h * HEAD : 2 * width + (h + 1) * HEAD]
                dc = dctx[at, h * HEAD : (h + 1) * HEAD]
                probs = prob[g % 2, h]
                full = probs.astype(F32)
                dprobs = mm(v, dc, NT)
                inner = jnp.sum(full * dprobs, axis=0, keepdims=True)
                dscores = (full * (dprobs - inner)).astype(BF)
                dv.append(mm(probs, dc, NN).astype(BF))
                dk.append(mm(dscores, q, NN).astype(BF))
                dq.append((mm(k, dscores, TN) * HEAD ** (-0.5)).astype(BF).T)
            joined = jnp.concatenate(dq + dk + dv, axis=1)
            dproj[at, 0 : 3 * width] = joined
            part[6 + z : 7 + z, 0 : 3 * width] += jnp.sum(joined.astype(F32), axis=0, keepdims=True)

        if fused:
            scatter.to_core(2 * z).wait_send()
        outer(z, 0, dproj, 3 * width, 0)
        outer(z, 1, ctx.at[z % 2], width, 3 * width)
        emit(z, 0, z)
        stage(8 + z)
        if z < 2:
            wide_copy(qkv_in, z + 2).start()
            ctx_copy(z + 2).start()

        @pl.loop(0, chunks)
        def _(c, z=z, weight=weight):
            at = pl.ds(pl.multiple_of(c * CHUNK, CHUNK), CHUNK)
            add = mm(dproj[at, 0 : 3 * width], square(weight)[:, 0 : 3 * width], NT)
            stream[at, :] = stream[at, :] + add

    input_copy = pltpu.make_async_copy(stream, input_out, end_sem.at[0])
    input_copy.start()
    if fused:
        n = len(Scatter.steps)
        scatter.small_stage(part, 0)
        for i in range(3):
            stage(n + i)
            scatter.small_stage(part, 1 + i)
        for m in (2, 1, 0):
            grad_out[m] = scatter.total(m)
        small_out[...] = scatter.small_stage(part, 4)
        scatter.finish(part)
    else:
        small_out[...] = part[...]
    input_copy.wait()


def run_backward(vectors, part, saved, rows, length):
    fused = lax.axis_size("dp") == 8 and lax.axis_size("mp") == 4
    hbm, vmem = pl.BlockSpec(memory_space=pl.ANY), pl.BlockSpec(memory_space=pltpu.VMEM)
    tokens = rows * length
    flat = (tokens, D)
    width = D // 4
    block = (4, 2, SLICE, D)
    shape = jax.ShapeDtypeStruct
    dma = pltpu.SemaphoreType.DMA
    whole_grad = shape((3, SLICE, D), F32) if fused else shape((3, 4) + block, BF)
    grads, sums, input_grad = pl.pallas_call(
        functools.partial(backward_kernel, fused, rows, length),
        out_shape=(whole_grad, shape((SMALL, D), F32), shape(flat, F32)),
        in_specs=[vmem] * 2 + [hbm] * 10,
        out_specs=(vmem if fused else hbm, vmem, hbm),
        scratch_shapes=([pltpu.VMEM(s, t) for s, t in Scatter.buffers] + [dma(s) for s in Scatter.sems] if fused else [])
        + [
            pltpu.VMEM((8,) + block, BF),
            pltpu.VMEM((4,) + block, BF),
            pltpu.VMEM((2,) + flat, BF),
            pltpu.VMEM((2,) + flat, BF),
            pltpu.VMEM(flat, BF),
            pltpu.VMEM(flat, F32),
            pltpu.VMEM(flat, F32),
            pltpu.VMEM((tokens, 128), F32),
            pltpu.VMEM(flat, BF),
            pltpu.VMEM((2, D, tokens), BF),
            pltpu.VMEM((2, D // HEAD // 4, length, length), BF),
            pltpu.VMEM((2, tokens, width), BF),
            pltpu.VMEM((tokens, width), BF),
            pltpu.VMEM((SMALL, D), F32),
            dma((4,)),
            dma((2,)),
            dma((2,)),
            dma((2,)),
            dma((2,)),
            dma((2,)),
            dma((4,)),
        ],
        compiler_params=pltpu.CompilerParams(
            collective_id=1 if fused else None, has_side_effects=True, vmem_limit_bytes=VMEM_MOST
        ),
        name="backward",
    )(vectors, part, *saved)
    if not fused:
        parts = lax.axis_size("dp")
        grads = lax.psum_scatter(grads.reshape(3, 4, D, D), "dp", scatter_dimension=2, tiled=True)
        grads = lax.psum_scatter(grads, "mp", scatter_dimension=1, tiled=True)
        grads = grads.reshape(3, D // parts, D).astype(F32)
        sums = lax.psum(sums, ("dp", "mp"))
    return input_grad, grads, sums


def update_all(state, reduced, sums):
    dp, mp = lax.axis_index("dp"), lax.axis_index("mp")
    groups, parts = lax.axis_size("mp"), lax.axis_size("dp")
    width = D // (groups * parts)
    cut = 3 * D // groups
    own = D // groups // HEAD
    rows = reduced.shape[1]
    vec = lax.dynamic_slice_in_dim(sums[:6], (dp * groups + mp) * width, width, 1)
    qv = lax.dynamic_slice_in_dim(sums, 6 + mp, 1, 0)[0, :cut].reshape(3, own, HEAD)
    qv = lax.dynamic_slice_in_dim(jnp.stack([qv[0], qv[2]]), dp * (HEAD // parts), HEAD // parts, 2)
    eb = lax.dynamic_slice_in_dim(sums, 10 + mp, 1, 0).reshape(D // HEAD, HEAD)
    eb = lax.dynamic_slice_in_dim(eb, dp * (HEAD // parts), HEAD // parts, 1)
    triple_grad = reduced[0, :, :cut].reshape(rows, 3, D // groups).transpose(1, 0, 2)
    grads = (triple_grad, qv, reduced[0, :, cut:].T, reduced[1], eb, reduced[2].T, vec)
    rates = (D ** (-0.5), 0.5, (D // 16) ** (-0.5), D ** (-0.5), 0.5, FF ** (-0.5), 0.3)
    outs = ()
    for i in range(7):
        outs = outs + adam_update(state[3 * i], state[3 * i + 1], state[3 * i + 2], grads[i], rates[i])
    return outs


def per_device(
    activations,
    cotangent,
    segments,
    triple_weight,
    query_value_bias,
    output_weight,
    expand_weight,
    expand_bias,
    shrink_weight,
    vector_params,
    *state,
):
    rows, length, _ = activations.shape
    mats = pack_weights(triple_weight, output_weight, expand_weight, shrink_weight)
    bias = pack_biases(query_value_bias, expand_bias)
    vectors = jnp.concatenate([vector_params.astype(F32), jnp.zeros((2, D), F32)])
    seg = lax.dynamic_slice_in_dim(segments, lax.axis_index("mp") * rows, rows, 0)
    *saved, result, part = run_forward(activations, cotangent, seg, vectors, mats, bias)
    input_grad, reduced, sums = run_backward(vectors, part, saved, rows, length)
    outs = (result.reshape(activations.shape), input_grad.reshape(activations.shape))
    return outs + update_all(state, reduced, sums)


STATE_SPECS = (
    P(None, "dp", "mp"),
    P(None, "mp", "dp"),
    P("mp", "dp"),
    P("dp", "mp"),
    P("mp", "dp"),
    P("mp", "dp"),
    P(None, ("dp", "mp")),
)


def solution(mesh):
    rows = P(("dp", "mp"), None, None)
    placed = (
        rows,
        rows,
        P("dp", None),
        P(None, None, "mp"),
        P(None, "mp", None),
        P("mp", None),
        P(None, "mp"),
        P("mp", None),
        P("mp", None),
        P(),
    )
    for spec in STATE_SPECS:
        placed = placed + (spec,) * 3
    out_specs = (rows, rows)
    for spec in STATE_SPECS:
        out_specs = out_specs + (spec,) * 4
    return jax.shard_map(per_device, mesh=mesh, in_specs=placed, out_specs=out_specs, check_vma=False)
```

```python
import functools

import jax
import jax.numpy as jnp
from jax import lax
from jax.experimental import pallas as pl
from jax.experimental.pallas import tpu as pltpu
from jax.sharding import PartitionSpec as P

D = 768
HEAD = 64
FF = 3072
STEP = 10


NORM_EPS = 1e-05
BETA_ONE = 0.5
BETA_TWO = 0.6
ADAM_EPS = 1e-08
WEIGHT_DECAY = 0.01
MASKED = -1e30
SQRT_HALF = 0.7071067811865476
INV_ROOT_TAU = 0.3989422804014327


def norm_forward(summed, gain, shift):
    centre = summed - jnp.mean(summed, axis=-1, keepdims=True)
    scale = lax.rsqrt(jnp.mean(centre * centre, axis=-1, keepdims=True) + NORM_EPS)
    normed = centre * scale
    return (gain * normed + shift, normed, scale)


def norm_backward(gradient, gain, normed, scale):
    scaled = gradient * gain
    centred = scaled - jnp.mean(scaled, axis=-1, keepdims=True)
    return scale * (centred - normed * jnp.mean(scaled * normed, axis=-1, keepdims=True))


def adam_update(master, first, second, gradient, rate):
    first_new = BETA_ONE * first + (1.0 - BETA_ONE) * gradient
    second_new = BETA_TWO * second + (1.0 - BETA_TWO) * gradient * gradient
    corrected = first_new / (1.0 - BETA_ONE**STEP)
    spread = jnp.sqrt(second_new / (1.0 - BETA_TWO**STEP))
    master_new = master - rate * (corrected / (spread + ADAM_EPS) + WEIGHT_DECAY * master)
    return (master_new, first_new, second_new, master_new.astype(jnp.bfloat16))


MESH = pl.DeviceIdType.MESH
BF = jnp.bfloat16
F32 = jnp.float32
HALF = 48
SLICE = 96
SMALL = 16
VECTORS = 8


def place():
    p, z = lax.axis_index("dp"), lax.axis_index("mp")
    core, xy = p % 2, p // 2
    x, y = xy % 2, xy // 2
    return p, z, core, xy, p + 1 - 2 * core, p + 2 - 4 * x, p + 4 - 8 * y, xy + 1 - 2 * x, xy + 2 - 4 * y


def remote(src, dst, send_sem, recv_sem, p, z):
    return pltpu.make_async_remote_copy(
        src_ref=src, dst_ref=dst, send_sem=send_sem, recv_sem=recv_sem, device_id=(p, z), device_id_type=MESH
    )


def greet(p, z, pc, px, py):
    barrier = pltpu.get_barrier_semaphore()
    for peer in ((pc, z), (px, z), (py, z), (p, (z + 1) % 4), (p, (z + 2) % 4), (p, (z + 3) % 4)):
        pl.semaphore_signal(barrier, inc=1, device_id=peer, device_id_type=MESH)
    pl.semaphore_wait(barrier, 6)


class Gather:
    steps = [(0, 1), (0, 2), (0, 3), (1, 1), (2, 1), (1, 2), (2, 2), (1, 3), (2, 3)]
    sems = [(3,)] + [(3, 3)] * 12 + [(3,)] * 2

    def __init__(self, mats, whole, bias, biases, sems):
        self.mats, self.whole, self.bias, self.biases = mats, whole, bias, biases
        (self.ls, self.zs, self.zr, self.xs, self.xr, self.ys, self.yr, self.as_, self.ar, self.bs, self.br, self.cs,
         self.cr, self.ss, self.sr) = sems
        self.where = place()

    def local(self, m):
        z = self.where[1]
        return pltpu.make_async_copy(self.mats[m - 1], self.whole.at[m, z], self.ls.at[m])

    def small(self, d):
        p, z = self.where[:2]
        return remote(self.bias, self.biases.at[z], self.ss.at[d - 1], self.sr.at[d - 1], p, (z + d) % 4)

    def along_z(self, m, d):
        p, z, core, xy = self.where[:4]
        own = self.whole.at[m, z] if m == 0 else self.mats[m - 1]
        return remote(own.at[xy, core], self.whole.at[m, z, xy, core], self.zs.at[m, d - 1],
                      self.zr.at[m, d - 1], p, (z + d) % 4)

    def plane(self, m, d, block, rows, send_sem, recv_sem, peer):
        z = self.where[1]
        part = self.whole.at[m, (z + 4 - d) % 4, block, self.where[2], rows]
        return remote(part, part, send_sem.at[m, d - 1], recv_sem.at[m, d - 1], peer, z)

    def to_x(self, m, d):
        return self.plane(m, d, self.where[3], slice(None), self.xs, self.xr, self.where[5])

    def to_y(self, m, d):
        return self.plane(m, d, self.where[3], slice(None), self.ys, self.yr, self.where[6])

    def on_to_y(self, m, d):
        return self.plane(m, d, self.where[7], pl.ds(0, HALF), self.as_, self.ar, self.where[6])

    def on_to_x(self, m, d):
        return self.plane(m, d, self.where[8], pl.ds(HALF, HALF), self.bs, self.br, self.where[5])

    def to_core(self, m, d):
        z = self.where[1]
        part = self.whole.at[m, (z + 4 - d) % 4, :, self.where[2]]
        return remote(part, part, self.cs.at[m, d - 1], self.cr.at[m, d - 1], self.where[4], z)

    def begin(self):
        p, z, _, _, pc, px, py = self.where[:7]
        greet(p, z, pc, px, py)
        for d in (1, 2, 3):
            self.along_z(0, d).start()
            self.small(d).start()

    def stage(self, i):
        steps, n = self.steps, len(self.steps)
        if i < n:
            m, d = steps[i]
            self.along_z(m, d).wait_recv()
            if i < 3:
                self.small(d).wait_recv()
            self.to_x(m, d).start()
            self.to_y(m, d).start()
            if m < 2:
                self.along_z(m + 1, d).start()
        if 0 <= i - 1 < n:
            self.to_x(*steps[i - 1]).wait_recv()
            self.to_y(*steps[i - 1]).wait_recv()
            self.on_to_y(*steps[i - 1]).start()
            self.on_to_x(*steps[i - 1]).start()
        if 0 <= i - 2 < n:
            self.on_to_y(*steps[i - 2]).wait_recv()
            self.on_to_x(*steps[i - 2]).wait_recv()
            self.to_core(*steps[i - 2]).start()
        if 0 <= i - 3 < n:
            self.to_core(*steps[i - 3]).wait_recv()

    def finish(self):
        for d in (1, 2, 3):
            self.small(d).wait_send()
        for m, d in self.steps:
            for copy in (self.along_z, self.to_x, self.to_y, self.on_to_y, self.on_to_x, self.to_core):
                copy(m, d).wait_send()


class Scatter:
    steps = [(m, k) for k in range(4) for m in (2, 1)] + [(0, k) for k in range(4)]
    slots = [k + 4 * j for k in range(4) for j in (0, 1)] + list(range(4))
    buffers = [((12, 4, SLICE, D), BF)] + [((12, 2, HALF, D), BF)] * 2 + [((12, HALF, D), BF)] * 2 + [
        ((3, 3, SLICE, D), BF), ((3, 4, SLICE, D), BF), ((6, SMALL, D), F32), ((3, SMALL, D), F32)]
    sems = [(12,)] * 2 + [(12, 2)] * 4 + [(12,)] * 4 + [(3, 3)] * 2 + [(6,)] * 2

    def __init__(self, grads, buffers, sems):
        self.grads = grads
        self.sum, self.rx, self.ry, self.ra, self.rb, self.rz, self.plane, self.rv, self.sv = buffers
        (self.cs, self.cr, self.xs, self.xr, self.ys, self.yr, self.as_, self.ar, self.bs, self.br, self.zs, self.zr,
         self.ss, self.sr) = sems
        self.where = place()

    def to_core(self, i):
        _, z, core, _, pc = self.where[:5]
        return remote(self.grads.at[self.slots[i], :, 1 - core], self.sum.at[i], self.cs.at[i], self.cr.at[i], pc, z)

    def to_x(self, i, t):
        q = (self.where[7], 3 - self.where[3])[t]
        return remote(self.sum.at[i, q, pl.ds(0, HALF)], self.rx.at[i, t], self.xs.at[i, t], self.xr.at[i, t],
                      self.where[5], self.where[1])

    def to_y(self, i, t):
        q = (self.where[8], 3 - self.where[3])[t]
        return remote(self.sum.at[i, q, pl.ds(HALF, HALF)], self.ry.at[i, t], self.ys.at[i, t], self.yr.at[i, t],
                      self.where[6], self.where[1])

    def on_to_y(self, i):
        return remote(self.sum.at[i, self.where[8], pl.ds(0, HALF)], self.ra.at[i], self.as_.at[i], self.ar.at[i],
                      self.where[6], self.where[1])

    def on_to_x(self, i):
        return remote(self.sum.at[i, self.where[7], pl.ds(HALF, HALF)], self.rb.at[i], self.bs.at[i], self.br.at[i],
                      self.where[5], self.where[1])

    def to_owner(self, m, k, d):
        p = self.where[0]
        return remote(self.plane.at[m, k], self.rz.at[m, d - 1], self.zs.at[m, d - 1], self.zr.at[m, d - 1], p, k)

    def along_z(self, m, d):
        return self.to_owner(m, (self.where[1] + d) % 4, d)

    def begin(self):
        p, z, _, _, pc, px, py = self.where[:7]
        greet(p, z, pc, px, py)

    def stage(self, i):
        n = len(self.steps)
        core, xy, xyx, xyy = self.where[2], self.where[3], self.where[7], self.where[8]
        low, high = slice(0, HALF), slice(HALF, SLICE)
        if i < n:
            self.to_core(i).start()
        j = i - 1
        if 0 <= j < n:
            self.to_core(j).wait_recv()

            @pl.loop(0, 4)
            def _(q):
                mine = self.grads[self.slots[j], q, core].astype(F32)
                self.sum[j, q] = (self.sum[j, q].astype(F32) + mine).astype(BF)

            for t in (0, 1):
                self.to_x(j, t).start()
                self.to_y(j, t).start()
        j = i - 2
        if 0 <= j < n:
            for t in (0, 1):
                self.to_x(j, t).wait_recv()
                self.to_y(j, t).wait_recv()
            self.sum[j, xyy, low] = (self.sum[j, xyy, low].astype(F32) + self.rx[j, 1].astype(F32)).astype(BF)
            self.sum[j, xyx, high] = (self.sum[j, xyx, high].astype(F32) + self.ry[j, 1].astype(F32)).astype(BF)
            self.on_to_y(j).start()
            self.on_to_x(j).start()
        j = i - 3
        if 0 <= j < n:
            m, k = self.steps[j]
            self.on_to_y(j).wait_recv()
            self.on_to_x(j).wait_recv()
            self.plane[m, k, low] = (
                self.sum[j, xy, low].astype(F32) + self.rx[j, 0].astype(F32) + self.ra[j].astype(F32)
            ).astype(BF)
            self.plane[m, k, high] = (
                self.sum[j, xy, high].astype(F32) + self.ry[j, 0].astype(F32) + self.rb[j].astype(F32)
            ).astype(BF)
            z = self.where[1]
            pl.when(z != k)(lambda: self.to_owner(m, k, (k + 4 - z) % 4).start())

    def total(self, m):
        for d in (1, 2, 3):
            self.along_z(m, d).wait_recv()
        own = self.plane[m, self.where[1]].astype(F32)
        return own + self.rz[m, 0].astype(F32) + self.rz[m, 1].astype(F32) + self.rz[m, 2].astype(F32)

    def small_to(self, s, src, p, z):
        return remote(src, self.rv.at[s], self.ss.at[s], self.sr.at[s], p, z)

    def small_copy(self, part, c):
        p, z, _, _, pc, px, py = self.where[:7]
        if c == 0:
            return self.small_to(0, part, pc, z)
        if c == 1:
            return self.small_to(1, self.sv.at[0], px, z)
        if c == 2:
            return self.small_to(2, self.sv.at[1], py, z)
        return self.small_to(c, self.sv.at[2], p, (z + c - 2) % 4)

    def small_stage(self, part, i):
        if i == 0:
            self.small_copy(part, 0).start()
        elif i < 4:
            self.small_copy(part, i - 1).wait_recv()
            before = part[...] if i == 1 else self.sv[i - 2]
            self.sv[i - 1] = before + self.rv[i - 1]
            for c in (i,) if i < 3 else (3, 4, 5):
                self.small_copy(part, c).start()
        else:
            for c in (3, 4, 5):
                self.small_copy(part, c).wait_recv()
            return self.sv[2] + self.rv[3] + self.rv[4] + self.rv[5]

    def finish(self, part):
        for c in range(6):
            self.small_copy(part, c).wait_send()
        for i in range(len(self.steps)):
            if self.slots[i] not in self.slots[i + 1 :]:
                self.to_core(i).wait_send()
            self.on_to_y(i).wait_send()
            self.on_to_x(i).wait_send()
            for t in (0, 1):
                self.to_x(i, t).wait_send()
                self.to_y(i, t).wait_send()
        for m in range(3):
            for d in (1, 2, 3):
                self.along_z(m, d).wait_send()


def mm(a, b, dims):
    return lax.dot_general(a, b, (dims, ((), ())), preferred_element_type=jnp.float32)


def pack_weights(triple_weight, output_weight, expand_weight, shrink_weight):
    width = triple_weight.shape[2]
    mixing = jnp.concatenate([triple_weight.transpose(1, 0, 2).reshape(D, 3 * width), output_weight.T], axis=1)
    return mixing, expand_weight, shrink_weight


def pack_biases(query_value_bias, expand_bias):
    pair = query_value_bias.reshape(2, -1)
    none = jnp.zeros_like(pair[0])
    first = jnp.concatenate([pair[0], none, pair[1], none])
    return jnp.concatenate([first[None], expand_bias.reshape(1, -1), jnp.zeros((VECTORS - 2, D), BF)]).astype(F32)


TN = ((0,), (0,))
NT = ((1,), (1,))
NN = ((1,), (0,))
CHUNK = 384
STRIP = 128
TILE = 256
VMEM_MOST = 60 << 20
ATTEND_STAGES = {(0, 1): 1, (0, 3): 2, (1, 1): 4, (2, 0): 5, (2, 3): 6, (3, 2): 7}
FEED_STAGES = {(0, 0): 8, (0, 2): 9, (1, 0): 10, (1, 2): 11}


def tile(n):
    return pl.ds(pl.multiple_of(n * TILE, TILE), TILE)


def strip(s):
    return pl.ds(pl.multiple_of(s * STRIP, STRIP), STRIP)


def forward_kernel(fused, rows, length, *refs):
    n_sem = len(Gather.sems) if fused else 0
    x_in, cot_in, seg_ref, vec_in = refs[:4]
    n_in = 10 if fused else 6
    ins = refs[4:n_in]
    outs = refs[n_in : n_in + 12]
    (whole_out, qkv_out, ctx_out, prob_out, act_out, slope_out, normed_out, rstd_out, ds_out, turned_out, result_out,
     part_out) = outs
    rest = refs[n_in + 12 :]
    gather_sems, rest = rest[:n_sem], rest[n_sem:]
    (whole, bias, biases, joint, vec, x, cot, qkv, ctx, prob, act, slope, mixed, normed, rstd, low, turned,
     result, part, in_sem, w_sem, qkv_sem, ctx_sem, prob_sem, act_sem, slope_sem, end_sem) = rest
    tokens = rows * length
    strips = tokens // STRIP
    heads = D // HEAD // 4
    width = heads * HEAD
    z_own = lax.axis_index("mp")
    x_copy = pltpu.make_async_copy(x_in, x, in_sem.at[0])
    cot_copy = pltpu.make_async_copy(cot_in, cot, in_sem.at[1])
    x_copy.start()
    if fused:
        triple_in, output_in, e_ref, s_ref, qv_ref, eb_ref = ins
        joint_copies = [
            pltpu.make_async_copy(triple_in.at[j], joint.at[pl.ds(j * width, width)], in_sem.at[2 + j]) for j in range(3)
        ] + [pltpu.make_async_copy(output_in, joint.at[pl.ds(3 * width, width)], in_sem.at[5])]
        for copy in joint_copies:
            copy.start()
        gather = Gather((e_ref, s_ref), whole, bias, biases, gather_sems)
        stage = gather.stage
        bias[...] = jnp.zeros_like(bias)
        for h in range(heads):
            for j in (0, 1):
                at = slice(2 * j * width + h * HEAD, 2 * j * width + (h + 1) * HEAD)
                bias[0:1, at] = qv_ref[h, j : j + 1, :].astype(F32)
        for b in range(D // HEAD):
            bias[1:2, b * HEAD : (b + 1) * HEAD] = eb_ref[b : b + 1, :].astype(F32)
        for copy in joint_copies:
            copy.wait()
        for j in (0, 1):
            half = joint[:, j * CHUNK : (j + 1) * CHUNK].T
            whole[0, z_own, 2 * j : 2 * j + 2] = half.reshape(2, 2, SLICE, D)
        gather.begin()
        gather.local(1).start()
        gather.local(2).start()
        own_bias = pltpu.make_async_copy(bias, biases.at[z_own], w_sem.at[0])
        own_bias.start()
        own_bias.wait()
    else:
        copy = pltpu.make_async_copy(ins[0], whole, w_sem.at[0])
        copy.start()
        small = pltpu.make_async_copy(ins[1], biases, w_sem.at[1])
        small.start()
        copy.wait()
        small.wait()
        stage = lambda i: None
    cot_copy.start()
    vec[0:6, :] = vec_in[...].astype(F32)

    def block(i):
        return (z_own + 3 * i) % 4

    def columns(m, z, n):
        return whole[m, z, :, :, :, tile(n)].reshape(D, TILE)

    def turned_copy(slot):
        return pltpu.make_async_copy(turned.at[slot], turned_out.at[slot], end_sem.at[slot])

    def qkv_copy(i):
        return pltpu.make_async_copy(qkv.at[i % 2], qkv_out.at[block(i)], qkv_sem.at[i % 2])

    def ctx_copy(i):
        return pltpu.make_async_copy(ctx.at[i % 2], ctx_out.at[block(i)], ctx_sem.at[i % 2])

    def prob_copy(i, r):
        return pltpu.make_async_copy(prob.at[r], prob_out.at[block(i), r], prob_sem.at[r])

    def act_copy(i):
        return pltpu.make_async_copy(act.at[i % 2], act_out.at[block(i)], act_sem.at[i % 2])

    def slope_copy(i):
        return pltpu.make_async_copy(slope.at[i % 2], slope_out.at[block(i)], slope_sem.at[i % 2])

    def whole_copy(m):
        return pltpu.make_async_copy(whole.at[m], whole_out.at[m], w_sem.at[m])

    x_copy.wait()
    if fused:
        stage(0)

    @pl.loop(0, 4)
    def _(i):
        z = block(i)
        slot = i % 2

        @pl.when(i >= 2)
        def _():
            qkv_copy(i - 2).wait()
            ctx_copy(i - 2).wait()

        @pl.loop(0, 3)
        def _(n):
            add = biases[z, 0:1, tile(n)]
            qkv[slot, :, tile(n)] = (mm(x[...], columns(0, z, n), NN) + add).astype(BF)

        qkv_copy(i).start()

        @pl.loop(0, rows)
        def _(r):
            at = pl.ds(pl.multiple_of(r * length, 32), length)
            pl.when(i >= 1)(lambda: prob_copy(i - 1, r).wait())
            pair = seg_ref[pl.ds(z_own * rows + r, 1), :]
            number = lax.broadcasted_iota(jnp.int32, (8, length), 0)
            among = jnp.where(number == pair, 1.0, 0.0).astype(BF)
            mask = (mm(among, among, TN) - 1.0) * -MASKED
            done = []
            for h in range(heads):
                q = qkv[slot, at, h * HEAD : (h + 1) * HEAD] * jnp.asarray(HEAD ** (-0.5), BF)
                k = qkv[slot, at, width + h * HEAD : width + (h + 1) * HEAD]
                v = qkv[slot, at, 2 * width + h * HEAD : 2 * width + (h + 1) * HEAD]
                scores = mm(k, q, NT) + mask
                weights = jnp.exp(scores - jnp.max(scores, axis=0, keepdims=True))
                share = 1.0 / jnp.sum(weights, axis=0, keepdims=True)
                probs = (weights * share).astype(BF)
                prob[r, h] = probs
                done.append(mm(v, probs, TN).astype(BF).T)
            ctx[slot, at, :] = jnp.concatenate(done, axis=1)
            prob_copy(i, r).start()
            for (a, b), number in ATTEND_STAGES.items():
                pl.when((i == a) & (r == b))(functools.partial(stage, number))

        ctx_copy(i).start()

        @pl.when(i == 0)
        def _():
            @pl.loop(0, strips)
            def _(s):
                value = x[strip(s), :]
                mixed[strip(s), :] = value.astype(F32) + vec[2:3, :]
                turned[0, :, strip(s)] = value.T

            turned_copy(0).start()
            stage(3)

        @pl.loop(0, tokens // CHUNK)
        def _(c):
            at = pl.ds(pl.multiple_of(c * CHUNK, CHUNK), CHUNK)
            add = mm(ctx[slot, at, :], whole[0, z].reshape(D, D)[:, 3 * width :], NT)
            mixed[at, :] = mixed[at, :] + add

    whole_copy(0).start()

    @pl.loop(0, strips)
    def _(s):
        at = strip(s)
        hidden, normal, scale = norm_forward(mixed[at, :], vec[0:1, :], vec[1:2, :])
        normed[at, :] = normal
        rstd[at, :] = jnp.broadcast_to(scale, (STRIP, 128))
        mixed[at, :] = hidden + vec[5:6, :]
        hidden = hidden.astype(BF)
        low[at, :] = hidden
        turned[1, :, at] = hidden.T

    turned_copy(1).start()
    normed_copy = pltpu.make_async_copy(normed, normed_out, end_sem.at[3])
    normed_copy.start()
    rstd_copy = pltpu.make_async_copy(rstd, rstd_out, end_sem.at[4])
    rstd_copy.start()
    if fused:
        gather.local(1).wait()
        gather.local(2).wait()

    @pl.loop(0, 4)
    def _(i):
        z = block(i)
        slot = i % 2

        @pl.when(i >= 2)
        def _():
            act_copy(i - 2).wait()
            slope_copy(i - 2).wait()

        @pl.loop(0, 3)
        def _(n):
            u = mm(low[...], columns(1, z, n), NN) + biases[z, 1:2, tile(n)]
            cumulative = 0.5 + 0.5 * lax.erf(u * SQRT_HALF)
            act[slot, :, tile(n)] = (u * cumulative).astype(BF)
            slope[slot, :, tile(n)] = (cumulative + u * jnp.exp(-0.5 * u * u) * INV_ROOT_TAU).astype(BF)
            for (a, b), number in FEED_STAGES.items():
                pl.when((i == a) & (n == b))(functools.partial(stage, number))

        act_copy(i).start()
        slope_copy(i).start()

        @pl.loop(0, 3)
        def _(n):
            mixed[:, tile(n)] = mixed[:, tile(n)] + mm(act[slot], columns(2, z, n), NN)

        @pl.when(i == 2)
        def _():
            whole_copy(1).start()
            whole_copy(2).start()

    normed_copy.wait()
    cot_copy.wait()
    part[...] = jnp.zeros_like(part)

    @pl.loop(0, strips)
    def _(s):
        at = strip(s)
        block_result, normal, scale = norm_forward(mixed[at, :], vec[3:4, :], vec[4:5, :])
        result[at, :] = block_result.astype(BF)
        back = cot[at, :].astype(F32)
        dsummed = norm_backward(back, vec[3:4, :], normal, scale)
        normed[at, :] = dsummed
        turned[2, :, at] = dsummed.astype(BF).T
        part[3:4, :] += jnp.sum(back * normal, axis=0, keepdims=True)
        part[4:5, :] += jnp.sum(back, axis=0, keepdims=True)
        part[5:6, :] += jnp.sum(dsummed, axis=0, keepdims=True)

    last = [
        turned_copy(2),
        pltpu.make_async_copy(normed, ds_out, end_sem.at[5]),
        pltpu.make_async_copy(result, result_out, end_sem.at[6]),
        pltpu.make_async_copy(part, part_out, end_sem.at[7]),
    ]
    for copy in last:
        copy.start()
    for i in (2, 3):
        qkv_copy(i).wait()
        ctx_copy(i).wait()
        act_copy(i).wait()
        slope_copy(i).wait()
    for r in range(rows):
        prob_copy(3, r).wait()
    turned_copy(0).wait()
    turned_copy(1).wait()
    rstd_copy.wait()
    for m in range(3):
        whole_copy(m).wait()
    for copy in last:
        copy.wait()
    if fused:
        gather.finish()


def run_forward(x, cot, segments, vector_params, weights, biases):
    rows, length, _ = x.shape
    tokens = rows * length
    fused = lax.axis_size("dp") == 8 and lax.axis_size("mp") == 4
    hbm, vmem = pl.BlockSpec(memory_space=pl.ANY), pl.BlockSpec(memory_space=pltpu.VMEM)
    flat = (tokens, D)
    width = D // 4
    block = (4, 2, SLICE, D)
    dense = [x.reshape(flat), cot.reshape(flat), segments, vector_params]
    if fused:
        triple, output, expand, shrink = weights
        held = [triple.transpose(0, 2, 1), output, expand.reshape(block), shrink.reshape(block)]
        held = held + [biases[0].transpose(1, 0, 2), biases[1]]
        spaces = [hbm, hbm, hbm, hbm, vmem, vmem]
    else:
        mats = pack_weights(*weights)
        held = [jnp.stack([lax.all_gather(m, "mp", axis=0) for m in mats]).reshape((3, 4) + block)]
        held = held + [lax.all_gather(pack_biases(*biases), "mp", axis=0)]
        spaces = [hbm, hbm]
    probs = (rows, D // HEAD // 4, length, length)
    shape = jax.ShapeDtypeStruct
    dma = pltpu.SemaphoreType.DMA
    return pl.pallas_call(
        functools.partial(forward_kernel, fused, rows, length),
        out_shape=(
            shape((3, 4) + block, BF),
            shape((4,) + flat, BF),
            shape((4, tokens, width), BF),
            shape((4,) + probs, BF),
            shape((4,) + flat, BF),
            shape((4,) + flat, BF),
            shape(flat, F32),
            shape((tokens, 128), F32),
            shape(flat, F32),
            shape((3, D, tokens), BF),
            shape(flat, BF),
            shape((VECTORS, D), F32),
        ),
        in_specs=[hbm, hbm, vmem, vmem] + spaces,
        out_specs=(hbm,) * 12,
        scratch_shapes=([dma(s) for s in Gather.sems] if fused else [])
        + [
            pltpu.VMEM((3, 4) + block, BF),
            pltpu.VMEM((VECTORS, D), F32),
            pltpu.VMEM((4, VECTORS, D), F32),
            pltpu.VMEM((D, D), BF),
            pltpu.VMEM((VECTORS, D), F32),
            pltpu.VMEM(flat, BF),
            pltpu.VMEM(flat, BF),
            pltpu.VMEM((2,) + flat, BF),
            pltpu.VMEM((2, tokens, width), BF),
            pltpu.VMEM(probs, BF),
            pltpu.VMEM((2,) + flat, BF),
            pltpu.VMEM((2,) + flat, BF),
            pltpu.VMEM(flat, F32),
            pltpu.VMEM(flat, F32),
            pltpu.VMEM((tokens, 128), F32),
            pltpu.VMEM(flat, BF),
            pltpu.VMEM((3, D, tokens), BF),
            pltpu.VMEM(flat, BF),
            pltpu.VMEM((VECTORS, D), F32),
            dma((6,)),
            dma((3,)),
            dma((2,)),
            dma((2,)),
            dma((rows,)),
            dma((2,)),
            dma((2,)),
            dma((8,)),
        ],
        compiler_params=pltpu.CompilerParams(
            collective_id=0 if fused else None, has_side_effects=True, vmem_limit_bytes=VMEM_MOST
        ),
        name="forward",
    )(*dense, *held)


def backward_kernel(fused, rows, length, *refs):
    n_sem = len(Scatter.sems) if fused else 0
    n_buf = len(Scatter.buffers) if fused else 0
    (vec_in, part_in, whole, qkv_in, ctx_in, prob_in, act_in, slope_in, normed_in, rstd_in, ds_in, turned_in) = refs[:12]
    grad_out, small_out, input_out = refs[12:15]
    rest = refs[15:]
    buffers, sems, rest = rest[:n_buf], rest[n_buf : n_buf + n_sem], rest[n_buf + n_sem :]
    (grads, weights, wide, tall, dexp, stream, normed, rstd, low, turned, prob, ctx, dctx, part, vec,
     w_sem, wide_sem, tall_sem, prob_sem, ctx_sem, turned_sem, end_sem) = rest
    tokens = rows * length
    strips = tokens // STRIP
    heads = D // HEAD // 4
    width = heads * HEAD

    def weight_copy(m, z, slot):
        return pltpu.make_async_copy(whole.at[m, z], weights.at[slot], w_sem.at[slot])

    def wide_copy(source, z):
        return pltpu.make_async_copy(source.at[z], wide.at[z % 2], wide_sem.at[z % 2])

    def tall_copy(z):
        return pltpu.make_async_copy(slope_in.at[z], tall.at[z % 2], tall_sem.at[z % 2])

    def turned_copy(source, slot):
        return pltpu.make_async_copy(turned_in.at[source], turned.at[slot], turned_sem.at[slot])

    def prob_copy(g):
        return pltpu.make_async_copy(prob_in.at[g // rows, g % rows], prob.at[g % 2], prob_sem.at[g % 2])

    def ctx_copy(z):
        return pltpu.make_async_copy(ctx_in.at[z], ctx.at[z % 2], ctx_sem.at[z % 2])

    stream_copy = pltpu.make_async_copy(ds_in, stream, end_sem.at[0])
    normed_copy = pltpu.make_async_copy(normed_in, normed, end_sem.at[1])
    rstd_copy = pltpu.make_async_copy(rstd_in, rstd, end_sem.at[2])
    turned_copy(2, 0).start()
    wide_copy(act_in, 0).start()
    stream_copy.start()
    weight_copy(2, 0, 0).start()
    tall_copy(0).start()
    turned_copy(1, 1).start()
    weight_copy(1, 0, 1).start()
    wide_copy(act_in, 1).start()
    tall_copy(1).start()
    weight_copy(2, 1, 2).start()
    weight_copy(1, 1, 3).start()
    normed_copy.start()
    rstd_copy.start()
    if fused:
        scatter = Scatter(grads, buffers, sems)
        scatter.begin()
        stage = scatter.stage
    else:
        stage = lambda i: None
    vec[0:6, :] = vec_in[...].astype(F32)
    part[...] = jnp.zeros_like(part)
    part[0:VECTORS, :] = part_in[...]

    def outer(slot, turned_slot, right, lanes, offset=0, size=TILE):
        product = mm(turned[turned_slot], right[:, lanes], NN).astype(BF)
        grads[slot, :, :, :, offset if size != TILE else lanes] = product.reshape(4, 2, SLICE, size)

    def emit(slot, m, z):
        if not fused:
            copy = pltpu.make_async_copy(grads.at[slot], grad_out.at[m, z], end_sem.at[3])
            copy.start()
            copy.wait()

    turned_copy(2, 0).wait()

    @pl.loop(0, 4)
    def _(z):
        half = z % 2
        slot = 2 * half
        wide_copy(act_in, z).wait()
        pl.loop(0, 3)(lambda n: outer(z, 0, wide.at[half], tile(n)))
        emit(z, 2, z)
        for k in range(4):
            pl.when(z == k)(functools.partial(stage, 2 * k))

        @pl.when(z == 0)
        def _():
            stream_copy.wait()

            @pl.loop(0, strips)
            def _(s):
                low[strip(s), :] = stream[strip(s), :].astype(BF)

            turned_copy(1, 1).wait()

        weight_copy(2, z, slot).wait()
        tall_copy(z).wait()

        @pl.loop(0, 3)
        def _(n):
            dactive = mm(low[...], weights[slot, tile(n), :], NT)
            value = (dactive * tall[half, :, tile(n)].astype(F32)).astype(BF)
            dexp[:, tile(n)] = value
            part[pl.ds(10 + z, 1), tile(n)] = jnp.sum(value.astype(F32), axis=0, keepdims=True)

        pl.loop(0, 3)(lambda n: outer(4 + z, 1, dexp, tile(n)))
        emit(4 + z, 1, z)
        for k in range(4):
            pl.when(z == k)(functools.partial(stage, 2 * k + 1))
        weight_copy(1, z, slot + 1).wait()

        @pl.loop(0, 3)
        def _(n):
            stream[:, tile(n)] = stream[:, tile(n)] + mm(dexp[...], weights[slot + 1, tile(n), :], NT)

        @pl.when(z < 2)
        def _():
            wide_copy(act_in, z + 2).start()
            tall_copy(z + 2).start()
            weight_copy(2, z + 2, slot).start()
            weight_copy(1, z + 2, slot + 1).start()

        @pl.when(z == 2)
        def _():
            wide_copy(qkv_in, 0).start()
            weight_copy(0, 0, 0).start()
            weight_copy(0, 1, 1).start()
            ctx_copy(0).start()
            ctx_copy(1).start()
            prob_copy(0).start()

        @pl.when(z == 3)
        def _():
            wide_copy(qkv_in, 1).start()
            weight_copy(0, 2, 2).start()
            weight_copy(0, 3, 3).start()
            turned_copy(0, 0).start()

    normed_copy.wait()
    rstd_copy.wait()

    @pl.loop(0, strips)
    def _(s):
        at = strip(s)
        dhidden, normal = stream[at, :], normed[at, :]
        dmixed = norm_backward(dhidden, vec[0:1, :], normal, rstd[at, 0:1])
        part[0:1, :] += jnp.sum(dhidden * normal, axis=0, keepdims=True)
        part[1:2, :] += jnp.sum(dhidden, axis=0, keepdims=True)
        part[2:3, :] += jnp.sum(dmixed, axis=0, keepdims=True)
        stream[at, :] = dmixed
        dmixed = dmixed.astype(BF)
        low[at, :] = dmixed
        turned[1, :, at] = dmixed.T

    turned_copy(0, 0).wait()
    dproj = tall
    dproj[:, :, 2 * TILE : D] = jnp.zeros((2, tokens, TILE), BF)

    def pull(z):
        @pl.loop(0, 3)
        def _(n):
            add = mm(dproj[z % 2, :, 0 : 3 * width], weights[z, tile(n), 0 : 3 * width], NT)
            stream[:, tile(n)] = stream[:, tile(n)] + add

    @pl.loop(0, 4)
    def _(z):
        half = z % 2
        weight_copy(0, z, z).wait()
        wide_copy(qkv_in, z).wait()
        ctx_copy(z).wait()
        dctx[...] = mm(low[...], weights[z, :, 3 * width :], NN).astype(BF)

        @pl.loop(0, rows)
        def _(r):
            at = pl.ds(pl.multiple_of(r * length, 32), length)
            g = z * rows + r
            prob_copy(g).wait()
            pl.when(g + 1 < 4 * rows)(lambda: prob_copy(g + 1).start())
            dq, dk, dv = [], [], []
            scale = jnp.asarray(HEAD ** (-0.5), BF)
            for h in range(heads):
                q = wide[half, at, h * HEAD : (h + 1) * HEAD] * scale
                k = wide[half, at, width + h * HEAD : width + (h + 1) * HEAD]
                v = wide[half, at, 2 * width + h * HEAD : 2 * width + (h + 1) * HEAD]
                dc = dctx[at, h * HEAD : (h + 1) * HEAD]
                probs = prob[g % 2, h]
                full = probs.astype(F32)
                dprobs = mm(v, dc, NT)
                inner = jnp.sum(full * dprobs, axis=0, keepdims=True)
                dscores = (full * (dprobs - inner)).astype(BF)
                dv.append(mm(probs, dc, NN).astype(BF))
                dk.append(mm(dscores, q, NN).astype(BF))
                dq.append((mm(k, dscores, TN) * HEAD ** (-0.5)).astype(BF).T)
            joined = jnp.concatenate(dq + dk + dv, axis=1)
            dproj[half, at, 0 : 3 * width] = joined
            line = pl.ds(6 + z, 1)
            before = jnp.where(r == 0, 0.0, part[line, 0 : 3 * width])
            part[line, 0 : 3 * width] = before + jnp.sum(joined.astype(F32), axis=0, keepdims=True)

        if fused:
            for k in range(4):
                pl.when(z == k)(lambda k=k: scatter.to_core(2 * k).wait_send())
        pl.loop(0, 3)(lambda n: outer(z, 0, dproj.at[half], tile(n)))
        outer(z, 1, ctx.at[half], slice(None), slice(3 * width, D), width)
        emit(z, 0, z)
        for k in range(4):
            pl.when(z == k)(functools.partial(stage, 8 + k))

        @pl.when(z < 2)
        def _():
            wide_copy(qkv_in, z + 2).start()
            ctx_copy(z + 2).start()
            pull(z)

    if fused:
        n = len(Scatter.steps)
        scatter.small_stage(part, 0)
    pull(2)
    if fused:
        stage(n)
        scatter.small_stage(part, 1)
    pull(3)
    input_copy = pltpu.make_async_copy(stream, input_out, end_sem.at[0])
    input_copy.start()
    if fused:
        stage(n + 1)
        scatter.small_stage(part, 2)
        grad_out[2] = scatter.total(2)
        scatter.small_stage(part, 3)
        stage(n + 2)
        grad_out[1] = scatter.total(1)
        small_out[...] = scatter.small_stage(part, 4)
        grad_out[0] = scatter.total(0)
        scatter.finish(part)
    else:
        small_out[...] = part[...]
    input_copy.wait()


def run_backward(vector_params, part, saved, rows, length):
    fused = lax.axis_size("dp") == 8 and lax.axis_size("mp") == 4
    hbm, vmem = pl.BlockSpec(memory_space=pl.ANY), pl.BlockSpec(memory_space=pltpu.VMEM)
    tokens = rows * length
    flat = (tokens, D)
    width = D // 4
    block = (4, 2, SLICE, D)
    shape = jax.ShapeDtypeStruct
    dma = pltpu.SemaphoreType.DMA
    whole_grad = shape((3, SLICE, D), F32) if fused else shape((3, 4) + block, BF)
    saved = [saved[0].reshape(3, 4, D, D)] + list(saved[1:])
    grads, sums, input_grad = pl.pallas_call(
        functools.partial(backward_kernel, fused, rows, length),
        out_shape=(whole_grad, shape((SMALL, D), F32), shape(flat, F32)),
        in_specs=[vmem] * 2 + [hbm] * 10,
        out_specs=(vmem if fused else hbm, vmem, hbm),
        scratch_shapes=([pltpu.VMEM(s, t) for s, t in Scatter.buffers] + [dma(s) for s in Scatter.sems] if fused else [])
        + [
            pltpu.VMEM((8,) + block, BF),
            pltpu.VMEM((4, D, D), BF),
            pltpu.VMEM((2,) + flat, BF),
            pltpu.VMEM((2,) + flat, BF),
            pltpu.VMEM(flat, BF),
            pltpu.VMEM(flat, F32),
            pltpu.VMEM(flat, F32),
            pltpu.VMEM((tokens, 128), F32),
            pltpu.VMEM(flat, BF),
            pltpu.VMEM((2, D, tokens), BF),
            pltpu.VMEM((2, D // HEAD // 4, length, length), BF),
            pltpu.VMEM((2, tokens, width), BF),
            pltpu.VMEM((tokens, width), BF),
            pltpu.VMEM((SMALL, D), F32),
            pltpu.VMEM((VECTORS, D), F32),
            dma((4,)),
            dma((2,)),
            dma((2,)),
            dma((2,)),
            dma((2,)),
            dma((2,)),
            dma((4,)),
        ],
        compiler_params=pltpu.CompilerParams(
            collective_id=1 if fused else None, has_side_effects=True, vmem_limit_bytes=VMEM_MOST
        ),
        name="backward",
    )(vector_params, part, *saved)
    if not fused:
        parts = lax.axis_size("dp")
        grads = lax.psum_scatter(grads.reshape(3, 4, D, D), "dp", scatter_dimension=2, tiled=True)
        grads = lax.psum_scatter(grads, "mp", scatter_dimension=1, tiled=True)
        grads = grads.reshape(3, D // parts, D).astype(F32)
        sums = lax.psum(sums, ("dp", "mp"))
    return input_grad, grads, sums


RATES = (D ** (-0.5), 0.5, (D // 16) ** (-0.5), D ** (-0.5), 0.5, FF ** (-0.5), 0.3)


def update_kernel(reduced, sums, result_in, input_in, *refs):
    state, outs, result_out, input_out, result, input_grad, sems = refs[:21], refs[21:49], *refs[49:]
    moves = [
        (pltpu.make_async_copy(input_in, input_grad, sems.at[0]), pltpu.make_async_copy(input_grad, input_out, sems.at[1])),
        (pltpu.make_async_copy(result_in, result, sems.at[2]), pltpu.make_async_copy(result, result_out, sems.at[3])),
    ]
    for load, _ in moves:
        load.start()
    dp, mp = lax.axis_index("dp"), lax.axis_index("mp")
    groups = lax.axis_size("mp")
    width = D // groups
    own = width // HEAD

    def update(i, gradient, at=Ellipsis):
        new = adam_update(*(state[3 * i + j][at] for j in range(3)), gradient, RATES[i])
        for j in range(4):
            outs[4 * i + j][at] = new[j]

    update(3, reduced[1])
    for load, store in moves:
        load.wait()
        store.start()
    mixing = reduced[0]
    for j in range(3):
        update(0, mixing[:, j * width : (j + 1) * width], j)
    update(2, mixing[:, 3 * width :].T)
    update(5, reduced[2])

    def lanes(row, count, start):
        return pltpu.roll(sums[pl.ds(row, count), :], lax.rem(D - start, D), 1)

    piece = state[3].shape[2]
    moved = lanes(6 + mp, 1, dp * piece)
    for j in (0, 1):
        for h in range(own):
            at = 2 * j * width + h * HEAD
            update(1, moved[:, at : at + piece], (h, slice(j, j + 1)))
    piece = state[12].shape[0]
    moved = lanes(10 + mp, 1, dp * piece)
    blocks = [moved[:, b * HEAD : b * HEAD + piece] for b in range(D // HEAD)]
    update(4, jnp.concatenate(blocks, axis=0).T)
    piece = state[18].shape[1]
    update(6, lanes(0, 8, (dp * groups + mp) * piece)[0:6, 0:piece])
    for _, store in moves:
        store.wait()


AXES = ((0, 1, 2), (1, 0, 2), (0, 1), (0, 1), (1, 0), (1, 0), (0, 1))


def update_all(state, reduced, sums, result, input_grad):
    hbm, vmem = pl.BlockSpec(memory_space=pl.ANY), pl.BlockSpec(memory_space=pltpu.VMEM)
    state = [s.transpose(AXES[i // 3]) for i, s in enumerate(state)]
    shapes = []
    for i in range(7):
        shapes = shapes + [jax.ShapeDtypeStruct(state[3 * i].shape, t) for t in (F32, F32, F32, BF)]
    kept = [jax.ShapeDtypeStruct(a.shape, a.dtype) for a in (result, input_grad)]
    *new, result, input_grad = pl.pallas_call(
        update_kernel,
        out_shape=tuple(shapes + kept),
        in_specs=[vmem] * 2 + [hbm] * 2 + [vmem] * 21,
        out_specs=(vmem,) * 28 + (hbm,) * 2,
        scratch_shapes=[pltpu.VMEM(a.shape, a.dtype) for a in kept] + [pltpu.SemaphoreType.DMA((4,))],
        name="update",
    )(reduced, sums, result, input_grad, *state)
    return result, input_grad, tuple(s.transpose(AXES[i // 4]) for i, s in enumerate(new))


def per_device(
    activations,
    cotangent,
    segments,
    triple_weight,
    query_value_bias,
    output_weight,
    expand_weight,
    expand_bias,
    shrink_weight,
    vector_params,
    *state,
):
    rows, length, _ = activations.shape
    weights = (triple_weight, output_weight, expand_weight, shrink_weight)
    *saved, result, part = run_forward(
        activations, cotangent, segments, vector_params, weights, (query_value_bias, expand_bias)
    )
    input_grad, reduced, sums = run_backward(vector_params, part, saved, rows, length)
    result, input_grad, new = update_all(state, reduced, sums, result, input_grad)
    return (result.reshape(activations.shape), input_grad.reshape(activations.shape)) + new


STATE_SPECS = (
    P(None, "dp", "mp"),
    P(None, "mp", "dp"),
    P("mp", "dp"),
    P("dp", "mp"),
    P("mp", "dp"),
    P("mp", "dp"),
    P(None, ("dp", "mp")),
)


def solution(mesh):
    rows = P(("dp", "mp"), None, None)
    placed = (
        rows,
        rows,
        P("dp", None),
        P(None, None, "mp"),
        P(None, "mp", None),
        P("mp", None),
        P(None, "mp"),
        P("mp", None),
        P("mp", None),
        P(),
    )
    for spec in STATE_SPECS:
        placed = placed + (spec,) * 3
    out_specs = (rows, rows)
    for spec in STATE_SPECS:
        out_specs = out_specs + (spec,) * 4
    return jax.shard_map(per_device, mesh=mesh, in_specs=placed, out_specs=out_specs, check_vma=False)
```

```python
import functools

import jax
import jax.numpy as jnp
from jax import lax
from jax.experimental import pallas as pl
from jax.experimental.pallas import tpu as pltpu
from jax.sharding import PartitionSpec as P

D = 768
HEAD = 64
FF = 3072
STEP = 10


NORM_EPS = 1e-05
BETA_ONE = 0.5
BETA_TWO = 0.6
ADAM_EPS = 1e-08
WEIGHT_DECAY = 0.01
MASKED = -1e30
SQRT_HALF = 0.7071067811865476
INV_ROOT_TAU = 0.3989422804014327


def norm_forward(summed, gain, shift):
    centre = summed - jnp.mean(summed, axis=-1, keepdims=True)
    scale = lax.rsqrt(jnp.mean(centre * centre, axis=-1, keepdims=True) + NORM_EPS)
    normed = centre * scale
    return (gain * normed + shift, normed, scale)


def norm_backward(gradient, gain, normed, scale):
    scaled = gradient * gain
    centred = scaled - jnp.mean(scaled, axis=-1, keepdims=True)
    return scale * (centred - normed * jnp.mean(scaled * normed, axis=-1, keepdims=True))


def adam_update(master, first, second, gradient, rate):
    first_new = BETA_ONE * first + (1.0 - BETA_ONE) * gradient
    second_new = BETA_TWO * second + (1.0 - BETA_TWO) * gradient * gradient
    corrected = first_new / (1.0 - BETA_ONE**STEP)
    spread = jnp.sqrt(second_new / (1.0 - BETA_TWO**STEP))
    master_new = master - rate * (corrected / (spread + ADAM_EPS) + WEIGHT_DECAY * master)
    return (master_new, first_new, second_new, master_new.astype(jnp.bfloat16))


MESH = pl.DeviceIdType.MESH
BF = jnp.bfloat16
F32 = jnp.float32
HALF = 48
SLICE = 96
SMALL = 16
VECTORS = 8


def place():
    p, z = lax.axis_index("dp"), lax.axis_index("mp")
    core, xy = p % 2, p // 2
    x, y = xy % 2, xy // 2
    return p, z, core, xy, p + 1 - 2 * core, p + 2 - 4 * x, p + 4 - 8 * y, xy + 1 - 2 * x, xy + 2 - 4 * y


def remote(src, dst, send_sem, recv_sem, p, z):
    return pltpu.make_async_remote_copy(
        src_ref=src, dst_ref=dst, send_sem=send_sem, recv_sem=recv_sem, device_id=(p, z), device_id_type=MESH
    )


def greet(p, z, pc, px, py):
    barrier = pltpu.get_barrier_semaphore()
    for peer in ((pc, z), (px, z), (py, z), (p, (z + 1) % 4), (p, (z + 2) % 4), (p, (z + 3) % 4)):
        pl.semaphore_signal(barrier, inc=1, device_id=peer, device_id_type=MESH)
    pl.semaphore_wait(barrier, 6)


class Gather:
    steps = [(0, 1), (0, 2), (0, 3), (1, 1), (2, 1), (1, 2), (2, 2), (1, 3), (2, 3)]
    sems = [(3,)] + [(3, 3)] * 12 + [(3,)] * 2

    def __init__(self, mats, whole, bias, biases, sems):
        self.mats, self.whole, self.bias, self.biases = mats, whole, bias, biases
        (self.ls, self.zs, self.zr, self.xs, self.xr, self.ys, self.yr, self.as_, self.ar, self.bs, self.br, self.cs,
         self.cr, self.ss, self.sr) = sems
        self.where = place()

    def local(self, m):
        z = self.where[1]
        return pltpu.make_async_copy(self.mats[m - 1], self.whole.at[m, z], self.ls.at[m])

    def small(self, d):
        p, z = self.where[:2]
        return remote(self.bias, self.biases.at[z], self.ss.at[d - 1], self.sr.at[d - 1], p, (z + d) % 4)

    def along_z(self, m, d):
        p, z, core, xy = self.where[:4]
        own = self.whole.at[m, z] if m == 0 else self.mats[m - 1]
        return remote(own.at[xy, core], self.whole.at[m, z, xy, core], self.zs.at[m, d - 1],
                      self.zr.at[m, d - 1], p, (z + d) % 4)

    def plane(self, m, d, block, rows, send_sem, recv_sem, peer):
        z = self.where[1]
        part = self.whole.at[m, (z + 4 - d) % 4, block, self.where[2], rows]
        return remote(part, part, send_sem.at[m, d - 1], recv_sem.at[m, d - 1], peer, z)

    def to_x(self, m, d):
        return self.plane(m, d, self.where[3], slice(None), self.xs, self.xr, self.where[5])

    def to_y(self, m, d):
        return self.plane(m, d, self.where[3], slice(None), self.ys, self.yr, self.where[6])

    def on_to_y(self, m, d):
        return self.plane(m, d, self.where[7], pl.ds(0, HALF), self.as_, self.ar, self.where[6])

    def on_to_x(self, m, d):
        return self.plane(m, d, self.where[8], pl.ds(HALF, HALF), self.bs, self.br, self.where[5])

    def to_core(self, m, d):
        z = self.where[1]
        part = self.whole.at[m, (z + 4 - d) % 4, :, self.where[2]]
        return remote(part, part, self.cs.at[m, d - 1], self.cr.at[m, d - 1], self.where[4], z)

    def begin(self):
        p, z, _, _, pc, px, py = self.where[:7]
        greet(p, z, pc, px, py)
        for d in (1, 2, 3):
            self.along_z(0, d).start()
            self.small(d).start()

    def run(self, kind, i):
        m, d = self.steps[i]
        if kind == 0:
            self.along_z(m, d).wait_recv()
            if i < 3:
                self.small(d).wait_recv()
            self.to_x(m, d).start()
            self.to_y(m, d).start()
            if m < 2:
                self.along_z(m + 1, d).start()
        elif kind == 1:
            self.to_x(m, d).wait_recv()
            self.to_y(m, d).wait_recv()
            self.on_to_y(m, d).start()
            self.on_to_x(m, d).start()
        elif kind == 2:
            self.on_to_y(m, d).wait_recv()
            self.on_to_x(m, d).wait_recv()
            self.to_core(m, d).start()
        else:
            self.to_core(m, d).wait_recv()

    def finish(self):
        for d in (1, 2, 3):
            self.small(d).wait_send()
        for m, d in self.steps:
            for copy in (self.along_z, self.to_x, self.to_y, self.on_to_y, self.on_to_x, self.to_core):
                copy(m, d).wait_send()


class Scatter:
    steps = [(m, k) for k in (0, 3, 2, 1) for m in (2, 1)] + [(0, k) for k in (0, 3, 2, 1)]
    slots = [k + 4 * j for k in range(4) for j in (0, 1)] + list(range(4))
    buffers = [((12, 4, SLICE, D), BF)] + [((12, 2, HALF, D), BF)] * 2 + [((12, HALF, D), BF)] * 2 + [
        ((3, 3, SLICE, D), BF), ((3, 4, SLICE, D), BF), ((6, SMALL, D), F32), ((3, SMALL, D), F32)]
    sems = [(12,)] * 2 + [(12, 2)] * 4 + [(12,)] * 4 + [(3, 3)] * 2 + [(6,)] * 2

    def __init__(self, grads, buffers, sems):
        self.grads = grads
        self.sum, self.rx, self.ry, self.ra, self.rb, self.rz, self.plane, self.rv, self.sv = buffers
        (self.cs, self.cr, self.xs, self.xr, self.ys, self.yr, self.as_, self.ar, self.bs, self.br, self.zs, self.zr,
         self.ss, self.sr) = sems
        self.where = place()

    def to_core(self, i):
        _, z, core, _, pc = self.where[:5]
        return remote(self.grads.at[self.slots[i], :, 1 - core], self.sum.at[i], self.cs.at[i], self.cr.at[i], pc, z)

    def to_x(self, i, t):
        q = (self.where[7], 3 - self.where[3])[t]
        return remote(self.sum.at[i, q, pl.ds(0, HALF)], self.rx.at[i, t], self.xs.at[i, t], self.xr.at[i, t],
                      self.where[5], self.where[1])

    def to_y(self, i, t):
        q = (self.where[8], 3 - self.where[3])[t]
        return remote(self.sum.at[i, q, pl.ds(HALF, HALF)], self.ry.at[i, t], self.ys.at[i, t], self.yr.at[i, t],
                      self.where[6], self.where[1])

    def on_to_y(self, i):
        return remote(self.sum.at[i, self.where[8], pl.ds(0, HALF)], self.ra.at[i], self.as_.at[i], self.ar.at[i],
                      self.where[6], self.where[1])

    def on_to_x(self, i):
        return remote(self.sum.at[i, self.where[7], pl.ds(HALF, HALF)], self.rb.at[i], self.bs.at[i], self.br.at[i],
                      self.where[5], self.where[1])

    def to_owner(self, m, k, d):
        p = self.where[0]
        return remote(self.plane.at[m, k], self.rz.at[m, d - 1], self.zs.at[m, d - 1], self.zr.at[m, d - 1], p, k)

    def along_z(self, m, d):
        return self.to_owner(m, (self.where[1] + d) % 4, d)

    def begin(self):
        p, z, _, _, pc, px, py = self.where[:7]
        greet(p, z, pc, px, py)

    def run(self, kind, j):
        core, xy, xyx, xyy = self.where[2], self.where[3], self.where[7], self.where[8]
        low, high = slice(0, HALF), slice(HALF, SLICE)
        if kind == 0:
            self.to_core(j).start()
        elif kind == 1:
            self.to_core(j).wait_recv()

            @pl.loop(0, 4)
            def _(q):
                mine = self.grads[self.slots[j], q, core].astype(F32)
                self.sum[j, q] = (self.sum[j, q].astype(F32) + mine).astype(BF)

            for t in (1, 0):
                self.to_x(j, t).start()
                self.to_y(j, t).start()
        elif kind == 2:
            for t in (0, 1):
                self.to_x(j, t).wait_recv()
                self.to_y(j, t).wait_recv()
            self.sum[j, xyy, low] = (self.sum[j, xyy, low].astype(F32) + self.rx[j, 1].astype(F32)).astype(BF)
            self.sum[j, xyx, high] = (self.sum[j, xyx, high].astype(F32) + self.ry[j, 1].astype(F32)).astype(BF)
            self.on_to_y(j).start()
            self.on_to_x(j).start()
        else:
            m, k = self.steps[j]
            self.on_to_y(j).wait_recv()
            self.on_to_x(j).wait_recv()
            self.plane[m, k, low] = (
                self.sum[j, xy, low].astype(F32) + self.rx[j, 0].astype(F32) + self.ra[j].astype(F32)
            ).astype(BF)
            self.plane[m, k, high] = (
                self.sum[j, xy, high].astype(F32) + self.ry[j, 0].astype(F32) + self.rb[j].astype(F32)
            ).astype(BF)
            z = self.where[1]
            pl.when(z != k)(lambda: self.to_owner(m, k, (k + 4 - z) % 4).start())

    def total(self, m):
        for d in (1, 2, 3):
            self.along_z(m, d).wait_recv()
        own = self.plane[m, self.where[1]].astype(F32)
        return own + self.rz[m, 0].astype(F32) + self.rz[m, 1].astype(F32) + self.rz[m, 2].astype(F32)

    def small_to(self, s, src, p, z):
        return remote(src, self.rv.at[s], self.ss.at[s], self.sr.at[s], p, z)

    def small_copy(self, part, c):
        p, z, _, _, pc, px, py = self.where[:7]
        if c == 0:
            return self.small_to(0, part, pc, z)
        if c == 1:
            return self.small_to(1, self.sv.at[0], px, z)
        if c == 2:
            return self.small_to(2, self.sv.at[1], py, z)
        return self.small_to(c, self.sv.at[2], p, (z + c - 2) % 4)

    def small_stage(self, part, i):
        if i == 0:
            self.small_copy(part, 0).start()
        elif i < 4:
            self.small_copy(part, i - 1).wait_recv()
            before = part[...] if i == 1 else self.sv[i - 2]
            self.sv[i - 1] = before + self.rv[i - 1]
            for c in (i,) if i < 3 else (3, 4, 5):
                self.small_copy(part, c).start()
        else:
            for c in (3, 4, 5):
                self.small_copy(part, c).wait_recv()
            return self.sv[2] + self.rv[3] + self.rv[4] + self.rv[5]

    def finish(self, part):
        for c in range(6):
            self.small_copy(part, c).wait_send()
        for i in range(len(self.steps)):
            if self.slots[i] not in self.slots[i + 1 :]:
                self.to_core(i).wait_send()
            self.on_to_y(i).wait_send()
            self.on_to_x(i).wait_send()
            for t in (0, 1):
                self.to_x(i, t).wait_send()
                self.to_y(i, t).wait_send()
        for m in range(3):
            for d in (1, 2, 3):
                self.along_z(m, d).wait_send()


def mm(a, b, dims):
    return lax.dot_general(a, b, (dims, ((), ())), preferred_element_type=jnp.float32)


def pack_weights(triple_weight, output_weight, expand_weight, shrink_weight):
    width = triple_weight.shape[2]
    mixing = jnp.concatenate([triple_weight.transpose(1, 0, 2).reshape(D, 3 * width), output_weight.T], axis=1)
    return mixing, expand_weight, shrink_weight


def pack_biases(query_value_bias, expand_bias):
    pair = query_value_bias.reshape(2, -1)
    none = jnp.zeros_like(pair[0])
    first = jnp.concatenate([pair[0], none, pair[1], none])
    return jnp.concatenate([first[None], expand_bias.reshape(1, -1), jnp.zeros((VECTORS - 2, D), BF)]).astype(F32)


TN = ((0,), (0,))
NT = ((1,), (1,))
NN = ((1,), (0,))
CHUNK = 384
STRIP = 128
TILE = 256
VMEM_MOST = 60 << 20
EVENTS = {
    "block": {(1, 0): ((1, 0), (0, 1), (2, 0), (0, 2), (3, 0)), (2, 0): ((0, 5), (1, 3), (3, 1)), (3, 0): ((2, 3),)},
    "project": {(1, 2): ((1, 1),)},
    "attend": {(0, 3): ((0, 0),), (1, 0): ((0, 3),), (1, 2): ((1, 2),), (1, 3): ((2, 1),), (2, 0): ((2, 2), (0, 7)), (2, 3): ((1, 5), (0, 4), (3, 2)), (3, 1): ((1, 7), (3, 3)), (3, 2): ((2, 5), (0, 6))},
    "turn": {},
    "norm": {(0, 0): ((1, 4), (0, 8), (3, 5), (2, 7))},
    "feed": {(1, 0): ((1, 8), (3, 4)), (2, 0): ((3, 6),)},
    "expand": {(0, 2): ((1, 6),), (1, 2): ((2, 6),), (2, 2): ((3, 8),)},
    "shrink": {(0, 1): ((3, 7),), (0, 2): ((2, 4),), (1, 1): ((2, 8),)},
}


def tile(n):
    return pl.ds(pl.multiple_of(n * TILE, TILE), TILE)


def strip(s):
    return pl.ds(pl.multiple_of(s * STRIP, STRIP), STRIP)


def forward_kernel(fused, rows, length, *refs):
    n_sem = len(Gather.sems) if fused else 0
    x_in, cot_in, seg_ref, vec_in = refs[:4]
    n_in = 10 if fused else 6
    ins = refs[4:n_in]
    outs = refs[n_in : n_in + 12]
    (whole_out, qkv_out, ctx_out, prob_out, act_out, slope_out, normed_out, rstd_out, ds_out, turned_out, result_out,
     part_out) = outs
    rest = refs[n_in + 12 :]
    gather_sems, rest = rest[:n_sem], rest[n_sem:]
    (whole, bias, biases, joint, vec, x, cot, qkv, ctx, prob, act, slope, mixed, normed, rstd, low, turned,
     result, part, in_sem, w_sem, qkv_sem, ctx_sem, prob_sem, act_sem, slope_sem, end_sem) = rest
    tokens = rows * length
    strips = tokens // STRIP
    heads = D // HEAD // 4
    width = heads * HEAD
    z_own = lax.axis_index("mp")
    x_copy = pltpu.make_async_copy(x_in, x, in_sem.at[0])
    cot_copy = pltpu.make_async_copy(cot_in, cot, in_sem.at[1])
    x_copy.start()
    if fused:
        triple_in, output_in, e_ref, s_ref, qv_ref, eb_ref = ins
        joint_copies = [
            pltpu.make_async_copy(triple_in.at[j], joint.at[pl.ds(j * width, width)], in_sem.at[2 + j]) for j in range(3)
        ] + [pltpu.make_async_copy(output_in, joint.at[pl.ds(3 * width, width)], in_sem.at[5])]
        for copy in joint_copies:
            copy.start()
        gather = Gather((e_ref, s_ref), whole, bias, biases, gather_sems)
        bias[...] = jnp.zeros_like(bias)
        for h in range(heads):
            for j in (0, 1):
                at = slice(2 * j * width + h * HEAD, 2 * j * width + (h + 1) * HEAD)
                bias[0:1, at] = qv_ref[h, j : j + 1, :].astype(F32)
        for b in range(D // HEAD):
            bias[1:2, b * HEAD : (b + 1) * HEAD] = eb_ref[b : b + 1, :].astype(F32)
        for copy in joint_copies:
            copy.wait()
        for j in (0, 1):
            half = joint[:, j * CHUNK : (j + 1) * CHUNK].T
            whole[0, z_own, 2 * j : 2 * j + 2] = half.reshape(2, 2, SLICE, D)
        gather.begin()
        gather.local(1).start()
        gather.local(2).start()
        own_bias = pltpu.make_async_copy(bias, biases.at[z_own], w_sem.at[0])
        own_bias.start()
        own_bias.wait()
    else:
        copy = pltpu.make_async_copy(ins[0], whole, w_sem.at[0])
        copy.start()
        small = pltpu.make_async_copy(ins[1], biases, w_sem.at[1])
        small.start()
        copy.wait()
        small.wait()
    cot_copy.start()
    vec[0:6, :] = vec_in[...].astype(F32)

    def block(i):
        return (z_own + 3 * i) % 4

    def columns(m, z, n):
        return whole[m, z, :, :, :, tile(n)].reshape(D, TILE)

    def turned_copy(slot):
        return pltpu.make_async_copy(turned.at[slot], turned_out.at[slot], end_sem.at[slot])

    def qkv_copy(i):
        return pltpu.make_async_copy(qkv.at[i % 2], qkv_out.at[block(i)], qkv_sem.at[i % 2])

    def ctx_copy(i):
        return pltpu.make_async_copy(ctx.at[i % 2], ctx_out.at[block(i)], ctx_sem.at[i % 2])

    def prob_copy(i, r):
        return pltpu.make_async_copy(prob.at[r], prob_out.at[block(i), r], prob_sem.at[r])

    def act_copy(i):
        return pltpu.make_async_copy(act.at[i % 2], act_out.at[block(i)], act_sem.at[i % 2])

    def slope_copy(i):
        return pltpu.make_async_copy(slope.at[i % 2], slope_out.at[block(i)], slope_sem.at[i % 2])

    def whole_copy(m):
        return pltpu.make_async_copy(whole.at[m], whole_out.at[m], w_sem.at[m])

    def events(place, i=0, n=0):
        for (a, b), due in EVENTS[place].items() if fused else ():

            @pl.when((i == a) & (n == b))
            def _(due=due):
                for kind, step in due:
                    gather.run(kind, step)

    x_copy.wait()

    @pl.loop(0, 4)
    def _(i):
        events("block", i)
        z = block(i)
        slot = i % 2

        @pl.when(i >= 2)
        def _():
            qkv_copy(i - 2).wait()
            ctx_copy(i - 2).wait()

        @pl.loop(0, 3)
        def _(n):
            add = biases[z, 0:1, tile(n)]
            qkv[slot, :, tile(n)] = (mm(x[...], columns(0, z, n), NN) + add).astype(BF)
            events("project", i, n)

        qkv_copy(i).start()

        @pl.loop(0, rows)
        def _(r):
            at = pl.ds(pl.multiple_of(r * length, 32), length)
            pl.when(i >= 1)(lambda: prob_copy(i - 1, r).wait())
            pair = seg_ref[pl.ds(z_own * rows + r, 1), :]
            number = lax.broadcasted_iota(jnp.int32, (8, length), 0)
            among = jnp.where(number == pair, 1.0, 0.0).astype(BF)
            mask = (mm(among, among, TN) - 1.0) * -MASKED
            done = []
            for h in range(heads):
                q = qkv[slot, at, h * HEAD : (h + 1) * HEAD] * jnp.asarray(HEAD ** (-0.5), BF)
                k = qkv[slot, at, width + h * HEAD : width + (h + 1) * HEAD]
                v = qkv[slot, at, 2 * width + h * HEAD : 2 * width + (h + 1) * HEAD]
                scores = mm(k, q, NT) + mask
                weights = jnp.exp(scores - jnp.max(scores, axis=0, keepdims=True))
                share = 1.0 / jnp.sum(weights, axis=0, keepdims=True)
                probs = (weights * share).astype(BF)
                prob[r, h] = probs
                done.append(mm(v, probs, TN).astype(BF).T)
            ctx[slot, at, :] = jnp.concatenate(done, axis=1)
            prob_copy(i, r).start()
            events("attend", i, r)

        ctx_copy(i).start()

        @pl.when(i == 0)
        def _():
            @pl.loop(0, strips)
            def _(s):
                value = x[strip(s), :]
                mixed[strip(s), :] = value.astype(F32) + vec[2:3, :]
                turned[0, :, strip(s)] = value.T

            turned_copy(0).start()
            events("turn")

        @pl.loop(0, tokens // CHUNK)
        def _(c):
            at = pl.ds(pl.multiple_of(c * CHUNK, CHUNK), CHUNK)
            add = mm(ctx[slot, at, :], whole[0, z].reshape(D, D)[:, 3 * width :], NT)
            mixed[at, :] = mixed[at, :] + add

    whole_copy(0).start()

    @pl.loop(0, strips)
    def _(s):
        at = strip(s)
        hidden, normal, scale = norm_forward(mixed[at, :], vec[0:1, :], vec[1:2, :])
        normed[at, :] = normal
        rstd[at, :] = jnp.broadcast_to(scale, (STRIP, 128))
        mixed[at, :] = hidden + vec[5:6, :]
        hidden = hidden.astype(BF)
        low[at, :] = hidden
        turned[1, :, at] = hidden.T

    events("norm")
    turned_copy(1).start()
    normed_copy = pltpu.make_async_copy(normed, normed_out, end_sem.at[3])
    normed_copy.start()
    rstd_copy = pltpu.make_async_copy(rstd, rstd_out, end_sem.at[4])
    rstd_copy.start()
    if fused:
        gather.local(1).wait()
        gather.local(2).wait()

    @pl.loop(0, 4)
    def _(i):
        events("feed", i)
        z = block(i)
        slot = i % 2

        @pl.when(i >= 2)
        def _():
            act_copy(i - 2).wait()
            slope_copy(i - 2).wait()

        @pl.loop(0, 3)
        def _(n):
            u = mm(low[...], columns(1, z, n), NN) + biases[z, 1:2, tile(n)]
            cumulative = 0.5 + 0.5 * lax.erf(u * SQRT_HALF)
            act[slot, :, tile(n)] = (u * cumulative).astype(BF)
            slope[slot, :, tile(n)] = (cumulative + u * jnp.exp(-0.5 * u * u) * INV_ROOT_TAU).astype(BF)
            events("expand", i, n)

        act_copy(i).start()
        slope_copy(i).start()

        @pl.loop(0, 3)
        def _(n):
            mixed[:, tile(n)] = mixed[:, tile(n)] + mm(act[slot], columns(2, z, n), NN)
            events("shrink", i, n)

        @pl.when(i == 2)
        def _():
            whole_copy(1).start()
            whole_copy(2).start()

    normed_copy.wait()
    cot_copy.wait()
    part[...] = jnp.zeros_like(part)

    @pl.loop(0, strips)
    def _(s):
        at = strip(s)
        block_result, normal, scale = norm_forward(mixed[at, :], vec[3:4, :], vec[4:5, :])
        result[at, :] = block_result.astype(BF)
        back = cot[at, :].astype(F32)
        dsummed = norm_backward(back, vec[3:4, :], normal, scale)
        normed[at, :] = dsummed
        turned[2, :, at] = dsummed.astype(BF).T
        part[3:4, :] += jnp.sum(back * normal, axis=0, keepdims=True)
        part[4:5, :] += jnp.sum(back, axis=0, keepdims=True)
        part[5:6, :] += jnp.sum(dsummed, axis=0, keepdims=True)

    last = [
        turned_copy(2),
        pltpu.make_async_copy(normed, ds_out, end_sem.at[5]),
        pltpu.make_async_copy(result, result_out, end_sem.at[6]),
        pltpu.make_async_copy(part, part_out, end_sem.at[7]),
    ]
    for copy in last:
        copy.start()
    for i in (2, 3):
        qkv_copy(i).wait()
        ctx_copy(i).wait()
        act_copy(i).wait()
        slope_copy(i).wait()
    for r in range(rows):
        prob_copy(3, r).wait()
    turned_copy(0).wait()
    turned_copy(1).wait()
    rstd_copy.wait()
    for m in range(3):
        whole_copy(m).wait()
    for copy in last:
        copy.wait()
    if fused:
        gather.finish()


def run_forward(x, cot, segments, vector_params, weights, biases):
    rows, length, _ = x.shape
    tokens = rows * length
    fused = lax.axis_size("dp") == 8 and lax.axis_size("mp") == 4
    hbm, vmem = pl.BlockSpec(memory_space=pl.ANY), pl.BlockSpec(memory_space=pltpu.VMEM)
    flat = (tokens, D)
    width = D // 4
    block = (4, 2, SLICE, D)
    dense = [x.reshape(flat), cot.reshape(flat), segments, vector_params]
    if fused:
        triple, output, expand, shrink = weights
        held = [triple.transpose(0, 2, 1), output, expand.reshape(block), shrink.reshape(block)]
        held = held + [biases[0].transpose(1, 0, 2), biases[1]]
        spaces = [hbm, hbm, hbm, hbm, vmem, vmem]
    else:
        mats = pack_weights(*weights)
        held = [jnp.stack([lax.all_gather(m, "mp", axis=0) for m in mats]).reshape((3, 4) + block)]
        held = held + [lax.all_gather(pack_biases(*biases), "mp", axis=0)]
        spaces = [hbm, hbm]
    probs = (rows, D // HEAD // 4, length, length)
    shape = jax.ShapeDtypeStruct
    dma = pltpu.SemaphoreType.DMA
    return pl.pallas_call(
        functools.partial(forward_kernel, fused, rows, length),
        out_shape=(
            shape((3, 4) + block, BF),
            shape((4,) + flat, BF),
            shape((4, tokens, width), BF),
            shape((4,) + probs, BF),
            shape((4,) + flat, BF),
            shape((4,) + flat, BF),
            shape(flat, F32),
            shape((tokens, 128), F32),
            shape(flat, F32),
            shape((3, D, tokens), BF),
            shape(flat, BF),
            shape((VECTORS, D), F32),
        ),
        in_specs=[hbm, hbm, vmem, vmem] + spaces,
        out_specs=(hbm,) * 12,
        scratch_shapes=([dma(s) for s in Gather.sems] if fused else [])
        + [
            pltpu.VMEM((3, 4) + block, BF),
            pltpu.VMEM((VECTORS, D), F32),
            pltpu.VMEM((4, VECTORS, D), F32),
            pltpu.VMEM((D, D), BF),
            pltpu.VMEM((VECTORS, D), F32),
            pltpu.VMEM(flat, BF),
            pltpu.VMEM(flat, BF),
            pltpu.VMEM((2,) + flat, BF),
            pltpu.VMEM((2, tokens, width), BF),
            pltpu.VMEM(probs, BF),
            pltpu.VMEM((2,) + flat, BF),
            pltpu.VMEM((2,) + flat, BF),
            pltpu.VMEM(flat, F32),
            pltpu.VMEM(flat, F32),
            pltpu.VMEM((tokens, 128), F32),
            pltpu.VMEM(flat, BF),
            pltpu.VMEM((3, D, tokens), BF),
            pltpu.VMEM(flat, BF),
            pltpu.VMEM((VECTORS, D), F32),
            dma((6,)),
            dma((3,)),
            dma((2,)),
            dma((2,)),
            dma((rows,)),
            dma((2,)),
            dma((2,)),
            dma((8,)),
        ],
        compiler_params=pltpu.CompilerParams(
            collective_id=0 if fused else None, has_side_effects=True, vmem_limit_bytes=VMEM_MOST
        ),
        name="forward",
    )(*dense, *held)


BACK_EVENTS = {
    "shrink": {(0, 2): ((0, 0),), (1, 2): ((0, 2),), (2, 2): ((0, 4),), (3, 1): ((3, 1),), (3, 2): ((0, 6),)},
    "slope": {(1, 1): ((1, 1),), (2, 0): ((2, 1), (1, 3)), (2, 2): ((3, 0),), (3, 0): ((1, 5),), (3, 2): ((2, 3),)},
    "expand": {(0, 2): ((0, 1), (1, 0)), (1, 1): ((2, 0),), (1, 2): ((0, 3), (1, 2)), (2, 2): ((0, 5), (1, 4)), (3, 2): ((0, 7), (1, 6))},
    "hidden": {(2, 1): ((2, 2),), (3, 2): ((2, 4),)},
    "norm": {(0, 0): ((3, 2), (1, 7))},
    "attend": {(0, 0): ((2, 5),), (0, 1): ((3, 3),), (1, 1): ((2, 7), (1, 8)), (1, 2): ((3, 5),), (2, 1): ((2, 8), (1, 9)), (3, 2): ((2, 9),), (3, 3): ((1, 10),)},
    "project": {(0, 0): ((0, 8), (2, 6)), (1, 0): ((0, 9), (3, 6), (3, 7)), (2, 0): ((0, 10), (3, 8)), (3, 0): ((0, 11),)},
    "pull": {(0, 1): ((3, 4),), (2, 2): ((3, 9),)},
    "last": {(0, 0): ((1, 11), (2, 10), (2, 11), (3, 10), (3, 11))},
}


def turn_block(j):
    return 3 * j % 4


def backward_kernel(fused, rows, length, *refs):
    n_sem = len(Scatter.sems) if fused else 0
    n_buf = len(Scatter.buffers) if fused else 0
    (vec_in, part_in, whole, qkv_in, ctx_in, prob_in, act_in, slope_in, normed_in, rstd_in, ds_in, turned_in) = refs[:12]
    grad_out, small_out, input_out = refs[12:15]
    rest = refs[15:]
    buffers, sems, rest = rest[:n_buf], rest[n_buf : n_buf + n_sem], rest[n_buf + n_sem :]
    (grads, weights, wide, tall, dexp, stream, normed, rstd, low, turned, prob, ctx, dctx, part, vec,
     w_sem, wide_sem, tall_sem, prob_sem, ctx_sem, turned_sem, end_sem) = rest
    tokens = rows * length
    strips = tokens // STRIP
    heads = D // HEAD // 4
    width = heads * HEAD

    def weight_copy(m, j, slot):
        return pltpu.make_async_copy(whole.at[m, turn_block(j)], weights.at[slot], w_sem.at[slot])

    def wide_copy(source, j):
        return pltpu.make_async_copy(source.at[turn_block(j)], wide.at[j % 2], wide_sem.at[j % 2])

    def tall_copy(j):
        return pltpu.make_async_copy(slope_in.at[turn_block(j)], tall.at[j % 2], tall_sem.at[j % 2])

    def turned_copy(source, slot):
        return pltpu.make_async_copy(turned_in.at[source], turned.at[slot], turned_sem.at[slot])

    def prob_copy(g):
        return pltpu.make_async_copy(prob_in.at[turn_block(g // rows), g % rows], prob.at[g % 2], prob_sem.at[g % 2])

    def ctx_copy(j):
        return pltpu.make_async_copy(ctx_in.at[turn_block(j)], ctx.at[j % 2], ctx_sem.at[j % 2])

    stream_copy = pltpu.make_async_copy(ds_in, stream, end_sem.at[0])
    normed_copy = pltpu.make_async_copy(normed_in, normed, end_sem.at[1])
    rstd_copy = pltpu.make_async_copy(rstd_in, rstd, end_sem.at[2])
    turned_copy(2, 0).start()
    wide_copy(act_in, 0).start()
    stream_copy.start()
    weight_copy(2, 0, 0).start()
    tall_copy(0).start()
    turned_copy(1, 1).start()
    weight_copy(1, 0, 1).start()
    wide_copy(act_in, 1).start()
    tall_copy(1).start()
    weight_copy(2, 1, 2).start()
    weight_copy(1, 1, 3).start()
    normed_copy.start()
    rstd_copy.start()
    if fused:
        scatter = Scatter(grads, buffers, sems)
        scatter.begin()

    def events(place, j=0, n=0):
        for (a, c), due in BACK_EVENTS[place].items() if fused else ():

            @pl.when((j == a) & (n == c))
            def _(due=due):
                for kind, step in due:
                    scatter.run(kind, step)

    vec[0:6, :] = vec_in[...].astype(F32)
    part[...] = jnp.zeros_like(part)
    part[0:VECTORS, :] = part_in[...]

    def outer(slot, turned_slot, right, lanes, offset=0, size=TILE):
        product = mm(turned[turned_slot], right[:, lanes], NN).astype(BF)
        grads[slot, :, :, :, offset if size != TILE else lanes] = product.reshape(4, 2, SLICE, size)

    def emit(slot, m, z):
        if not fused:
            copy = pltpu.make_async_copy(grads.at[slot], grad_out.at[m, z], end_sem.at[3])
            copy.start()
            copy.wait()

    turned_copy(2, 0).wait()

    @pl.loop(0, 4)
    def _(j):
        half = j % 2
        slot = 2 * half
        z = turn_block(j)
        wide_copy(act_in, j).wait()

        @pl.loop(0, 3)
        def _(n):
            outer(j, 0, wide.at[half], tile(n))
            events("shrink", j, n)

        emit(j, 2, z)

        @pl.when(j == 0)
        def _():
            stream_copy.wait()

            @pl.loop(0, strips)
            def _(s):
                low[strip(s), :] = stream[strip(s), :].astype(BF)

            turned_copy(1, 1).wait()

        weight_copy(2, j, slot).wait()
        tall_copy(j).wait()

        @pl.loop(0, 3)
        def _(n):
            dactive = mm(low[...], weights[slot, tile(n), :], NT)
            value = (dactive * tall[half, :, tile(n)].astype(F32)).astype(BF)
            dexp[:, tile(n)] = value
            part[pl.ds(10 + z, 1), tile(n)] = jnp.sum(value.astype(F32), axis=0, keepdims=True)
            events("slope", j, n)

        @pl.loop(0, 3)
        def _(n):
            outer(4 + j, 1, dexp, tile(n))
            events("expand", j, n)

        emit(4 + j, 1, z)
        weight_copy(1, j, slot + 1).wait()

        @pl.loop(0, 3)
        def _(n):
            stream[:, tile(n)] = stream[:, tile(n)] + mm(dexp[...], weights[slot + 1, tile(n), :], NT)
            events("hidden", j, n)

        @pl.when(j < 2)
        def _():
            wide_copy(act_in, j + 2).start()
            tall_copy(j + 2).start()
            weight_copy(2, j + 2, slot).start()
            weight_copy(1, j + 2, slot + 1).start()

        @pl.when(j == 2)
        def _():
            wide_copy(qkv_in, 0).start()
            weight_copy(0, 0, 0).start()
            weight_copy(0, 1, 1).start()
            ctx_copy(0).start()
            ctx_copy(1).start()
            prob_copy(0).start()

        @pl.when(j == 3)
        def _():
            wide_copy(qkv_in, 1).start()
            weight_copy(0, 2, 2).start()
            weight_copy(0, 3, 3).start()
            turned_copy(0, 0).start()

    normed_copy.wait()
    rstd_copy.wait()

    @pl.loop(0, strips)
    def _(s):
        at = strip(s)
        dhidden, normal = stream[at, :], normed[at, :]
        dmixed = norm_backward(dhidden, vec[0:1, :], normal, rstd[at, 0:1])
        part[0:1, :] += jnp.sum(dhidden * normal, axis=0, keepdims=True)
        part[1:2, :] += jnp.sum(dhidden, axis=0, keepdims=True)
        part[2:3, :] += jnp.sum(dmixed, axis=0, keepdims=True)
        stream[at, :] = dmixed
        dmixed = dmixed.astype(BF)
        low[at, :] = dmixed
        turned[1, :, at] = dmixed.T

    events("norm")
    turned_copy(0, 0).wait()
    dproj = tall
    dproj[:, :, 2 * TILE : D] = jnp.zeros((2, tokens, TILE), BF)

    def pull(j):
        @pl.loop(0, 3)
        def _(n):
            add = mm(dproj[j % 2, :, 0 : 3 * width], weights[j, tile(n), 0 : 3 * width], NT)
            stream[:, tile(n)] = stream[:, tile(n)] + add
            events("pull", j, n)

    @pl.loop(0, 4)
    def _(j):
        half = j % 2
        z = turn_block(j)
        weight_copy(0, j, j).wait()
        wide_copy(qkv_in, j).wait()
        ctx_copy(j).wait()
        dctx[...] = mm(low[...], weights[j, :, 3 * width :], NN).astype(BF)

        @pl.loop(0, rows)
        def _(r):
            at = pl.ds(pl.multiple_of(r * length, 32), length)
            g = j * rows + r
            prob_copy(g).wait()
            pl.when(g + 1 < 4 * rows)(lambda: prob_copy(g + 1).start())
            dq, dk, dv = [], [], []
            scale = jnp.asarray(HEAD ** (-0.5), BF)
            for h in range(heads):
                q = wide[half, at, h * HEAD : (h + 1) * HEAD] * scale
                k = wide[half, at, width + h * HEAD : width + (h + 1) * HEAD]
                v = wide[half, at, 2 * width + h * HEAD : 2 * width + (h + 1) * HEAD]
                dc = dctx[at, h * HEAD : (h + 1) * HEAD]
                probs = prob[g % 2, h]
                full = probs.astype(F32)
                dprobs = mm(v, dc, NT)
                inner = jnp.sum(full * dprobs, axis=0, keepdims=True)
                dscores = (full * (dprobs - inner)).astype(BF)
                dv.append(mm(probs, dc, NN).astype(BF))
                dk.append(mm(dscores, q, NN).astype(BF))
                dq.append((mm(k, dscores, TN) * HEAD ** (-0.5)).astype(BF).T)
            joined = jnp.concatenate(dq + dk + dv, axis=1)
            dproj[half, at, 0 : 3 * width] = joined
            line = pl.ds(6 + z, 1)
            before = jnp.where(r == 0, 0.0, part[line, 0 : 3 * width])
            part[line, 0 : 3 * width] = before + jnp.sum(joined.astype(F32), axis=0, keepdims=True)
            events("attend", j, r)

        if fused:
            for k in range(4):
                pl.when(j == k)(lambda k=k: scatter.to_core(2 * k).wait_send())
            pl.when(j == 3)(lambda: scatter.small_stage(part, 0))

        pl.loop(0, 3)(lambda n: outer(j, 0, dproj.at[half], tile(n)))
        outer(j, 1, ctx.at[half], slice(None), slice(3 * width, D), width)
        emit(j, 0, z)
        events("project", j)

        @pl.when(j < 2)
        def _():
            wide_copy(qkv_in, j + 2).start()
            ctx_copy(j + 2).start()
            pull(j)

    if fused:
        scatter.small_stage(part, 1)
    pull(2)
    if fused:
        scatter.small_stage(part, 2)
    pull(3)
    input_copy = pltpu.make_async_copy(stream, input_out, end_sem.at[0])
    input_copy.start()
    if fused:
        events("last")
        scatter.small_stage(part, 3)
        grad_out[2] = scatter.total(2)
        grad_out[1] = scatter.total(1)
        small_out[...] = scatter.small_stage(part, 4)
        grad_out[0] = scatter.total(0)
        scatter.finish(part)
    else:
        small_out[...] = part[...]
    input_copy.wait()


def run_backward(vector_params, part, saved, rows, length):
    fused = lax.axis_size("dp") == 8 and lax.axis_size("mp") == 4
    hbm, vmem = pl.BlockSpec(memory_space=pl.ANY), pl.BlockSpec(memory_space=pltpu.VMEM)
    tokens = rows * length
    flat = (tokens, D)
    width = D // 4
    block = (4, 2, SLICE, D)
    shape = jax.ShapeDtypeStruct
    dma = pltpu.SemaphoreType.DMA
    whole_grad = shape((3, SLICE, D), F32) if fused else shape((3, 4) + block, BF)
    saved = [saved[0].reshape(3, 4, D, D)] + list(saved[1:])
    grads, sums, input_grad = pl.pallas_call(
        functools.partial(backward_kernel, fused, rows, length),
        out_shape=(whole_grad, shape((SMALL, D), F32), shape(flat, F32)),
        in_specs=[vmem] * 2 + [hbm] * 10,
        out_specs=(vmem if fused else hbm, vmem, hbm),
        scratch_shapes=([pltpu.VMEM(s, t) for s, t in Scatter.buffers] + [dma(s) for s in Scatter.sems] if fused else [])
        + [
            pltpu.VMEM((8,) + block, BF),
            pltpu.VMEM((4, D, D), BF),
            pltpu.VMEM((2,) + flat, BF),
            pltpu.VMEM((2,) + flat, BF),
            pltpu.VMEM(flat, BF),
            pltpu.VMEM(flat, F32),
            pltpu.VMEM(flat, F32),
            pltpu.VMEM((tokens, 128), F32),
            pltpu.VMEM(flat, BF),
            pltpu.VMEM((2, D, tokens), BF),
            pltpu.VMEM((2, D // HEAD // 4, length, length), BF),
            pltpu.VMEM((2, tokens, width), BF),
            pltpu.VMEM((tokens, width), BF),
            pltpu.VMEM((SMALL, D), F32),
            pltpu.VMEM((VECTORS, D), F32),
            dma((4,)),
            dma((2,)),
            dma((2,)),
            dma((2,)),
            dma((2,)),
            dma((2,)),
            dma((4,)),
        ],
        compiler_params=pltpu.CompilerParams(
            collective_id=1 if fused else None, has_side_effects=True, vmem_limit_bytes=VMEM_MOST
        ),
        name="backward",
    )(vector_params, part, *saved)
    if not fused:
        parts = lax.axis_size("dp")
        grads = lax.psum_scatter(grads.reshape(3, 4, D, D), "dp", scatter_dimension=2, tiled=True)
        grads = lax.psum_scatter(grads, "mp", scatter_dimension=1, tiled=True)
        grads = grads.reshape(3, D // parts, D).astype(F32)
        sums = lax.psum(sums, ("dp", "mp"))
    return input_grad, grads, sums


RATES = (D ** (-0.5), 0.5, (D // 16) ** (-0.5), D ** (-0.5), 0.5, FF ** (-0.5), 0.3)


def update_kernel(reduced, sums, result_in, input_in, *refs):
    state, outs, result_out, input_out, result, input_grad, sems = refs[:21], refs[21:49], *refs[49:]
    moves = [
        (pltpu.make_async_copy(input_in, input_grad, sems.at[0]), pltpu.make_async_copy(input_grad, input_out, sems.at[1])),
        (pltpu.make_async_copy(result_in, result, sems.at[2]), pltpu.make_async_copy(result, result_out, sems.at[3])),
    ]
    for load, _ in moves:
        load.start()
    dp, mp = lax.axis_index("dp"), lax.axis_index("mp")
    groups = lax.axis_size("mp")
    width = D // groups
    own = width // HEAD

    def update(i, gradient, at=Ellipsis):
        new = adam_update(*(state[3 * i + j][at] for j in range(3)), gradient, RATES[i])
        for j in range(4):
            outs[4 * i + j][at] = new[j]

    update(3, reduced[1])
    for load, store in moves:
        load.wait()
        store.start()
    mixing = reduced[0]
    for j in range(3):
        update(0, mixing[:, j * width : (j + 1) * width], j)
    update(2, mixing[:, 3 * width :].T)
    update(5, reduced[2])

    def lanes(row, count, start):
        return pltpu.roll(sums[pl.ds(row, count), :], lax.rem(D - start, D), 1)

    piece = state[3].shape[2]
    moved = lanes(6 + mp, 1, dp * piece)
    for j in (0, 1):
        for h in range(own):
            at = 2 * j * width + h * HEAD
            update(1, moved[:, at : at + piece], (h, slice(j, j + 1)))
    piece = state[12].shape[0]
    moved = lanes(10 + mp, 1, dp * piece)
    blocks = [moved[:, b * HEAD : b * HEAD + piece] for b in range(D // HEAD)]
    update(4, jnp.concatenate(blocks, axis=0).T)
    piece = state[18].shape[1]
    update(6, lanes(0, 8, (dp * groups + mp) * piece)[0:6, 0:piece])
    for _, store in moves:
        store.wait()


AXES = ((0, 1, 2), (1, 0, 2), (0, 1), (0, 1), (1, 0), (1, 0), (0, 1))


def update_all(state, reduced, sums, result, input_grad):
    hbm, vmem = pl.BlockSpec(memory_space=pl.ANY), pl.BlockSpec(memory_space=pltpu.VMEM)
    state = [s.transpose(AXES[i // 3]) for i, s in enumerate(state)]
    shapes = []
    for i in range(7):
        shapes = shapes + [jax.ShapeDtypeStruct(state[3 * i].shape, t) for t in (F32, F32, F32, BF)]
    kept = [jax.ShapeDtypeStruct(a.shape, a.dtype) for a in (result, input_grad)]
    *new, result, input_grad = pl.pallas_call(
        update_kernel,
        out_shape=tuple(shapes + kept),
        in_specs=[vmem] * 2 + [hbm] * 2 + [vmem] * 21,
        out_specs=(vmem,) * 28 + (hbm,) * 2,
        scratch_shapes=[pltpu.VMEM(a.shape, a.dtype) for a in kept] + [pltpu.SemaphoreType.DMA((4,))],
        name="update",
    )(reduced, sums, result, input_grad, *state)
    return result, input_grad, tuple(s.transpose(AXES[i // 4]) for i, s in enumerate(new))


def per_device(
    activations,
    cotangent,
    segments,
    triple_weight,
    query_value_bias,
    output_weight,
    expand_weight,
    expand_bias,
    shrink_weight,
    vector_params,
    *state,
):
    rows, length, _ = activations.shape
    weights = (triple_weight, output_weight, expand_weight, shrink_weight)
    *saved, result, part = run_forward(
        activations, cotangent, segments, vector_params, weights, (query_value_bias, expand_bias)
    )
    input_grad, reduced, sums = run_backward(vector_params, part, saved, rows, length)
    result, input_grad, new = update_all(state, reduced, sums, result, input_grad)
    return (result.reshape(activations.shape), input_grad.reshape(activations.shape)) + new


STATE_SPECS = (
    P(None, "dp", "mp"),
    P(None, "mp", "dp"),
    P("mp", "dp"),
    P("dp", "mp"),
    P("mp", "dp"),
    P("mp", "dp"),
    P(None, ("dp", "mp")),
)


def solution(mesh):
    rows = P(("dp", "mp"), None, None)
    placed = (
        rows,
        rows,
        P("dp", None),
        P(None, None, "mp"),
        P(None, "mp", None),
        P("mp", None),
        P(None, "mp"),
        P("mp", None),
        P("mp", None),
        P(),
    )
    for spec in STATE_SPECS:
        placed = placed + (spec,) * 3
    out_specs = (rows, rows)
    for spec in STATE_SPECS:
        out_specs = out_specs + (spec,) * 4
    return jax.shard_map(per_device, mesh=mesh, in_specs=placed, out_specs=out_specs, check_vma=False)
```

```python
import functools

import jax
import jax.numpy as jnp
from jax import lax
from jax.experimental import pallas as pl
from jax.experimental.pallas import tpu as pltpu
from jax.sharding import PartitionSpec as P

D = 768
HEAD = 64
FF = 3072
STEP = 10


NORM_EPS = 1e-05
BETA_ONE = 0.5
BETA_TWO = 0.6
ADAM_EPS = 1e-08
WEIGHT_DECAY = 0.01
MASKED = -1e30
SQRT_HALF = 0.7071067811865476
INV_ROOT_TAU = 0.3989422804014327


def norm_forward(summed, gain, shift):
    centre = summed - jnp.mean(summed, axis=-1, keepdims=True)
    scale = lax.rsqrt(jnp.mean(centre * centre, axis=-1, keepdims=True) + NORM_EPS)
    normed = centre * scale
    return (gain * normed + shift, normed, scale)


def norm_backward(gradient, gain, normed, scale):
    scaled = gradient * gain
    centred = scaled - jnp.mean(scaled, axis=-1, keepdims=True)
    return scale * (centred - normed * jnp.mean(scaled * normed, axis=-1, keepdims=True))


def adam_update(master, first, second, gradient, rate):
    first_new = BETA_ONE * first + (1.0 - BETA_ONE) * gradient
    second_new = BETA_TWO * second + (1.0 - BETA_TWO) * gradient * gradient
    corrected = first_new / (1.0 - BETA_ONE**STEP)
    spread = jnp.sqrt(second_new / (1.0 - BETA_TWO**STEP))
    master_new = master - rate * (corrected / (spread + ADAM_EPS) + WEIGHT_DECAY * master)
    return (master_new, first_new, second_new, master_new.astype(jnp.bfloat16))


MESH = pl.DeviceIdType.MESH
BF = jnp.bfloat16
F32 = jnp.float32
HALF = 48
SLICE = 96
SMALL = 16
VECTORS = 8


def place():
    p, z = lax.axis_index("dp"), lax.axis_index("mp")
    core, xy = p % 2, p // 2
    x, y = xy % 2, xy // 2
    return p, z, core, xy, p + 1 - 2 * core, p + 2 - 4 * x, p + 4 - 8 * y, xy + 1 - 2 * x, xy + 2 - 4 * y


def remote(src, dst, send_sem, recv_sem, p, z):
    return pltpu.make_async_remote_copy(
        src_ref=src, dst_ref=dst, send_sem=send_sem, recv_sem=recv_sem, device_id=(p, z), device_id_type=MESH
    )


def greet(p, z, pc, px, py):
    barrier = pltpu.get_barrier_semaphore()
    for peer in ((pc, z), (px, z), (py, z), (p, (z + 1) % 4), (p, (z + 2) % 4), (p, (z + 3) % 4)):
        pl.semaphore_signal(barrier, inc=1, device_id=peer, device_id_type=MESH)
    pl.semaphore_wait(barrier, 6)


def crossed(z, d):
    return (z // 2 + d // 2) % 2 * 2 + (z % 2 + d % 2) % 2


class Gather:
    steps = [(1, 1), (0, 1), (0, 2), (0, 3), (2, 1), (1, 2), (2, 2), (1, 3), (2, 3)]
    sems = [(3,)] + [(3, 3)] * 12 + [(3,)] * 2

    def __init__(self, mats, whole, bias, biases, sems):
        self.mats, self.whole, self.bias, self.biases = mats, whole, bias, biases
        (self.ls, self.zs, self.zr, self.xs, self.xr, self.ys, self.yr, self.as_, self.ar, self.bs, self.br, self.cs,
         self.cr, self.ss, self.sr) = sems
        self.where = place()

    def local(self, m):
        z = self.where[1]
        return pltpu.make_async_copy(self.mats[m - 1], self.whole.at[m, z], self.ls.at[m])

    def small(self, d):
        p, z = self.where[:2]
        return remote(self.bias, self.biases.at[z], self.ss.at[d - 1], self.sr.at[d - 1], p, crossed(z, d))

    def along_z(self, m, d):
        p, z, core, xy = self.where[:4]
        own = self.whole.at[m, z] if m == 0 else self.mats[m - 1]
        return remote(own.at[xy, core], self.whole.at[m, z, xy, core], self.zs.at[m, d - 1],
                      self.zr.at[m, d - 1], p, crossed(z, d))

    def plane(self, m, d, block, rows, send_sem, recv_sem, peer):
        z = self.where[1]
        part = self.whole.at[m, crossed(z, d), block, self.where[2], rows]
        return remote(part, part, send_sem.at[m, d - 1], recv_sem.at[m, d - 1], peer, z)

    def to_x(self, m, d):
        return self.plane(m, d, self.where[3], slice(None), self.xs, self.xr, self.where[5])

    def to_y(self, m, d):
        return self.plane(m, d, self.where[3], slice(None), self.ys, self.yr, self.where[6])

    def on_to_y(self, m, d):
        return self.plane(m, d, self.where[7], pl.ds(0, HALF), self.as_, self.ar, self.where[6])

    def on_to_x(self, m, d):
        return self.plane(m, d, self.where[8], pl.ds(HALF, HALF), self.bs, self.br, self.where[5])

    def to_core(self, m, d):
        z = self.where[1]
        part = self.whole.at[m, crossed(z, d), :, self.where[2]]
        return remote(part, part, self.cs.at[m, d - 1], self.cr.at[m, d - 1], self.where[4], z)

    def begin(self):
        p, z, _, _, pc, px, py = self.where[:7]
        greet(p, z, pc, px, py)
        self.along_z(1, 1).start()

    def begin_first(self):
        for d in (1, 2, 3):
            self.along_z(0, d).start()
            self.small(d).start()

    def run(self, kind, i):
        m, d = self.steps[i]
        if kind == 0:
            self.along_z(m, d).wait_recv()
            if m == 0:
                self.small(d).wait_recv()
            self.to_x(m, d).start()
            self.to_y(m, d).start()
            if m < 2 and (m, d) != (0, 1):
                self.along_z(m + 1, d).start()
        elif kind == 1:
            self.to_x(m, d).wait_recv()
            self.to_y(m, d).wait_recv()
            self.on_to_y(m, d).start()
            self.on_to_x(m, d).start()
        elif kind == 2:
            self.on_to_y(m, d).wait_recv()
            self.on_to_x(m, d).wait_recv()
            self.to_core(m, d).start()
        else:
            self.to_core(m, d).wait_recv()

    def finish(self):
        for d in (1, 2, 3):
            self.small(d).wait_send()
        for m, d in self.steps:
            for copy in (self.along_z, self.to_x, self.to_y, self.on_to_y, self.on_to_x, self.to_core):
                copy(m, d).wait_send()


class Scatter:
    steps = [(m, k) for k in (0, 3, 2, 1) for m in (2, 1)] + [(0, k) for k in (0, 3, 2, 1)]
    slots = [k + 4 * j for k in range(4) for j in (0, 1)] + list(range(4))
    buffers = [((12, 4, SLICE, D), BF)] + [((12, 2, HALF, D), BF)] * 2 + [((12, HALF, D), BF)] * 2 + [
        ((3, 3, SLICE, D), BF), ((3, 4, SLICE, D), BF), ((6, SMALL, D), F32), ((3, SMALL, D), F32)]
    sems = [(12,)] * 2 + [(12, 2)] * 4 + [(12,)] * 4 + [(3, 3)] * 2 + [(6,)] * 2

    def __init__(self, grads, buffers, sems):
        self.grads = grads
        self.sum, self.rx, self.ry, self.ra, self.rb, self.rz, self.plane, self.rv, self.sv = buffers
        (self.cs, self.cr, self.xs, self.xr, self.ys, self.yr, self.as_, self.ar, self.bs, self.br, self.zs, self.zr,
         self.ss, self.sr) = sems
        self.where = place()

    def to_core(self, i):
        _, z, core, _, pc = self.where[:5]
        return remote(self.grads.at[self.slots[i], :, 1 - core], self.sum.at[i], self.cs.at[i], self.cr.at[i], pc, z)

    def to_x(self, i, t):
        q = (self.where[7], 3 - self.where[3])[t]
        return remote(self.sum.at[i, q, pl.ds(0, HALF)], self.rx.at[i, t], self.xs.at[i, t], self.xr.at[i, t],
                      self.where[5], self.where[1])

    def to_y(self, i, t):
        q = (self.where[8], 3 - self.where[3])[t]
        return remote(self.sum.at[i, q, pl.ds(HALF, HALF)], self.ry.at[i, t], self.ys.at[i, t], self.yr.at[i, t],
                      self.where[6], self.where[1])

    def on_to_y(self, i):
        return remote(self.sum.at[i, self.where[8], pl.ds(0, HALF)], self.ra.at[i], self.as_.at[i], self.ar.at[i],
                      self.where[6], self.where[1])

    def on_to_x(self, i):
        return remote(self.sum.at[i, self.where[7], pl.ds(HALF, HALF)], self.rb.at[i], self.bs.at[i], self.br.at[i],
                      self.where[5], self.where[1])

    def to_owner(self, m, k, d):
        p = self.where[0]
        return remote(self.plane.at[m, k], self.rz.at[m, d - 1], self.zs.at[m, d - 1], self.zr.at[m, d - 1], p, k)

    def along_z(self, m, d):
        return self.to_owner(m, (self.where[1] + d) % 4, d)

    def begin(self):
        p, z, _, _, pc, px, py = self.where[:7]
        greet(p, z, pc, px, py)

    def run(self, kind, j):
        core, xy, xyx, xyy = self.where[2], self.where[3], self.where[7], self.where[8]
        low, high = slice(0, HALF), slice(HALF, SLICE)
        if kind == 0:
            self.to_core(j).start()
        elif kind == 1:
            self.to_core(j).wait_recv()

            @pl.loop(0, 4)
            def _(q):
                mine = self.grads[self.slots[j], q, core].astype(F32)
                self.sum[j, q] = (self.sum[j, q].astype(F32) + mine).astype(BF)

            for t in (1, 0):
                self.to_x(j, t).start()
                self.to_y(j, t).start()
        elif kind == 2:
            for t in (0, 1):
                self.to_x(j, t).wait_recv()
                self.to_y(j, t).wait_recv()
            self.sum[j, xyy, low] = (self.sum[j, xyy, low].astype(F32) + self.rx[j, 1].astype(F32)).astype(BF)
            self.sum[j, xyx, high] = (self.sum[j, xyx, high].astype(F32) + self.ry[j, 1].astype(F32)).astype(BF)
            self.on_to_y(j).start()
            self.on_to_x(j).start()
        else:
            m, k = self.steps[j]
            self.on_to_y(j).wait_recv()
            self.on_to_x(j).wait_recv()
            self.plane[m, k, low] = (
                self.sum[j, xy, low].astype(F32) + self.rx[j, 0].astype(F32) + self.ra[j].astype(F32)
            ).astype(BF)
            self.plane[m, k, high] = (
                self.sum[j, xy, high].astype(F32) + self.ry[j, 0].astype(F32) + self.rb[j].astype(F32)
            ).astype(BF)
            z = self.where[1]
            pl.when(z != k)(lambda: self.to_owner(m, k, (k + 4 - z) % 4).start())

    def total(self, m):
        for d in (1, 2, 3):
            self.along_z(m, d).wait_recv()
        own = self.plane[m, self.where[1]].astype(F32)
        return own + self.rz[m, 0].astype(F32) + self.rz[m, 1].astype(F32) + self.rz[m, 2].astype(F32)

    def small_to(self, s, src, p, z):
        return remote(src, self.rv.at[s], self.ss.at[s], self.sr.at[s], p, z)

    def small_copy(self, part, c):
        p, z, _, _, pc, px, py = self.where[:7]
        if c == 0:
            return self.small_to(0, part, pc, z)
        if c == 1:
            return self.small_to(1, self.sv.at[0], px, z)
        if c == 2:
            return self.small_to(2, self.sv.at[1], py, z)
        return self.small_to(c, self.sv.at[2], p, (z + c - 2) % 4)

    def small_stage(self, part, i):
        if i == 0:
            self.small_copy(part, 0).start()
        elif i < 4:
            self.small_copy(part, i - 1).wait_recv()
            before = part[...] if i == 1 else self.sv[i - 2]
            self.sv[i - 1] = before + self.rv[i - 1]
            for c in (i,) if i < 3 else (3, 4, 5):
                self.small_copy(part, c).start()
        else:
            for c in (3, 4, 5):
                self.small_copy(part, c).wait_recv()
            return self.sv[2] + self.rv[3] + self.rv[4] + self.rv[5]

    def finish(self, part):
        for c in range(6):
            self.small_copy(part, c).wait_send()
        for i in range(len(self.steps)):
            if self.slots[i] not in self.slots[i + 1 :]:
                self.to_core(i).wait_send()
            self.on_to_y(i).wait_send()
            self.on_to_x(i).wait_send()
            for t in (0, 1):
                self.to_x(i, t).wait_send()
                self.to_y(i, t).wait_send()
        for m in range(3):
            for d in (1, 2, 3):
                self.along_z(m, d).wait_send()


def mm(a, b, dims):
    return lax.dot_general(a, b, (dims, ((), ())), preferred_element_type=jnp.float32)


def pack_weights(triple_weight, output_weight, expand_weight, shrink_weight):
    width = triple_weight.shape[2]
    mixing = jnp.concatenate([triple_weight.transpose(1, 0, 2).reshape(D, 3 * width), output_weight.T], axis=1)
    return mixing, expand_weight, shrink_weight


def pack_biases(query_value_bias, expand_bias):
    pair = query_value_bias.reshape(2, -1)
    none = jnp.zeros_like(pair[0])
    first = jnp.concatenate([pair[0], none, pair[1], none])
    return jnp.concatenate([first[None], expand_bias.reshape(1, -1), jnp.zeros((VECTORS - 2, D), BF)]).astype(F32)


TN = ((0,), (0,))
NT = ((1,), (1,))
NN = ((1,), (0,))
CHUNK = 384
STRIP = 128
VMEM_MOST = 60 << 20
EVENTS = {
    "block": {(1, 0): ((0, 2), (1, 0), (0, 4), (1, 1), (0, 3), (1, 2), (2, 0), (3, 0), (1, 4), (0, 5), (2, 1), (3, 1)), (2, 0): ((3, 2),), (3, 0): ((1, 7), (3, 3))},
    "project": {(1, 1): ((1, 3),), (2, 1): ((1, 5),), (3, 1): ((2, 5),)},
    "attend": {(0, 1): ((0, 0),), (1, 1): ((2, 2),), (1, 2): ((0, 7), (2, 4)), (2, 0): ((3, 4),), (2, 1): ((2, 3),), (2, 2): ((0, 6),), (3, 2): ((0, 8), (1, 6)), (3, 3): ((3, 5),)},
    "turn": {(0, 0): ((0, 1),)},
    "norm": {(0, 0): ((2, 7),)},
    "feed": {},
    "middle": {},
    "expand": {(0, 0): ((3, 7), (1, 8)), (0, 1): ((2, 6),), (1, 0): ((2, 8),), (1, 1): ((3, 6),), (2, 0): ((3, 8),)},
    "shrink": {},
}


def half(n, tokens):
    return pl.ds(pl.multiple_of(n * (tokens // 2), 32), tokens // 2)


def square(whole, m, z):
    return whole[m, z].reshape(D, D)


def strip(s):
    return pl.ds(pl.multiple_of(s * STRIP, STRIP), STRIP)


def forward_kernel(fused, rows, length, *refs):
    n_sem = len(Gather.sems) if fused else 0
    x_in, cot_in, seg_ref, vec_in = refs[:4]
    n_in = 10 if fused else 6
    ins = refs[4:n_in]
    outs = refs[n_in : n_in + 12]
    (whole_out, qkv_out, ctx_out, prob_out, act_out, slope_out, normed_out, rstd_out, ds_out, turned_out, result_out,
     part_out) = outs
    rest = refs[n_in + 12 :]
    gather_sems, rest = rest[:n_sem], rest[n_sem:]
    (whole, bias, biases, joint, vec, x, cot, qkv, ctx, prob, act, slope, mixed, normed, rstd, low, turned,
     result, part, in_sem, w_sem, qkv_sem, ctx_sem, prob_sem, act_sem, slope_sem, end_sem) = rest
    tokens = rows * length
    strips = tokens // STRIP
    heads = D // HEAD // 4
    width = heads * HEAD
    z_own = lax.axis_index("mp")
    x_copy = pltpu.make_async_copy(x_in, x, in_sem.at[0])
    cot_copy = pltpu.make_async_copy(cot_in, cot, in_sem.at[1])
    x_copy.start()
    if fused:
        triple_in, output_in, e_ref, s_ref, qv_ref, eb_ref = ins
        joint_copies = [
            pltpu.make_async_copy(triple_in.at[j], joint.at[pl.ds(j * width, width)], in_sem.at[2 + j]) for j in range(3)
        ] + [pltpu.make_async_copy(output_in, joint.at[pl.ds(3 * width, width)], in_sem.at[5])]
        for copy in joint_copies:
            copy.start()
        gather = Gather((e_ref, s_ref), whole, bias, biases, gather_sems)
        gather.begin()
        bias[...] = jnp.zeros_like(bias)
        for h in range(heads):
            for j in (0, 1):
                at = slice(2 * j * width + h * HEAD, 2 * j * width + (h + 1) * HEAD)
                bias[0:1, at] = qv_ref[h, j : j + 1, :].astype(F32)
        for b in range(D // HEAD):
            bias[1:2, b * HEAD : (b + 1) * HEAD] = eb_ref[b : b + 1, :].astype(F32)
        for copy in joint_copies:
            copy.wait()
        for j in (0, 1):
            columns = joint[:, j * CHUNK : (j + 1) * CHUNK].T
            whole[0, z_own, 2 * j : 2 * j + 2] = columns.reshape(2, 2, SLICE, D)
        gather.begin_first()
        gather.local(1).start()
        gather.local(2).start()
        own_bias = pltpu.make_async_copy(bias, biases.at[z_own], w_sem.at[0])
        own_bias.start()
        own_bias.wait()
    else:
        copy = pltpu.make_async_copy(ins[0], whole, w_sem.at[0])
        copy.start()
        small = pltpu.make_async_copy(ins[1], biases, w_sem.at[1])
        small.start()
        copy.wait()
        small.wait()
    cot_copy.start()
    vec[0:6, :] = vec_in[...].astype(F32)

    def block(i):
        return crossed(z_own, i)

    def turned_copy(slot):
        return pltpu.make_async_copy(turned.at[slot], turned_out.at[slot], end_sem.at[slot])

    def qkv_copy(i):
        return pltpu.make_async_copy(qkv.at[i % 2], qkv_out.at[block(i)], qkv_sem.at[i % 2])

    def ctx_copy(i):
        return pltpu.make_async_copy(ctx.at[i % 2], ctx_out.at[block(i)], ctx_sem.at[i % 2])

    def prob_copy(i, r):
        return pltpu.make_async_copy(prob.at[r], prob_out.at[block(i), r], prob_sem.at[r])

    def act_copy(i):
        return pltpu.make_async_copy(act.at[i % 2], act_out.at[block(i)], act_sem.at[i % 2])

    def slope_copy(i):
        return pltpu.make_async_copy(slope.at[i % 2], slope_out.at[block(i)], slope_sem.at[i % 2])

    def whole_copy(m):
        return pltpu.make_async_copy(whole.at[m], whole_out.at[m], w_sem.at[m])

    def events(place, i=0, n=0):
        for (a, b), due in EVENTS[place].items() if fused else ():

            @pl.when((i == a) & (n == b))
            def _(due=due):
                for kind, step in due:
                    gather.run(kind, step)

    x_copy.wait()

    @pl.loop(0, 4)
    def _(i):
        events("block", i)
        z = block(i)
        slot = i % 2

        @pl.when(i >= 2)
        def _():
            qkv_copy(i - 2).wait()
            ctx_copy(i - 2).wait()

        @pl.loop(0, 2)
        def _(n):
            at = half(n, tokens)
            qkv[slot, at, :] = (mm(x[at, :], square(whole, 0, z), NN) + biases[z, 0:1, :]).astype(BF)
            events("project", i, n)

        qkv_copy(i).start()

        @pl.loop(0, rows)
        def _(r):
            at = pl.ds(pl.multiple_of(r * length, 32), length)
            pl.when(i >= 1)(lambda: prob_copy(i - 1, r).wait())
            pair = seg_ref[pl.ds(z_own * rows + r, 1), :]
            number = lax.broadcasted_iota(jnp.int32, (8, length), 0)
            among = jnp.where(number == pair, 1.0, 0.0).astype(BF)
            mask = (mm(among, among, TN) - 1.0) * -MASKED

            def part_of(j, h):
                return qkv[slot, at, j * width + h * HEAD : j * width + (h + 1) * HEAD]

            scale = jnp.asarray(HEAD ** (-0.5), BF)
            scores = [mm(part_of(1, h), part_of(0, h) * scale, NT) + mask for h in range(heads)]
            probs = []
            for h in range(heads):
                weights = jnp.exp(scores[h] - jnp.max(scores[h], axis=0, keepdims=True))
                share = 1.0 / jnp.sum(weights, axis=0, keepdims=True)
                probs.append((weights * share).astype(BF))
            for h in range(heads):
                prob[r, h] = probs[h]
            done = [mm(part_of(2, h), probs[h], TN).astype(BF) for h in range(heads)]
            ctx[slot, at, :] = jnp.concatenate(done, axis=0).T
            prob_copy(i, r).start()
            events("attend", i, r)

        ctx_copy(i).start()

        @pl.when(i == 0)
        def _():
            @pl.loop(0, strips)
            def _(s):
                value = x[strip(s), :]
                mixed[strip(s), :] = value.astype(F32) + vec[2:3, :]
                turned[0, :, strip(s)] = value.T

            turned_copy(0).start()
            events("turn")

        @pl.loop(0, tokens // CHUNK)
        def _(c):
            at = pl.ds(pl.multiple_of(c * CHUNK, CHUNK), CHUNK)
            add = mm(ctx[slot, at, :], square(whole, 0, z)[:, 3 * width :], NT)
            mixed[at, :] = mixed[at, :] + add

    whole_copy(0).start()

    @pl.loop(0, strips)
    def _(s):
        at = strip(s)
        hidden, normal, scale = norm_forward(mixed[at, :], vec[0:1, :], vec[1:2, :])
        normed[at, :] = normal
        rstd[at, :] = jnp.broadcast_to(scale, (STRIP, 128))
        mixed[at, :] = hidden + vec[5:6, :]
        hidden = hidden.astype(BF)
        low[at, :] = hidden
        turned[1, :, at] = hidden.T

    events("norm")
    turned_copy(1).start()
    normed_copy = pltpu.make_async_copy(normed, normed_out, end_sem.at[3])
    normed_copy.start()
    rstd_copy = pltpu.make_async_copy(rstd, rstd_out, end_sem.at[4])
    rstd_copy.start()
    if fused:
        gather.local(1).wait()
        gather.local(2).wait()

    @pl.loop(0, 4)
    def _(i):
        events("feed", i)
        z = block(i)
        slot = i % 2

        @pl.when(i >= 2)
        def _():
            act_copy(i - 2).wait()
            slope_copy(i - 2).wait()

        @pl.loop(0, 2)
        def _(n):
            at = half(n, tokens)
            u = mm(low[at, :], square(whole, 1, z), NN) + biases[z, 1:2, :]
            cumulative = 0.5 + 0.5 * lax.erf(u * SQRT_HALF)
            act[slot, at, :] = (u * cumulative).astype(BF)
            slope[slot, at, :] = (cumulative + u * jnp.exp(-0.5 * u * u) * INV_ROOT_TAU).astype(BF)
            events("expand", i, n)

        act_copy(i).start()
        slope_copy(i).start()
        events("middle", i)

        @pl.loop(0, 2)
        def _(n):
            at = half(n, tokens)
            mixed[at, :] = mixed[at, :] + mm(act[slot, at, :], square(whole, 2, z), NN)
            events("shrink", i, n)

        @pl.when(i == 2)
        def _():
            whole_copy(1).start()
            whole_copy(2).start()

    normed_copy.wait()
    cot_copy.wait()
    part[...] = jnp.zeros_like(part)

    @pl.loop(0, strips)
    def _(s):
        at = strip(s)
        block_result, normal, scale = norm_forward(mixed[at, :], vec[3:4, :], vec[4:5, :])
        result[at, :] = block_result.astype(BF)
        back = cot[at, :].astype(F32)
        dsummed = norm_backward(back, vec[3:4, :], normal, scale)
        normed[at, :] = dsummed
        turned[2, :, at] = dsummed.astype(BF).T
        part[3:4, :] += jnp.sum(back * normal, axis=0, keepdims=True)
        part[4:5, :] += jnp.sum(back, axis=0, keepdims=True)
        part[5:6, :] += jnp.sum(dsummed, axis=0, keepdims=True)
        pltpu.make_async_copy(normed.at[at], ds_out.at[at], end_sem.at[5]).start()
        pltpu.make_async_copy(result.at[at], result_out.at[at], end_sem.at[6]).start()

    last = [
        turned_copy(2),
        pltpu.make_async_copy(part, part_out, end_sem.at[7]),
    ]
    for copy in last:
        copy.start()
    last = last + [
        pltpu.make_async_copy(normed, ds_out, end_sem.at[5]),
        pltpu.make_async_copy(result, result_out, end_sem.at[6]),
    ]
    for i in (2, 3):
        qkv_copy(i).wait()
        ctx_copy(i).wait()
        act_copy(i).wait()
        slope_copy(i).wait()
    for r in range(rows):
        prob_copy(3, r).wait()
    turned_copy(0).wait()
    turned_copy(1).wait()
    rstd_copy.wait()
    for m in range(3):
        whole_copy(m).wait()
    for copy in last:
        copy.wait()
    if fused:
        gather.finish()


def run_forward(x, cot, segments, vector_params, weights, biases):
    rows, length, _ = x.shape
    tokens = rows * length
    fused = lax.axis_size("dp") == 8 and lax.axis_size("mp") == 4
    hbm, vmem = pl.BlockSpec(memory_space=pl.ANY), pl.BlockSpec(memory_space=pltpu.VMEM)
    flat = (tokens, D)
    width = D // 4
    block = (4, 2, SLICE, D)
    dense = [x.reshape(flat), cot.reshape(flat), segments, vector_params]
    if fused:
        triple, output, expand, shrink = weights
        held = [triple.transpose(0, 2, 1), output, expand.reshape(block), shrink.reshape(block)]
        held = held + [biases[0].transpose(1, 0, 2), biases[1]]
        spaces = [hbm, hbm, hbm, hbm, vmem, vmem]
    else:
        mats = pack_weights(*weights)
        held = [jnp.stack([lax.all_gather(m, "mp", axis=0) for m in mats]).reshape((3, 4) + block)]
        held = held + [lax.all_gather(pack_biases(*biases), "mp", axis=0)]
        spaces = [hbm, hbm]
    probs = (rows, D // HEAD // 4, length, length)
    shape = jax.ShapeDtypeStruct
    dma = pltpu.SemaphoreType.DMA
    return pl.pallas_call(
        functools.partial(forward_kernel, fused, rows, length),
        out_shape=(
            shape((3, 4) + block, BF),
            shape((4,) + flat, BF),
            shape((4, tokens, width), BF),
            shape((4,) + probs, BF),
            shape((4,) + flat, BF),
            shape((4,) + flat, BF),
            shape(flat, F32),
            shape((tokens, 128), F32),
            shape(flat, F32),
            shape((3, D, tokens), BF),
            shape(flat, BF),
            shape((VECTORS, D), F32),
        ),
        in_specs=[hbm, hbm, vmem, vmem] + spaces,
        out_specs=(hbm,) * 12,
        scratch_shapes=([dma(s) for s in Gather.sems] if fused else [])
        + [
            pltpu.VMEM((3, 4) + block, BF),
            pltpu.VMEM((VECTORS, D), F32),
            pltpu.VMEM((4, VECTORS, D), F32),
            pltpu.VMEM((D, D), BF),
            pltpu.VMEM((VECTORS, D), F32),
            pltpu.VMEM(flat, BF),
            pltpu.VMEM(flat, BF),
            pltpu.VMEM((2,) + flat, BF),
            pltpu.VMEM((2, tokens, width), BF),
            pltpu.VMEM(probs, BF),
            pltpu.VMEM((2,) + flat, BF),
            pltpu.VMEM((2,) + flat, BF),
            pltpu.VMEM(flat, F32),
            pltpu.VMEM(flat, F32),
            pltpu.VMEM((tokens, 128), F32),
            pltpu.VMEM(flat, BF),
            pltpu.VMEM((3, D, tokens), BF),
            pltpu.VMEM(flat, BF),
            pltpu.VMEM((VECTORS, D), F32),
            dma((6,)),
            dma((3,)),
            dma((2,)),
            dma((2,)),
            dma((rows,)),
            dma((2,)),
            dma((2,)),
            dma((8,)),
        ],
        compiler_params=pltpu.CompilerParams(
            collective_id=0 if fused else None, has_side_effects=True, vmem_limit_bytes=VMEM_MOST
        ),
        name="forward",
    )(*dense, *held)


BACK_EVENTS = {
    "shrink": {(0, 0): ((0, 0),), (1, 0): ((0, 2),), (2, 0): ((0, 4), (2, 1), (1, 3)), (3, 0): ((0, 6), (1, 5))},
    "slope": {(1, 0): ((1, 1),), (1, 1): ((2, 0),), (2, 0): ((3, 0),), (3, 0): ((2, 3),)},
    "expand": {(0, 0): ((0, 1), (1, 0)), (1, 0): ((0, 3), (1, 2)), (2, 0): ((0, 5), (1, 4), (2, 2)), (3, 0): ((0, 7), (1, 6), (2, 4))},
    "hidden": {(2, 0): ((3, 1),), (3, 1): ((3, 2),)},
    "norm": {(0, 0): ((1, 7), (2, 5))},
    "attend": {(0, 0): ((3, 3),), (0, 2): ((2, 6),), (0, 3): ((3, 4),), (1, 0): ((3, 5),), (1, 1): ((1, 8), (3, 6)), (1, 2): ((3, 7),), (2, 1): ((1, 9), (3, 8)), (3, 0): ((2, 9),), (3, 2): ((1, 10),), (3, 3): ((3, 9),)},
    "project": {(0, 0): ((0, 8),), (1, 0): ((0, 9),), (2, 0): ((0, 10),), (3, 0): ((0, 11),)},
    "pull": {(0, 0): ((2, 7),), (1, 0): ((2, 8),), (3, 0): ((2, 10),)},
    "last": {(0, 0): ((1, 11), (3, 10), (2, 11), (3, 11))},
}


def turn_block(j):
    return 3 * j % 4


def backward_kernel(fused, rows, length, *refs):
    n_sem = len(Scatter.sems) if fused else 0
    n_buf = len(Scatter.buffers) if fused else 0
    (vec_in, part_in, whole, qkv_in, ctx_in, prob_in, act_in, slope_in, normed_in, rstd_in, ds_in, turned_in) = refs[:12]
    grad_out, small_out, input_out = refs[12:15]
    rest = refs[15:]
    buffers, sems, rest = rest[:n_buf], rest[n_buf : n_buf + n_sem], rest[n_buf + n_sem :]
    (grads, weights, wide, tall, dexp, stream, normed, rstd, low, turned, prob, ctx, dctx, part, vec,
     w_sem, wide_sem, tall_sem, prob_sem, ctx_sem, turned_sem, end_sem) = rest
    tokens = rows * length
    strips = tokens // STRIP
    heads = D // HEAD // 4
    width = heads * HEAD

    def weight_copy(m, j, slot):
        return pltpu.make_async_copy(whole.at[m, turn_block(j)], weights.at[slot], w_sem.at[slot])

    def wide_copy(source, j):
        return pltpu.make_async_copy(source.at[turn_block(j)], wide.at[j % 2], wide_sem.at[j % 2])

    def tall_copy(j):
        return pltpu.make_async_copy(slope_in.at[turn_block(j)], tall.at[j % 2], tall_sem.at[j % 2])

    def turned_copy(source, slot):
        return pltpu.make_async_copy(turned_in.at[source], turned.at[slot], turned_sem.at[slot])

    def prob_copy(g):
        return pltpu.make_async_copy(prob_in.at[turn_block(g // rows), g % rows], prob.at[g % 2], prob_sem.at[g % 2])

    def ctx_copy(j):
        return pltpu.make_async_copy(ctx_in.at[turn_block(j)], ctx.at[j % 2], ctx_sem.at[j % 2])

    stream_copy = pltpu.make_async_copy(ds_in, stream, end_sem.at[0])
    normed_copy = pltpu.make_async_copy(normed_in, normed, end_sem.at[1])
    rstd_copy = pltpu.make_async_copy(rstd_in, rstd, end_sem.at[2])
    turned_copy(2, 0).start()
    wide_copy(act_in, 0).start()
    stream_copy.start()
    weight_copy(2, 0, 0).start()
    tall_copy(0).start()
    turned_copy(1, 1).start()
    weight_copy(1, 0, 1).start()
    wide_copy(act_in, 1).start()
    tall_copy(1).start()
    weight_copy(2, 1, 2).start()
    weight_copy(1, 1, 3).start()
    normed_copy.start()
    rstd_copy.start()
    if fused:
        scatter = Scatter(grads, buffers, sems)
        scatter.begin()

    def events(place, j=0, n=0):
        for (a, c), due in BACK_EVENTS[place].items() if fused else ():

            @pl.when((j == a) & (n == c))
            def _(due=due):
                for kind, step in due:
                    scatter.run(kind, step)

    vec[0:6, :] = vec_in[...].astype(F32)
    part[...] = jnp.zeros_like(part)
    part[0:VECTORS, :] = part_in[...]

    def outer(slot, turned_slot, right, offset=0):
        product = mm(turned[turned_slot], right, NN).astype(BF)
        count = product.shape[1]
        grads[slot, :, :, :, offset : offset + count] = product.reshape(4, 2, SLICE, count)

    def emit(slot, m, z):
        if not fused:
            copy = pltpu.make_async_copy(grads.at[slot], grad_out.at[m, z], end_sem.at[3])
            copy.start()
            copy.wait()

    turned_copy(2, 0).wait()

    @pl.loop(0, 4)
    def _(j):
        parity = j % 2
        slot = 2 * parity
        z = turn_block(j)
        wide_copy(act_in, j).wait()

        outer(j, 0, wide[parity])
        events("shrink", j)
        emit(j, 2, z)

        @pl.when(j == 0)
        def _():
            stream_copy.wait()

            @pl.loop(0, strips)
            def _(s):
                low[strip(s), :] = stream[strip(s), :].astype(BF)

            turned_copy(1, 1).wait()

        weight_copy(2, j, slot).wait()
        tall_copy(j).wait()

        @pl.loop(0, 2)
        def _(n):
            at = half(n, tokens)
            dactive = mm(low[at, :], weights[slot], NT)
            value = (dactive * tall[parity, at, :].astype(F32)).astype(BF)
            dexp[at, :] = value
            line = pl.ds(10 + z, 1)
            part[line, :] = part[line, :] + jnp.sum(value.astype(F32), axis=0, keepdims=True)
            events("slope", j, n)

        outer(4 + j, 1, dexp[...])
        events("expand", j)
        emit(4 + j, 1, z)
        weight_copy(1, j, slot + 1).wait()

        @pl.loop(0, 2)
        def _(n):
            at = half(n, tokens)
            stream[at, :] = stream[at, :] + mm(dexp[at, :], weights[slot + 1], NT)
            events("hidden", j, n)

        @pl.when(j < 2)
        def _():
            wide_copy(act_in, j + 2).start()
            tall_copy(j + 2).start()
            weight_copy(2, j + 2, slot).start()
            weight_copy(1, j + 2, slot + 1).start()

        @pl.when(j == 2)
        def _():
            wide_copy(qkv_in, 0).start()
            weight_copy(0, 0, 0).start()
            weight_copy(0, 1, 1).start()
            ctx_copy(0).start()
            ctx_copy(1).start()
            prob_copy(0).start()

        @pl.when(j == 3)
        def _():
            wide_copy(qkv_in, 1).start()
            weight_copy(0, 2, 2).start()
            weight_copy(0, 3, 3).start()
            turned_copy(0, 0).start()

    normed_copy.wait()
    rstd_copy.wait()

    @pl.loop(0, strips)
    def _(s):
        at = strip(s)
        dhidden, normal = stream[at, :], normed[at, :]
        dmixed = norm_backward(dhidden, vec[0:1, :], normal, rstd[at, 0:1])
        part[0:1, :] += jnp.sum(dhidden * normal, axis=0, keepdims=True)
        part[1:2, :] += jnp.sum(dhidden, axis=0, keepdims=True)
        part[2:3, :] += jnp.sum(dmixed, axis=0, keepdims=True)
        stream[at, :] = dmixed
        dmixed = dmixed.astype(BF)
        low[at, :] = dmixed
        turned[1, :, at] = dmixed.T

    events("norm")
    turned_copy(0, 0).wait()
    dproj = tall

    def pull(j):
        @pl.loop(0, 2)
        def _(n):
            at = half(n, tokens)
            stream[at, :] = stream[at, :] + mm(dproj[j % 2, at, 0 : 3 * width], weights[j, :, 0 : 3 * width], NT)
            events("pull", j, n)

    @pl.loop(0, 4)
    def _(j):
        parity = j % 2
        z = turn_block(j)
        weight_copy(0, j, j).wait()
        wide_copy(qkv_in, j).wait()
        ctx_copy(j).wait()
        dctx[...] = mm(low[...], weights[j, :, 3 * width :], NN).astype(BF)

        @pl.loop(0, rows)
        def _(r):
            at = pl.ds(pl.multiple_of(r * length, 32), length)
            g = j * rows + r
            prob_copy(g).wait()
            pl.when(g + 1 < 4 * rows)(lambda: prob_copy(g + 1).start())
            scale = jnp.asarray(HEAD ** (-0.5), BF)

            def part_of(i, h):
                return wide[parity, at, i * width + h * HEAD : i * width + (h + 1) * HEAD]

            def dc(h):
                return dctx[at, h * HEAD : (h + 1) * HEAD]

            dprobs = [mm(part_of(2, h), dc(h), NT) for h in range(heads)]
            dscores = []
            for h in range(heads):
                full = prob[g % 2, h].astype(F32)
                inner = jnp.sum(full * dprobs[h], axis=0, keepdims=True)
                dscores.append((full * (dprobs[h] - inner)).astype(BF))
            dv = [mm(prob[g % 2, h], dc(h), NN).astype(BF) for h in range(heads)]
            dk = [mm(dscores[h], part_of(0, h) * scale, NN).astype(BF) for h in range(heads)]
            dq = [(mm(part_of(1, h), dscores[h], TN) * HEAD ** (-0.5)).astype(BF) for h in range(heads)]
            dq = [jnp.concatenate(dq, axis=0).T]
            joined = jnp.concatenate(dq + dk + dv, axis=1)
            dproj[parity, at, 0 : 3 * width] = joined
            line = pl.ds(6 + z, 1)
            before = jnp.where(r == 0, 0.0, part[line, 0 : 3 * width])
            part[line, 0 : 3 * width] = before + jnp.sum(joined.astype(F32), axis=0, keepdims=True)
            events("attend", j, r)

        if fused:
            for k in range(4):
                pl.when(j == k)(lambda k=k: scatter.to_core(2 * k).wait_send())
            pl.when(j == 3)(lambda: scatter.small_stage(part, 0))

        outer(j, 0, dproj[parity, :, 0 : 3 * width])
        outer(j, 1, ctx[parity], 3 * width)
        emit(j, 0, z)
        events("project", j)

        @pl.when(j < 2)
        def _():
            wide_copy(qkv_in, j + 2).start()
            ctx_copy(j + 2).start()
            pull(j)

    if fused:
        scatter.small_stage(part, 1)
    pull(2)
    if fused:
        scatter.small_stage(part, 2)
    pull(3)
    input_copy = pltpu.make_async_copy(stream, input_out, end_sem.at[0])
    input_copy.start()
    if fused:
        events("last")
        scatter.small_stage(part, 3)
        grad_out[2] = scatter.total(2)
        grad_out[1] = scatter.total(1)
        small_out[...] = scatter.small_stage(part, 4)
        grad_out[0] = scatter.total(0)
        scatter.finish(part)
    else:
        small_out[...] = part[...]
    input_copy.wait()


def run_backward(vector_params, part, saved, rows, length):
    fused = lax.axis_size("dp") == 8 and lax.axis_size("mp") == 4
    hbm, vmem = pl.BlockSpec(memory_space=pl.ANY), pl.BlockSpec(memory_space=pltpu.VMEM)
    tokens = rows * length
    flat = (tokens, D)
    width = D // 4
    block = (4, 2, SLICE, D)
    shape = jax.ShapeDtypeStruct
    dma = pltpu.SemaphoreType.DMA
    whole_grad = shape((3, SLICE, D), F32) if fused else shape((3, 4) + block, BF)
    saved = [saved[0].reshape(3, 4, D, D)] + list(saved[1:])
    grads, sums, input_grad = pl.pallas_call(
        functools.partial(backward_kernel, fused, rows, length),
        out_shape=(whole_grad, shape((SMALL, D), F32), shape(flat, F32)),
        in_specs=[vmem] * 2 + [hbm] * 10,
        out_specs=(vmem if fused else hbm, vmem, hbm),
        scratch_shapes=([pltpu.VMEM(s, t) for s, t in Scatter.buffers] + [dma(s) for s in Scatter.sems] if fused else [])
        + [
            pltpu.VMEM((8,) + block, BF),
            pltpu.VMEM((4, D, D), BF),
            pltpu.VMEM((2,) + flat, BF),
            pltpu.VMEM((2,) + flat, BF),
            pltpu.VMEM(flat, BF),
            pltpu.VMEM(flat, F32),
            pltpu.VMEM(flat, F32),
            pltpu.VMEM((tokens, 128), F32),
            pltpu.VMEM(flat, BF),
            pltpu.VMEM((2, D, tokens), BF),
            pltpu.VMEM((2, D // HEAD // 4, length, length), BF),
            pltpu.VMEM((2, tokens, width), BF),
            pltpu.VMEM((tokens, width), BF),
            pltpu.VMEM((SMALL, D), F32),
            pltpu.VMEM((VECTORS, D), F32),
            dma((4,)),
            dma((2,)),
            dma((2,)),
            dma((2,)),
            dma((2,)),
            dma((2,)),
            dma((4,)),
        ],
        compiler_params=pltpu.CompilerParams(
            collective_id=1 if fused else None, has_side_effects=True, vmem_limit_bytes=VMEM_MOST
        ),
        name="backward",
    )(vector_params, part, *saved)
    if not fused:
        parts = lax.axis_size("dp")
        grads = lax.psum_scatter(grads.reshape(3, 4, D, D), "dp", scatter_dimension=2, tiled=True)
        grads = lax.psum_scatter(grads, "mp", scatter_dimension=1, tiled=True)
        grads = grads.reshape(3, D // parts, D).astype(F32)
        sums = lax.psum(sums, ("dp", "mp"))
    return input_grad, grads, sums


RATES = (D ** (-0.5), 0.5, (D // 16) ** (-0.5), D ** (-0.5), 0.5, FF ** (-0.5), 0.3)


def update_kernel(reduced, sums, result_in, input_in, *refs):
    state, outs, result_out, input_out, result, input_grad, sems = refs[:21], refs[21:49], *refs[49:]
    moves = [
        (pltpu.make_async_copy(input_in, input_grad, sems.at[0]), pltpu.make_async_copy(input_grad, input_out, sems.at[1])),
        (pltpu.make_async_copy(result_in, result, sems.at[2]), pltpu.make_async_copy(result, result_out, sems.at[3])),
    ]
    for load, _ in moves:
        load.start()
    dp, mp = lax.axis_index("dp"), lax.axis_index("mp")
    groups = lax.axis_size("mp")
    width = D // groups
    own = width // HEAD

    def update(i, gradient, at=Ellipsis):
        new = adam_update(*(state[3 * i + j][at] for j in range(3)), gradient, RATES[i])
        for j in range(4):
            outs[4 * i + j][at] = new[j]

    update(3, reduced[1])
    for load, store in moves:
        load.wait()
        store.start()
    mixing = reduced[0]
    for j in range(3):
        update(0, mixing[:, j * width : (j + 1) * width], j)
    update(2, mixing[:, 3 * width :].T)
    update(5, reduced[2])

    def lanes(row, count, start):
        return pltpu.roll(sums[pl.ds(row, count), :], lax.rem(D - start, D), 1)

    piece = state[3].shape[2]
    moved = lanes(6 + mp, 1, dp * piece)
    for j in (0, 1):
        for h in range(own):
            at = 2 * j * width + h * HEAD
            update(1, moved[:, at : at + piece], (h, slice(j, j + 1)))
    piece = state[12].shape[0]
    moved = lanes(10 + mp, 1, dp * piece)
    blocks = [moved[:, b * HEAD : b * HEAD + piece] for b in range(D // HEAD)]
    update(4, jnp.concatenate(blocks, axis=0).T)
    piece = state[18].shape[1]
    update(6, lanes(0, 8, (dp * groups + mp) * piece)[0:6, 0:piece])
    for _, store in moves:
        store.wait()


AXES = ((0, 1, 2), (1, 0, 2), (0, 1), (0, 1), (1, 0), (1, 0), (0, 1))


def update_all(state, reduced, sums, result, input_grad):
    hbm, vmem = pl.BlockSpec(memory_space=pl.ANY), pl.BlockSpec(memory_space=pltpu.VMEM)
    state = [s.transpose(AXES[i // 3]) for i, s in enumerate(state)]
    shapes = []
    for i in range(7):
        shapes = shapes + [jax.ShapeDtypeStruct(state[3 * i].shape, t) for t in (F32, F32, F32, BF)]
    kept = [jax.ShapeDtypeStruct(a.shape, a.dtype) for a in (result, input_grad)]
    *new, result, input_grad = pl.pallas_call(
        update_kernel,
        out_shape=tuple(shapes + kept),
        in_specs=[vmem] * 2 + [hbm] * 2 + [vmem] * 21,
        out_specs=(vmem,) * 28 + (hbm,) * 2,
        scratch_shapes=[pltpu.VMEM(a.shape, a.dtype) for a in kept] + [pltpu.SemaphoreType.DMA((4,))],
        name="update",
    )(reduced, sums, result, input_grad, *state)
    return result, input_grad, tuple(s.transpose(AXES[i // 4]) for i, s in enumerate(new))


def per_device(
    activations,
    cotangent,
    segments,
    triple_weight,
    query_value_bias,
    output_weight,
    expand_weight,
    expand_bias,
    shrink_weight,
    vector_params,
    *state,
):
    rows, length, _ = activations.shape
    weights = (triple_weight, output_weight, expand_weight, shrink_weight)
    *saved, result, part = run_forward(
        activations, cotangent, segments, vector_params, weights, (query_value_bias, expand_bias)
    )
    input_grad, reduced, sums = run_backward(vector_params, part, saved, rows, length)
    result, input_grad, new = update_all(state, reduced, sums, result, input_grad)
    return (result.reshape(activations.shape), input_grad.reshape(activations.shape)) + new


STATE_SPECS = (
    P(None, "dp", "mp"),
    P(None, "mp", "dp"),
    P("mp", "dp"),
    P("dp", "mp"),
    P("mp", "dp"),
    P("mp", "dp"),
    P(None, ("dp", "mp")),
)


def solution(mesh):
    rows = P(("dp", "mp"), None, None)
    placed = (
        rows,
        rows,
        P("dp", None),
        P(None, None, "mp"),
        P(None, "mp", None),
        P("mp", None),
        P(None, "mp"),
        P("mp", None),
        P("mp", None),
        P(),
    )
    for spec in STATE_SPECS:
        placed = placed + (spec,) * 3
    out_specs = (rows, rows)
    for spec in STATE_SPECS:
        out_specs = out_specs + (spec,) * 4
    return jax.shard_map(per_device, mesh=mesh, in_specs=placed, out_specs=out_specs, check_vma=False)
```

```python
import functools

import jax
import jax.numpy as jnp
from jax import lax
from jax.experimental import pallas as pl
from jax.experimental.pallas import tpu as pltpu
from jax.sharding import PartitionSpec as P

D = 768
HEAD = 64
FF = 3072
STEP = 10


NORM_EPS = 1e-05
BETA_ONE = 0.5
BETA_TWO = 0.6
ADAM_EPS = 1e-08
WEIGHT_DECAY = 0.01
MASKED = -1e30
SQRT_HALF = 0.7071067811865476
INV_ROOT_TAU = 0.3989422804014327


def norm_forward(summed, gain, shift):
    centre = summed - jnp.mean(summed, axis=-1, keepdims=True)
    scale = lax.rsqrt(jnp.mean(centre * centre, axis=-1, keepdims=True) + NORM_EPS)
    normed = centre * scale
    return (gain * normed + shift, normed, scale)


def norm_backward(gradient, gain, normed, scale):
    scaled = gradient * gain
    centred = scaled - jnp.mean(scaled, axis=-1, keepdims=True)
    return scale * (centred - normed * jnp.mean(scaled * normed, axis=-1, keepdims=True))


def adam_update(master, first, second, gradient, rate):
    first_new = BETA_ONE * first + (1.0 - BETA_ONE) * gradient
    second_new = BETA_TWO * second + (1.0 - BETA_TWO) * gradient * gradient
    corrected = first_new / (1.0 - BETA_ONE**STEP)
    spread = jnp.sqrt(second_new / (1.0 - BETA_TWO**STEP))
    master_new = master - rate * (corrected / (spread + ADAM_EPS) + WEIGHT_DECAY * master)
    return (master_new, first_new, second_new, master_new.astype(jnp.bfloat16))


MESH = pl.DeviceIdType.MESH
BF = jnp.bfloat16
F32 = jnp.float32
HALF = 48
SLICE = 96
SMALL = 16
VECTORS = 8


def place():
    p, z = lax.axis_index("dp"), lax.axis_index("mp")
    core, xy = p % 2, p // 2
    x, y = xy % 2, xy // 2
    return p, z, core, xy, p + 1 - 2 * core, p + 2 - 4 * x, p + 4 - 8 * y, xy + 1 - 2 * x, xy + 2 - 4 * y


def remote(src, dst, send_sem, recv_sem, p, z):
    return pltpu.make_async_remote_copy(
        src_ref=src, dst_ref=dst, send_sem=send_sem, recv_sem=recv_sem, device_id=(p, z), device_id_type=MESH
    )


def greet(p, z, pc, px, py):
    barrier = pltpu.get_barrier_semaphore()
    for peer in ((pc, z), (px, z), (py, z), (p, (z + 1) % 4), (p, (z + 2) % 4), (p, (z + 3) % 4)):
        pl.semaphore_signal(barrier, inc=1, device_id=peer, device_id_type=MESH)
    pl.semaphore_wait(barrier, 6)


def crossed(z, d):
    return (z // 2 + d // 2) % 2 * 2 + (z % 2 + d % 2) % 2


class Gather:
    steps = [(1, 1), (0, 1), (0, 2), (0, 3), (2, 1), (1, 2), (2, 2), (1, 3), (2, 3)]
    sems = [(3,)] + [(3, 3)] * 12 + [(3,)] * 2

    def __init__(self, mats, whole, bias, biases, sems):
        self.mats, self.whole, self.bias, self.biases = mats, whole, bias, biases
        (self.ls, self.zs, self.zr, self.xs, self.xr, self.ys, self.yr, self.as_, self.ar, self.bs, self.br, self.cs,
         self.cr, self.ss, self.sr) = sems
        self.where = place()

    def local(self, m):
        z = self.where[1]
        return pltpu.make_async_copy(self.mats[m - 1], self.whole.at[m, z], self.ls.at[m])

    def small(self, d):
        p, z = self.where[:2]
        return remote(self.bias, self.biases.at[z], self.ss.at[d - 1], self.sr.at[d - 1], p, crossed(z, d))

    def along_z(self, m, d):
        p, z, core, xy = self.where[:4]
        own = self.whole.at[m, z] if m == 0 else self.mats[m - 1]
        return remote(own.at[xy, core], self.whole.at[m, z, xy, core], self.zs.at[m, d - 1],
                      self.zr.at[m, d - 1], p, crossed(z, d))

    def plane(self, m, d, block, rows, send_sem, recv_sem, peer):
        z = self.where[1]
        part = self.whole.at[m, crossed(z, d), block, self.where[2], rows]
        return remote(part, part, send_sem.at[m, d - 1], recv_sem.at[m, d - 1], peer, z)

    def to_x(self, m, d):
        return self.plane(m, d, self.where[3], slice(None), self.xs, self.xr, self.where[5])

    def to_y(self, m, d):
        return self.plane(m, d, self.where[3], slice(None), self.ys, self.yr, self.where[6])

    def on_to_y(self, m, d):
        return self.plane(m, d, self.where[7], pl.ds(0, HALF), self.as_, self.ar, self.where[6])

    def on_to_x(self, m, d):
        return self.plane(m, d, self.where[8], pl.ds(HALF, HALF), self.bs, self.br, self.where[5])

    def to_core(self, m, d):
        z = self.where[1]
        part = self.whole.at[m, crossed(z, d), :, self.where[2]]
        return remote(part, part, self.cs.at[m, d - 1], self.cr.at[m, d - 1], self.where[4], z)

    def begin(self):
        p, z, _, _, pc, px, py = self.where[:7]
        greet(p, z, pc, px, py)
        self.along_z(1, 1).start()

    def begin_first(self):
        for d in (1, 2, 3):
            self.along_z(0, d).start()
            self.small(d).start()

    def run(self, kind, i):
        m, d = self.steps[i]
        if kind == 0:
            self.along_z(m, d).wait_recv()
            if m == 0:
                self.small(d).wait_recv()
            self.to_x(m, d).start()
            self.to_y(m, d).start()
            if m < 2 and (m, d) != (0, 1):
                self.along_z(m + 1, d).start()
        elif kind == 1:
            self.to_x(m, d).wait_recv()
            self.to_y(m, d).wait_recv()
            self.on_to_y(m, d).start()
            self.on_to_x(m, d).start()
        elif kind == 2:
            self.on_to_y(m, d).wait_recv()
            self.on_to_x(m, d).wait_recv()
            self.to_core(m, d).start()
        else:
            self.to_core(m, d).wait_recv()

    def finish(self):
        for d in (1, 2, 3):
            self.small(d).wait_send()
        for m, d in self.steps:
            for copy in (self.along_z, self.to_x, self.to_y, self.on_to_y, self.on_to_x, self.to_core):
                copy(m, d).wait_send()


class Scatter:
    steps = [(m, k) for k in (0, 3, 2, 1) for m in (2, 1)] + [(0, k) for k in (0, 3, 2, 1)]
    slots = [k + 4 * j for k in range(4) for j in (0, 1)] + list(range(4))
    buffers = [((12, 4, SLICE, D), BF)] + [((12, 2, HALF, D), BF)] * 2 + [((12, HALF, D), BF)] * 2 + [
        ((3, 3, SLICE, D), BF), ((3, 4, SLICE, D), BF), ((6, SMALL, D), F32), ((3, SMALL, D), F32)]
    sems = [(12,)] * 2 + [(12, 2)] * 4 + [(12,)] * 4 + [(3, 3)] * 2 + [(6,)] * 2

    def __init__(self, grads, buffers, sems):
        self.grads = grads
        self.sum, self.rx, self.ry, self.ra, self.rb, self.rz, self.plane, self.rv, self.sv = buffers
        (self.cs, self.cr, self.xs, self.xr, self.ys, self.yr, self.as_, self.ar, self.bs, self.br, self.zs, self.zr,
         self.ss, self.sr) = sems
        self.where = place()

    def to_core(self, i):
        _, z, core, _, pc = self.where[:5]
        return remote(self.grads.at[self.slots[i], :, 1 - core], self.sum.at[i], self.cs.at[i], self.cr.at[i], pc, z)

    def to_x(self, i, t):
        q = (self.where[7], 3 - self.where[3])[t]
        return remote(self.sum.at[i, q, pl.ds(0, HALF)], self.rx.at[i, t], self.xs.at[i, t], self.xr.at[i, t],
                      self.where[5], self.where[1])

    def to_y(self, i, t):
        q = (self.where[8], 3 - self.where[3])[t]
        return remote(self.sum.at[i, q, pl.ds(HALF, HALF)], self.ry.at[i, t], self.ys.at[i, t], self.yr.at[i, t],
                      self.where[6], self.where[1])

    def on_to_y(self, i):
        return remote(self.sum.at[i, self.where[8], pl.ds(0, HALF)], self.ra.at[i], self.as_.at[i], self.ar.at[i],
                      self.where[6], self.where[1])

    def on_to_x(self, i):
        return remote(self.sum.at[i, self.where[7], pl.ds(HALF, HALF)], self.rb.at[i], self.bs.at[i], self.br.at[i],
                      self.where[5], self.where[1])

    def to_owner(self, m, k, d):
        p = self.where[0]
        return remote(self.plane.at[m, k], self.rz.at[m, d - 1], self.zs.at[m, d - 1], self.zr.at[m, d - 1], p, k)

    def along_z(self, m, d):
        return self.to_owner(m, (self.where[1] + d) % 4, d)

    def begin(self):
        p, z, _, _, pc, px, py = self.where[:7]
        greet(p, z, pc, px, py)

    def run(self, kind, j):
        core, xy, xyx, xyy = self.where[2], self.where[3], self.where[7], self.where[8]
        low, high = slice(0, HALF), slice(HALF, SLICE)
        if kind == 0:
            self.to_core(j).start()
        elif kind == 1:
            self.to_core(j).wait_recv()

            @pl.loop(0, 4)
            def _(q):
                self.sum[j, q] = self.sum[j, q] + self.grads[self.slots[j], q, core]

            for t in (1, 0):
                self.to_x(j, t).start()
                self.to_y(j, t).start()
        elif kind == 2:
            for t in (0, 1):
                self.to_x(j, t).wait_recv()
                self.to_y(j, t).wait_recv()
            self.sum[j, xyy, low] = (self.sum[j, xyy, low].astype(F32) + self.rx[j, 1].astype(F32)).astype(BF)
            self.sum[j, xyx, high] = (self.sum[j, xyx, high].astype(F32) + self.ry[j, 1].astype(F32)).astype(BF)
            self.on_to_y(j).start()
            self.on_to_x(j).start()
        else:
            m, k = self.steps[j]
            self.on_to_y(j).wait_recv()
            self.on_to_x(j).wait_recv()
            self.plane[m, k, low] = (
                self.sum[j, xy, low].astype(F32) + self.rx[j, 0].astype(F32) + self.ra[j].astype(F32)
            ).astype(BF)
            self.plane[m, k, high] = (
                self.sum[j, xy, high].astype(F32) + self.ry[j, 0].astype(F32) + self.rb[j].astype(F32)
            ).astype(BF)
            z = self.where[1]
            pl.when(z != k)(lambda: self.to_owner(m, k, (k + 4 - z) % 4).start())

    def total(self, m):
        for d in (1, 2, 3):
            self.along_z(m, d).wait_recv()
        own = self.plane[m, self.where[1]].astype(F32)
        return own + self.rz[m, 0].astype(F32) + self.rz[m, 1].astype(F32) + self.rz[m, 2].astype(F32)

    def small_to(self, s, src, p, z):
        return remote(src, self.rv.at[s], self.ss.at[s], self.sr.at[s], p, z)

    def small_copy(self, part, c):
        p, z, _, _, pc, px, py = self.where[:7]
        if c == 0:
            return self.small_to(0, part, pc, z)
        if c == 1:
            return self.small_to(1, self.sv.at[0], px, z)
        if c == 2:
            return self.small_to(2, self.sv.at[1], py, z)
        return self.small_to(c, self.sv.at[2], p, (z + c - 2) % 4)

    def small_stage(self, part, i):
        if i == 0:
            self.small_copy(part, 0).start()
        elif i < 4:
            self.small_copy(part, i - 1).wait_recv()
            before = part[...] if i == 1 else self.sv[i - 2]
            self.sv[i - 1] = before + self.rv[i - 1]
            for c in (i,) if i < 3 else (3, 4, 5):
                self.small_copy(part, c).start()
        else:
            for c in (3, 4, 5):
                self.small_copy(part, c).wait_recv()
            return self.sv[2] + self.rv[3] + self.rv[4] + self.rv[5]

    def finish(self, part):
        for c in range(6):
            self.small_copy(part, c).wait_send()
        for i in range(len(self.steps)):
            if self.slots[i] not in self.slots[i + 1 :]:
                self.to_core(i).wait_send()
            self.on_to_y(i).wait_send()
            self.on_to_x(i).wait_send()
            for t in (0, 1):
                self.to_x(i, t).wait_send()
                self.to_y(i, t).wait_send()
        for m in range(3):
            for d in (1, 2, 3):
                self.along_z(m, d).wait_send()


def mm(a, b, dims):
    return lax.dot_general(a, b, (dims, ((), ())), preferred_element_type=jnp.float32)


def pack_weights(triple_weight, output_weight, expand_weight, shrink_weight):
    width = triple_weight.shape[2]
    mixing = jnp.concatenate([triple_weight.transpose(1, 0, 2).reshape(D, 3 * width), output_weight.T], axis=1)
    return mixing, expand_weight, shrink_weight


def pack_biases(query_value_bias, expand_bias):
    pair = query_value_bias.reshape(2, -1)
    none = jnp.zeros_like(pair[0])
    first = jnp.concatenate([pair[0], none, pair[1], none])
    return jnp.concatenate([first[None], expand_bias.reshape(1, -1), jnp.zeros((VECTORS - 2, D), BF)]).astype(F32)


TN = ((0,), (0,))
NT = ((1,), (1,))
NN = ((1,), (0,))
CHUNK = 384
STRIP = 128
VMEM_MOST = 60 << 20
EVENTS = {
    "block": {(1, 0): ((1, 0), (1, 1), (0, 2), (2, 0), (0, 3), (3, 0), (2, 1), (1, 2), (3, 1)), (2, 0): ((2, 3), (3, 2))},
    "project": {},
    "attend": {(0, 1): ((0, 0),), (1, 1): ((1, 3), (0, 5)), (1, 2): ((2, 2), (0, 4)), (2, 0): ((0, 7), (3, 3)), (2, 1): ((1, 5),), (3, 0): ((0, 6),), (3, 1): ((1, 7), (1, 4)), (3, 2): ((2, 5),)},
    "turn": {(0, 0): ((0, 1),)},
    "norm": {(0, 0): ((3, 5), (1, 6), (0, 8))},
    "feed": {},
    "middle": {},
    "expand": {(0, 0): ((2, 7),), (0, 1): ((2, 4),), (1, 0): ((3, 7),), (1, 1): ((3, 4), (1, 8), (2, 6)), (2, 1): ((3, 6), (2, 8)), (3, 1): ((3, 8),)},
    "shrink": {},
}


def half(n, tokens):
    return pl.ds(pl.multiple_of(n * (tokens // 2), 32), tokens // 2)


def square(whole, m, z):
    return whole[m, z].reshape(D, D)


def strip(s):
    return pl.ds(pl.multiple_of(s * STRIP, STRIP), STRIP)


def forward_kernel(fused, rows, length, *refs):
    n_sem = len(Gather.sems) if fused else 0
    x_in, cot_in, seg_ref, vec_in = refs[:4]
    n_in = 10 if fused else 6
    ins = refs[4:n_in]
    outs = refs[n_in : n_in + 13]
    (whole_out, qkv_out, ctx_out, prob_out, act_out, slope_out, normed_out, rstd_out, ds_out, turned_out, low_out,
     result_out, part_out) = outs
    rest = refs[n_in + 13 :]
    gather_sems, rest = rest[:n_sem], rest[n_sem:]
    (whole, bias, biases, joint, vec, x, cot, qkv, ctx, prob, act, slope, mixed, normed, rstd, low, turned,
     result, part, in_sem, w_sem, qkv_sem, ctx_sem, prob_sem, act_sem, slope_sem, end_sem) = rest
    tokens = rows * length
    strips = tokens // STRIP
    heads = D // HEAD // 4
    width = heads * HEAD
    z_own = lax.axis_index("mp")
    x_copy = pltpu.make_async_copy(x_in, x, in_sem.at[0])
    cot_copy = pltpu.make_async_copy(cot_in, cot, in_sem.at[1])
    x_copy.start()
    if fused:
        triple_in, output_in, e_ref, s_ref, qv_ref, eb_ref = ins
        joint_copies = [
            pltpu.make_async_copy(triple_in.at[j], joint.at[pl.ds(j * width, width)], in_sem.at[2 + j]) for j in range(3)
        ] + [pltpu.make_async_copy(output_in, joint.at[pl.ds(3 * width, width)], in_sem.at[5])]
        for copy in joint_copies:
            copy.start()
        gather = Gather((e_ref, s_ref), whole, bias, biases, gather_sems)
        gather.begin()
        bias[...] = jnp.zeros_like(bias)
        for h in range(heads):
            for j in (0, 1):
                at = slice(2 * j * width + h * HEAD, 2 * j * width + (h + 1) * HEAD)
                bias[0:1, at] = qv_ref[h, j : j + 1, :].astype(F32)
        for b in range(D // HEAD):
            bias[1:2, b * HEAD : (b + 1) * HEAD] = eb_ref[b : b + 1, :].astype(F32)
        for copy in joint_copies:
            copy.wait()
        for j in (0, 1):
            columns = joint[:, j * CHUNK : (j + 1) * CHUNK].T
            whole[0, z_own, 2 * j : 2 * j + 2] = columns.reshape(2, 2, SLICE, D)
        gather.begin_first()
        gather.local(1).start()
        gather.local(2).start()
        own_bias = pltpu.make_async_copy(bias, biases.at[z_own], w_sem.at[0])
        own_bias.start()
        own_bias.wait()
    else:
        copy = pltpu.make_async_copy(ins[0], whole, w_sem.at[0])
        copy.start()
        small = pltpu.make_async_copy(ins[1], biases, w_sem.at[1])
        small.start()
        copy.wait()
        small.wait()
    cot_copy.start()
    vec[0:6, :] = vec_in[...].astype(F32)

    def block(i):
        return crossed(z_own, i)

    def turned_copy(slot):
        return pltpu.make_async_copy(turned.at[slot], turned_out.at[slot], end_sem.at[slot])

    def qkv_copy(i):
        return pltpu.make_async_copy(qkv.at[i % 2], qkv_out.at[block(i)], qkv_sem.at[i % 2])

    def ctx_copy(i):
        return pltpu.make_async_copy(ctx.at[i % 2], ctx_out.at[block(i)], ctx_sem.at[i % 2])

    def prob_copy(i, r):
        return pltpu.make_async_copy(prob.at[r], prob_out.at[block(i), r], prob_sem.at[r])

    def act_copy(i):
        return pltpu.make_async_copy(act.at[i % 2], act_out.at[block(i)], act_sem.at[i % 2])

    def slope_copy(i):
        return pltpu.make_async_copy(slope.at[i % 2], slope_out.at[block(i)], slope_sem.at[i % 2])

    def whole_copy(m):
        return pltpu.make_async_copy(whole.at[m], whole_out.at[m], w_sem.at[m])

    def events(place, i=0, n=0):
        for (a, b), due in EVENTS[place].items() if fused else ():

            @pl.when((i == a) & (n == b))
            def _(due=due):
                for kind, step in due:
                    gather.run(kind, step)

    x_copy.wait()

    @pl.loop(0, 4)
    def _(i):
        events("block", i)
        z = block(i)
        slot = i % 2

        @pl.when(i >= 2)
        def _():
            qkv_copy(i - 2).wait()
            ctx_copy(i - 2).wait()

        @pl.loop(0, 2)
        def _(n):
            at = half(n, tokens)
            qkv[slot, at, :] = (mm(x[at, :], square(whole, 0, z), NN) + biases[z, 0:1, :]).astype(BF)
            events("project", i, n)

        qkv_copy(i).start()

        @pl.loop(0, rows)
        def _(r):
            at = pl.ds(pl.multiple_of(r * length, 32), length)
            pl.when(i >= 1)(lambda: prob_copy(i - 1, r).wait())
            pair = seg_ref[pl.ds(z_own * rows + r, 1), :]
            number = lax.broadcasted_iota(jnp.int32, (8, length), 0)
            among = jnp.where(number == pair, 1.0, 0.0).astype(BF)
            mask = (mm(among, among, TN) - 1.0) * -MASKED

            def part_of(j, h):
                return qkv[slot, at, j * width + h * HEAD : j * width + (h + 1) * HEAD]

            scale = jnp.asarray(HEAD ** (-0.5), BF)
            scores = [mm(part_of(1, h), part_of(0, h) * scale, NT) + mask for h in range(heads)]
            probs = []
            for h in range(heads):
                weights = jnp.exp(scores[h] - jnp.max(scores[h], axis=0, keepdims=True))
                share = 1.0 / jnp.sum(weights, axis=0, keepdims=True)
                probs.append((weights * share).astype(BF))
            for h in range(heads):
                prob[r, h] = probs[h]
            done = [mm(part_of(2, h), probs[h], TN).astype(BF) for h in range(heads)]
            ctx[slot, at, :] = jnp.concatenate(done, axis=0).T
            prob_copy(i, r).start()
            events("attend", i, r)

        ctx_copy(i).start()

        @pl.when(i == 0)
        def _():
            @pl.loop(0, strips)
            def _(s):
                value = x[strip(s), :]
                mixed[strip(s), :] = value.astype(F32) + vec[2:3, :]
                turned[0, :, strip(s)] = value.T

            turned_copy(0).start()
            events("turn")

        @pl.loop(0, tokens // CHUNK)
        def _(c):
            at = pl.ds(pl.multiple_of(c * CHUNK, CHUNK), CHUNK)
            add = mm(ctx[slot, at, :], square(whole, 0, z)[:, 3 * width :], NT)
            mixed[at, :] = mixed[at, :] + add

    whole_copy(0).start()

    @pl.loop(0, strips)
    def _(s):
        at = strip(s)
        hidden, normal, scale = norm_forward(mixed[at, :], vec[0:1, :], vec[1:2, :])
        normed[at, :] = normal
        rstd[at, :] = jnp.broadcast_to(scale, (STRIP, 128))
        mixed[at, :] = hidden + vec[5:6, :]
        hidden = hidden.astype(BF)
        low[at, :] = hidden
        turned[1, :, at] = hidden.T

    events("norm")
    turned_copy(1).start()
    normed_copy = pltpu.make_async_copy(normed, normed_out, end_sem.at[3])
    normed_copy.start()
    rstd_copy = pltpu.make_async_copy(rstd, rstd_out, end_sem.at[4])
    rstd_copy.start()
    if fused:
        gather.local(1).wait()
        gather.local(2).wait()

    @pl.loop(0, 4)
    def _(i):
        events("feed", i)
        z = block(i)
        slot = i % 2

        @pl.when(i >= 2)
        def _():
            act_copy(i - 2).wait()
            slope_copy(i - 2).wait()

        @pl.loop(0, 2)
        def _(n):
            at = half(n, tokens)
            u = mm(low[at, :], square(whole, 1, z), NN) + biases[z, 1:2, :]
            cumulative = 0.5 + 0.5 * lax.erf(u * SQRT_HALF)
            act[slot, at, :] = (u * cumulative).astype(BF)
            slope[slot, at, :] = (cumulative + u * jnp.exp(-0.5 * u * u) * INV_ROOT_TAU).astype(BF)
            events("expand", i, n)

        act_copy(i).start()
        slope_copy(i).start()
        events("middle", i)
        for m in (1, 2):
            pltpu.make_async_copy(whole.at[m, z], whole_out.at[m, z], w_sem.at[m]).start()

        @pl.loop(0, 2)
        def _(n):
            at = half(n, tokens)
            mixed[at, :] = mixed[at, :] + mm(act[slot, at, :], square(whole, 2, z), NN)
            events("shrink", i, n)

    normed_copy.wait()
    cot_copy.wait()
    part[...] = jnp.zeros_like(part)

    @pl.loop(0, strips)
    def _(s):
        at = strip(s)
        block_result, normal, scale = norm_forward(mixed[at, :], vec[3:4, :], vec[4:5, :])
        result[at, :] = block_result.astype(BF)
        back = cot[at, :].astype(F32)
        dsummed = norm_backward(back, vec[3:4, :], normal, scale)
        normed[at, :] = dsummed
        dsummed_low = dsummed.astype(BF)
        low[at, :] = dsummed_low
        turned[2, :, at] = dsummed_low.T
        part[3:4, :] += jnp.sum(back * normal, axis=0, keepdims=True)
        part[4:5, :] += jnp.sum(back, axis=0, keepdims=True)
        part[5:6, :] += jnp.sum(dsummed, axis=0, keepdims=True)
        pltpu.make_async_copy(normed.at[at], ds_out.at[at], end_sem.at[5]).start()
        pltpu.make_async_copy(result.at[at], result_out.at[at], end_sem.at[6]).start()
        pltpu.make_async_copy(low.at[at], low_out.at[at], end_sem.at[8]).start()

    last = [
        turned_copy(2),
        pltpu.make_async_copy(part, part_out, end_sem.at[7]),
    ]
    for copy in last:
        copy.start()
    last = last + [
        pltpu.make_async_copy(normed, ds_out, end_sem.at[5]),
        pltpu.make_async_copy(result, result_out, end_sem.at[6]),
        pltpu.make_async_copy(low, low_out, end_sem.at[8]),
    ]
    for i in (2, 3):
        qkv_copy(i).wait()
        ctx_copy(i).wait()
        act_copy(i).wait()
        slope_copy(i).wait()
    for r in range(rows):
        prob_copy(3, r).wait()
    turned_copy(0).wait()
    turned_copy(1).wait()
    rstd_copy.wait()
    for m in range(3):
        whole_copy(m).wait()
    for copy in last:
        copy.wait()
    if fused:
        gather.finish()


def run_forward(x, cot, segments, vector_params, weights, biases):
    rows, length, _ = x.shape
    tokens = rows * length
    fused = lax.axis_size("dp") == 8 and lax.axis_size("mp") == 4
    hbm, vmem = pl.BlockSpec(memory_space=pl.ANY), pl.BlockSpec(memory_space=pltpu.VMEM)
    flat = (tokens, D)
    width = D // 4
    block = (4, 2, SLICE, D)
    dense = [x.reshape(flat), cot.reshape(flat), segments, vector_params]
    if fused:
        triple, output, expand, shrink = weights
        held = [triple.transpose(0, 2, 1), output, expand.reshape(block), shrink.reshape(block)]
        held = held + [biases[0].transpose(1, 0, 2), biases[1]]
        spaces = [hbm, hbm, hbm, hbm, vmem, vmem]
    else:
        mats = pack_weights(*weights)
        held = [jnp.stack([lax.all_gather(m, "mp", axis=0) for m in mats]).reshape((3, 4) + block)]
        held = held + [lax.all_gather(pack_biases(*biases), "mp", axis=0)]
        spaces = [hbm, hbm]
    probs = (rows, D // HEAD // 4, length, length)
    shape = jax.ShapeDtypeStruct
    dma = pltpu.SemaphoreType.DMA
    return pl.pallas_call(
        functools.partial(forward_kernel, fused, rows, length),
        out_shape=(
            shape((3, 4) + block, BF),
            shape((4,) + flat, BF),
            shape((4, tokens, width), BF),
            shape((4,) + probs, BF),
            shape((4,) + flat, BF),
            shape((4,) + flat, BF),
            shape(flat, F32),
            shape((tokens, 128), F32),
            shape(flat, F32),
            shape((3, D, tokens), BF),
            shape(flat, BF),
            shape(flat, BF),
            shape((VECTORS, D), F32),
        ),
        in_specs=[hbm, hbm, vmem, vmem] + spaces,
        out_specs=(hbm,) * 13,
        scratch_shapes=([dma(s) for s in Gather.sems] if fused else [])
        + [
            pltpu.VMEM((3, 4) + block, BF),
            pltpu.VMEM((VECTORS, D), F32),
            pltpu.VMEM((4, VECTORS, D), F32),
            pltpu.VMEM((D, D), BF),
            pltpu.VMEM((VECTORS, D), F32),
            pltpu.VMEM(flat, BF),
            pltpu.VMEM(flat, BF),
            pltpu.VMEM((2,) + flat, BF),
            pltpu.VMEM((2, tokens, width), BF),
            pltpu.VMEM(probs, BF),
            pltpu.VMEM((2,) + flat, BF),
            pltpu.VMEM((2,) + flat, BF),
            pltpu.VMEM(flat, F32),
            pltpu.VMEM(flat, F32),
            pltpu.VMEM((tokens, 128), F32),
            pltpu.VMEM(flat, BF),
            pltpu.VMEM((3, D, tokens), BF),
            pltpu.VMEM(flat, BF),
            pltpu.VMEM((VECTORS, D), F32),
            dma((6,)),
            dma((3,)),
            dma((2,)),
            dma((2,)),
            dma((rows,)),
            dma((2,)),
            dma((2,)),
            dma((9,)),
        ],
        compiler_params=pltpu.CompilerParams(
            collective_id=0 if fused else None, has_side_effects=True, vmem_limit_bytes=VMEM_MOST
        ),
        name="forward",
    )(*dense, *held)


BACK_EVENTS = {
    "shrink": {(0, 0): ((0, 0),), (1, 0): ((0, 2),), (2, 0): ((0, 4), (2, 1), (1, 3)), (3, 0): ((0, 6), (1, 5))},
    "slope": {(1, 0): ((1, 1),), (1, 1): ((2, 0),), (2, 0): ((3, 0),), (3, 0): ((2, 3),)},
    "expand": {(0, 0): ((0, 1), (1, 0)), (1, 0): ((0, 3), (1, 2)), (2, 0): ((0, 5), (1, 4), (2, 2)), (3, 0): ((0, 7), (1, 6), (2, 4))},
    "hidden": {(2, 0): ((3, 1),), (3, 1): ((3, 2),)},
    "norm": {(0, 0): ((1, 7), (2, 5))},
    "attend": {(0, 0): ((3, 3),), (0, 2): ((2, 6),), (0, 3): ((3, 4),), (1, 0): ((3, 5),), (1, 1): ((1, 8), (3, 6)), (1, 2): ((3, 7),), (2, 0): ((2, 8),), (2, 2): ((1, 9),), (2, 3): ((3, 8),), (3, 1): ((2, 9),), (3, 2): ((1, 10),)},
    "project": {(0, 0): ((0, 8),), (1, 0): ((0, 9),), (2, 0): ((0, 10),), (3, 0): ((0, 11), (3, 9))},
    "pull": {(0, 0): ((2, 7),), (2, 0): ((2, 10),), (3, 0): ((1, 11),)},
    "last": {(0, 0): ((3, 10), (2, 11), (3, 11))},
}


def turn_block(j):
    return 3 * j % 4


def backward_kernel(fused, rows, length, *refs):
    n_sem = len(Scatter.sems) if fused else 0
    n_buf = len(Scatter.buffers) if fused else 0
    (vec_in, part_in, whole, qkv_in, ctx_in, prob_in, act_in, slope_in, normed_in, rstd_in, ds_in, turned_in,
     low_in) = refs[:13]
    grad_out, small_out, input_out = refs[13:16]
    rest = refs[16:]
    buffers, sems, rest = rest[:n_buf], rest[n_buf : n_buf + n_sem], rest[n_buf + n_sem :]
    (grads, weights, wide, tall, stream, normed, rstd, low, turned, prob, ctx, dctx, part, vec,
     w_sem, wide_sem, tall_sem, prob_sem, ctx_sem, turned_sem, end_sem) = rest
    tokens = rows * length
    strips = tokens // STRIP
    heads = D // HEAD // 4
    width = heads * HEAD

    def weight_copy(m, j, slot):
        return pltpu.make_async_copy(whole.at[m, turn_block(j)], weights.at[slot], w_sem.at[slot])

    def wide_copy(source, j):
        return pltpu.make_async_copy(source.at[turn_block(j)], wide.at[j % 2], wide_sem.at[j % 2])

    def tall_copy(j):
        return pltpu.make_async_copy(slope_in.at[turn_block(j)], tall.at[j % 2], tall_sem.at[j % 2])

    def turned_copy(source, slot):
        return pltpu.make_async_copy(turned_in.at[source], turned.at[slot], turned_sem.at[slot])

    def prob_copy(g):
        return pltpu.make_async_copy(prob_in.at[turn_block(g // rows), g % rows], prob.at[g % 2], prob_sem.at[g % 2])

    def ctx_copy(j):
        return pltpu.make_async_copy(ctx_in.at[turn_block(j)], ctx.at[j % 2], ctx_sem.at[j % 2])

    stream_copy = pltpu.make_async_copy(ds_in, stream, end_sem.at[0])
    normed_copy = pltpu.make_async_copy(normed_in, normed, end_sem.at[1])
    rstd_copy = pltpu.make_async_copy(rstd_in, rstd, end_sem.at[2])
    low_copy = pltpu.make_async_copy(low_in, low, end_sem.at[4])
    for t in range(PIECES):
        for source, target, sem in ((turned_in.at[2], turned.at[0], turned_sem), (act_in.at[0], wide.at[0], wide_sem)):
            at = pl.ds(t * (source.shape[0] // PIECES), source.shape[0] // PIECES)
            pltpu.make_async_copy(source.at[at], target.at[at], sem.at[0]).start()
    weight_copy(2, 0, 0).start()
    low_copy.start()
    tall_copy(0).start()
    turned_copy(1, 1).start()
    weight_copy(1, 0, 1).start()
    stream_copy.start()
    wide_copy(act_in, 1).start()
    tall_copy(1).start()
    weight_copy(2, 1, 2).start()
    weight_copy(1, 1, 3).start()
    normed_copy.start()
    rstd_copy.start()
    if fused:
        scatter = Scatter(grads, buffers, sems)
        scatter.begin()

    def events(place, j=0, n=0):
        for (a, c), due in BACK_EVENTS[place].items() if fused else ():

            @pl.when((j == a) & (n == c))
            def _(due=due):
                for kind, step in due:
                    scatter.run(kind, step)

    vec[0:6, :] = vec_in[...].astype(F32)
    part[...] = jnp.zeros_like(part)
    part[0:VECTORS, :] = part_in[...]

    def outer(slot, turned_slot, right, offset=0):
        product = mm(turned[turned_slot], right, NN).astype(BF)
        count = product.shape[1]
        grads[slot, :, :, :, offset : offset + count] = product.reshape(4, 2, SLICE, count)

    def emit(slot, m, z):
        if not fused:
            copy = pltpu.make_async_copy(grads.at[slot], grad_out.at[m, z], end_sem.at[3])
            copy.start()
            copy.wait()

    turned_copy(2, 0).wait()

    @pl.loop(0, 4)
    def _(j):
        parity = j % 2
        slot = 2 * parity
        z = turn_block(j)
        wide_copy(act_in, j).wait()

        outer(j, 0, wide[parity])
        events("shrink", j)
        emit(j, 2, z)

        @pl.when(j == 0)
        def _():
            low_copy.wait()
            turned_copy(1, 1).wait()
            stream_copy.wait()

        weight_copy(2, j, slot).wait()
        tall_copy(j).wait()

        @pl.loop(0, 2)
        def _(n):
            at = half(n, tokens)
            dactive = mm(low[at, :], weights[slot], NT)
            value = (dactive * tall[parity, at, :].astype(F32)).astype(BF)
            tall[2, at, :] = value
            line = pl.ds(10 + z, 1)
            part[line, :] = part[line, :] + jnp.sum(value.astype(F32), axis=0, keepdims=True)
            events("slope", j, n)

        outer(4 + j, 1, tall[2])
        events("expand", j)
        emit(4 + j, 1, z)
        weight_copy(1, j, slot + 1).wait()

        @pl.loop(0, 2)
        def _(n):
            at = half(n, tokens)
            stream[at, :] = stream[at, :] + mm(tall[2, at, :], weights[slot + 1], NT)
            events("hidden", j, n)

        @pl.when(j < 2)
        def _():
            wide_copy(act_in, j + 2).start()
            tall_copy(j + 2).start()
            weight_copy(2, j + 2, slot).start()
            weight_copy(1, j + 2, slot + 1).start()

        @pl.when(j == 2)
        def _():
            wide_copy(qkv_in, 0).start()
            weight_copy(0, 0, 0).start()
            weight_copy(0, 1, 1).start()
            ctx_copy(0).start()
            ctx_copy(1).start()
            prob_copy(0).start()

        @pl.when(j == 3)
        def _():
            wide_copy(qkv_in, 1).start()
            weight_copy(0, 2, 2).start()
            weight_copy(0, 3, 3).start()
            turned_copy(0, 0).start()

    normed_copy.wait()
    rstd_copy.wait()

    @pl.loop(0, strips)
    def _(s):
        at = strip(s)
        dhidden, normal = stream[at, :], normed[at, :]
        dmixed = norm_backward(dhidden, vec[0:1, :], normal, rstd[at, 0:1])
        part[0:1, :] += jnp.sum(dhidden * normal, axis=0, keepdims=True)
        part[1:2, :] += jnp.sum(dhidden, axis=0, keepdims=True)
        part[2:3, :] += jnp.sum(dmixed, axis=0, keepdims=True)
        stream[at, :] = dmixed
        dmixed = dmixed.astype(BF)
        low[at, :] = dmixed
        turned[1, :, at] = dmixed.T

    events("norm")
    turned_copy(0, 0).wait()
    dproj = tall

    def pull(j):
        @pl.loop(0, 2)
        def _(n):
            at = half(n, tokens)
            stream[at, :] = stream[at, :] + mm(dproj[j % 3, at, 0 : 3 * width], weights[j, :, 0 : 3 * width], NT)
            events("pull", j, n)

    @pl.loop(0, 4)
    def _(j):
        parity = j % 2
        z = turn_block(j)
        weight_copy(0, j, j).wait()
        wide_copy(qkv_in, j).wait()
        ctx_copy(j).wait()
        dctx[...] = mm(low[...], weights[j, :, 3 * width :], NN).astype(BF)

        @pl.loop(0, rows)
        def _(r):
            at = pl.ds(pl.multiple_of(r * length, 32), length)
            g = j * rows + r
            prob_copy(g).wait()
            pl.when(g + 1 < 4 * rows)(lambda: prob_copy(g + 1).start())
            scale = jnp.asarray(HEAD ** (-0.5), BF)

            def part_of(i, h):
                return wide[parity, at, i * width + h * HEAD : i * width + (h + 1) * HEAD]

            def dc(h):
                return dctx[at, h * HEAD : (h + 1) * HEAD]

            dprobs = [mm(part_of(2, h), dc(h), NT) for h in range(heads)]
            dscores = []
            for h in range(heads):
                full = prob[g % 2, h].astype(F32)
                inner = jnp.sum(full * dprobs[h], axis=0, keepdims=True)
                dscores.append((full * (dprobs[h] - inner)).astype(BF))
            dv = [mm(prob[g % 2, h], dc(h), NN).astype(BF) for h in range(heads)]
            dk = [mm(dscores[h], part_of(0, h) * scale, NN).astype(BF) for h in range(heads)]
            dq = [(mm(part_of(1, h), dscores[h], TN) * HEAD ** (-0.5)).astype(BF) for h in range(heads)]
            dq = [jnp.concatenate(dq, axis=0).T]
            joined = jnp.concatenate(dq + dk + dv, axis=1)
            dproj[j % 3, at, 0 : 3 * width] = joined
            line = pl.ds(6 + z, 1)
            before = jnp.where(r == 0, 0.0, part[line, 0 : 3 * width])
            part[line, 0 : 3 * width] = before + jnp.sum(joined.astype(F32), axis=0, keepdims=True)
            events("attend", j, r)

        if fused:
            for k in range(4):
                pl.when(j == k)(lambda k=k: scatter.to_core(2 * k).wait_send())
            pl.when(j == 3)(lambda: scatter.small_stage(part, 0))

        outer(j, 0, dproj[j % 3, :, 0 : 3 * width])
        outer(j, 1, ctx[parity], 3 * width)
        emit(j, 0, z)
        events("project", j)

        @pl.when(j < 2)
        def _():
            wide_copy(qkv_in, j + 2).start()
            ctx_copy(j + 2).start()

        pl.when(j == 0)(lambda: pull(j))

    pull(1)
    if fused:
        scatter.small_stage(part, 1)
    pull(2)
    if fused:
        scatter.small_stage(part, 2)
    pull(3)
    input_copy = pltpu.make_async_copy(stream, input_out, end_sem.at[0])
    input_copy.start()
    if fused:
        events("last")
        scatter.small_stage(part, 3)
        grad_out[2] = scatter.total(2)
        grad_out[1] = scatter.total(1)
        small_out[...] = scatter.small_stage(part, 4)
        grad_out[0] = scatter.total(0)
        scatter.finish(part)
    else:
        small_out[...] = part[...]
    input_copy.wait()


def run_backward(vector_params, part, saved, rows, length):
    fused = lax.axis_size("dp") == 8 and lax.axis_size("mp") == 4
    hbm, vmem = pl.BlockSpec(memory_space=pl.ANY), pl.BlockSpec(memory_space=pltpu.VMEM)
    tokens = rows * length
    flat = (tokens, D)
    width = D // 4
    block = (4, 2, SLICE, D)
    shape = jax.ShapeDtypeStruct
    dma = pltpu.SemaphoreType.DMA
    whole_grad = shape((3, SLICE, D), F32) if fused else shape((3, 4) + block, BF)
    saved = [saved[0].reshape(3, 4, D, D)] + list(saved[1:])
    grads, sums, input_grad = pl.pallas_call(
        functools.partial(backward_kernel, fused, rows, length),
        out_shape=(whole_grad, shape((SMALL, D), F32), shape(flat, F32)),
        in_specs=[vmem] * 2 + [hbm] * 11,
        out_specs=(vmem if fused else hbm, vmem, hbm),
        scratch_shapes=([pltpu.VMEM(s, t) for s, t in Scatter.buffers] + [dma(s) for s in Scatter.sems] if fused else [])
        + [
            pltpu.VMEM((8,) + block, BF),
            pltpu.VMEM((4, D, D), BF),
            pltpu.VMEM((2,) + flat, BF),
            pltpu.VMEM((3,) + flat, BF),
            pltpu.VMEM(flat, F32),
            pltpu.VMEM(flat, F32),
            pltpu.VMEM((tokens, 128), F32),
            pltpu.VMEM(flat, BF),
            pltpu.VMEM((2, D, tokens), BF),
            pltpu.VMEM((2, D // HEAD // 4, length, length), BF),
            pltpu.VMEM((2, tokens, width), BF),
            pltpu.VMEM((tokens, width), BF),
            pltpu.VMEM((SMALL, D), F32),
            pltpu.VMEM((VECTORS, D), F32),
            dma((4,)),
            dma((2,)),
            dma((2,)),
            dma((2,)),
            dma((2,)),
            dma((2,)),
            dma((5,)),
        ],
        compiler_params=pltpu.CompilerParams(
            collective_id=1 if fused else None, has_side_effects=True, vmem_limit_bytes=VMEM_MOST
        ),
        name="backward",
    )(vector_params, part, *saved)
    if not fused:
        parts = lax.axis_size("dp")
        grads = lax.psum_scatter(grads.reshape(3, 4, D, D), "dp", scatter_dimension=2, tiled=True)
        grads = lax.psum_scatter(grads, "mp", scatter_dimension=1, tiled=True)
        grads = grads.reshape(3, D // parts, D).astype(F32)
        sums = lax.psum(sums, ("dp", "mp"))
    return input_grad, grads, sums


RATES = (D ** (-0.5), 0.5, (D // 16) ** (-0.5), D ** (-0.5), 0.5, FF ** (-0.5), 0.3)


LARGE = (3, 5, 0, 2)
PIECES = 4


def update_kernel(reduced, sums, result_in, input_in, *refs):
    state, outs = list(refs[:21]), list(refs[21:49])
    result_out, input_out, result, input_grad = refs[49:53]
    held, load_sem, store_sem, sems = refs[53:81], *refs[81:]
    piece = input_in.shape[0] // PIECES
    moves = []
    for t in range(PIECES):
        at = pl.ds(t * piece, piece)
        for j, (source, middle, target) in enumerate(((input_in, input_grad, input_out), (result_in, result, result_out))):
            moves.append((
                pltpu.make_async_copy(source.at[at], middle.at[at], sems.at[2 * j, t]),
                pltpu.make_async_copy(middle.at[at], target.at[at], sems.at[2 * j + 1, t]),
            ))
    loads, stores = {}, {}
    for t, i in enumerate(LARGE):
        mine = held[7 * t : 7 * t + 7]
        loads[i] = [pltpu.make_async_copy(state[3 * i + j], mine[j], load_sem.at[t, j]) for j in range(3)]
        stores[i] = [pltpu.make_async_copy(mine[3 + j], outs[4 * i + j], store_sem.at[t, j]) for j in range(4)]
        state[3 * i : 3 * i + 3] = mine[:3]
        outs[4 * i : 4 * i + 4] = mine[3:]
    for copy in loads[3]:
        copy.start()
    for load, _ in moves:
        load.start()
    for i in LARGE[1:]:
        for copy in loads[i]:
            copy.start()
    dp, mp = lax.axis_index("dp"), lax.axis_index("mp")
    groups = lax.axis_size("mp")
    width = D // groups
    own = width // HEAD

    def update(i, gradient, at=Ellipsis):
        new = adam_update(*(state[3 * i + j][at] for j in range(3)), gradient, RATES[i])
        for j in range(4):
            outs[4 * i + j][at] = new[j]

    def wait(copies):
        for copy in copies:
            copy.wait()

    def start(copies):
        for copy in copies:
            copy.start()

    wait(loads[3])
    update(3, reduced[1])
    start(stores[3])
    for load, store in moves:
        load.wait()
        store.start()
    wait(loads[5])
    update(5, reduced[2])
    start(stores[5])
    wait(loads[0])
    mixing = reduced[0]
    for j in range(3):
        update(0, mixing[:, j * width : (j + 1) * width], j)
    start(stores[0])
    wait(loads[2])
    update(2, mixing[:, 3 * width :].T)
    start(stores[2])

    def lanes(row, count, first):
        return pltpu.roll(sums[pl.ds(row, count), :], lax.rem(D - first, D), 1)

    piece = state[3].shape[2]
    moved = lanes(6 + mp, 1, dp * piece)
    for j in (0, 1):
        for h in range(own):
            at = 2 * j * width + h * HEAD
            update(1, moved[:, at : at + piece], (h, slice(j, j + 1)))
    piece = state[12].shape[0]
    moved = lanes(10 + mp, 1, dp * piece)
    blocks = [moved[:, b * HEAD : b * HEAD + piece] for b in range(D // HEAD)]
    update(4, jnp.concatenate(blocks, axis=0).T)
    piece = state[18].shape[1]
    update(6, lanes(0, 8, (dp * groups + mp) * piece)[0:6, 0:piece])
    for i in LARGE:
        wait(stores[i])
    for _, store in moves:
        store.wait()


AXES = ((0, 1, 2), (1, 0, 2), (0, 1), (0, 1), (1, 0), (1, 0), (0, 1))


def update_all(state, reduced, sums, result, input_grad):
    hbm, vmem = pl.BlockSpec(memory_space=pl.ANY), pl.BlockSpec(memory_space=pltpu.VMEM)
    state = [s.transpose(AXES[i // 3]) for i, s in enumerate(state)]
    shapes = []
    for i in range(7):
        shapes = shapes + [jax.ShapeDtypeStruct(state[3 * i].shape, t) for t in (F32, F32, F32, BF)]
    kept = [jax.ShapeDtypeStruct(a.shape, a.dtype) for a in (result, input_grad)]
    held = []
    for i in LARGE:
        held = held + [pltpu.VMEM(state[3 * i].shape, t) for t in (F32,) * 6 + (BF,)]
    dma = pltpu.SemaphoreType.DMA
    state_specs = [hbm if i // 3 in LARGE else vmem for i in range(21)]
    new_specs = [hbm if i // 4 in LARGE else vmem for i in range(28)]
    *new, result, input_grad = pl.pallas_call(
        update_kernel,
        out_shape=tuple(shapes + kept),
        in_specs=[vmem] * 2 + [hbm] * 2 + state_specs,
        out_specs=tuple(new_specs) + (hbm,) * 2,
        scratch_shapes=[pltpu.VMEM(a.shape, a.dtype) for a in kept] + held + [dma((4, 3)), dma((4, 4)), dma((4, PIECES))],
        name="update",
    )(reduced, sums, result, input_grad, *state)
    return result, input_grad, tuple(s.transpose(AXES[i // 4]) for i, s in enumerate(new))


def per_device(
    activations,
    cotangent,
    segments,
    triple_weight,
    query_value_bias,
    output_weight,
    expand_weight,
    expand_bias,
    shrink_weight,
    vector_params,
    *state,
):
    rows, length, _ = activations.shape
    weights = (triple_weight, output_weight, expand_weight, shrink_weight)
    *saved, result, part = run_forward(
        activations, cotangent, segments, vector_params, weights, (query_value_bias, expand_bias)
    )
    input_grad, reduced, sums = run_backward(vector_params, part, saved, rows, length)
    result, input_grad, new = update_all(state, reduced, sums, result, input_grad)
    return (result.reshape(activations.shape), input_grad.reshape(activations.shape)) + new


STATE_SPECS = (
    P(None, "dp", "mp"),
    P(None, "mp", "dp"),
    P("mp", "dp"),
    P("dp", "mp"),
    P("mp", "dp"),
    P("mp", "dp"),
    P(None, ("dp", "mp")),
)


def solution(mesh):
    rows = P(("dp", "mp"), None, None)
    placed = (
        rows,
        rows,
        P("dp", None),
        P(None, None, "mp"),
        P(None, "mp", None),
        P("mp", None),
        P(None, "mp"),
        P("mp", None),
        P("mp", None),
        P(),
    )
    for spec in STATE_SPECS:
        placed = placed + (spec,) * 3
    out_specs = (rows, rows)
    for spec in STATE_SPECS:
        out_specs = out_specs + (spec,) * 4
    return jax.shard_map(per_device, mesh=mesh, in_specs=placed, out_specs=out_specs, check_vma=False)
```

```python
import functools

import jax
import jax.numpy as jnp
from jax import lax
from jax.experimental import pallas as pl
from jax.experimental.pallas import tpu as pltpu
from jax.sharding import PartitionSpec as P

D = 768
HEAD = 64
FF = 3072
STEP = 10


NORM_EPS = 1e-05
BETA_ONE = 0.5
BETA_TWO = 0.6
ADAM_EPS = 1e-08
WEIGHT_DECAY = 0.01
MASKED = -1e30
SQRT_HALF = 0.7071067811865476
INV_ROOT_TAU = 0.3989422804014327


def norm_forward(summed, gain, shift):
    centre = summed - jnp.mean(summed, axis=-1, keepdims=True)
    scale = lax.rsqrt(jnp.mean(centre * centre, axis=-1, keepdims=True) + NORM_EPS)
    normed = centre * scale
    return (gain * normed + shift, normed, scale)


def norm_backward(gradient, gain, normed, scale):
    scaled = gradient * gain
    centred = scaled - jnp.mean(scaled, axis=-1, keepdims=True)
    return scale * (centred - normed * jnp.mean(scaled * normed, axis=-1, keepdims=True))


def adam_update(master, first, second, gradient, rate):
    first_new = BETA_ONE * first + (1.0 - BETA_ONE) * gradient
    second_new = BETA_TWO * second + (1.0 - BETA_TWO) * gradient * gradient
    corrected = first_new / (1.0 - BETA_ONE**STEP)
    spread = jnp.sqrt(second_new / (1.0 - BETA_TWO**STEP))
    master_new = master - rate * (corrected / (spread + ADAM_EPS) + WEIGHT_DECAY * master)
    return (master_new, first_new, second_new, master_new.astype(jnp.bfloat16))


MESH = pl.DeviceIdType.MESH
BF = jnp.bfloat16
F32 = jnp.float32
HALF = 48
SLICE = 96
SMALL = 16
VECTORS = 8


def place():
    p, z = lax.axis_index("dp"), lax.axis_index("mp")
    core, xy = p % 2, p // 2
    x, y = xy % 2, xy // 2
    return p, z, core, xy, p + 1 - 2 * core, p + 2 - 4 * x, p + 4 - 8 * y, xy + 1 - 2 * x, xy + 2 - 4 * y


def remote(src, dst, send_sem, recv_sem, p, z):
    return pltpu.make_async_remote_copy(
        src_ref=src, dst_ref=dst, send_sem=send_sem, recv_sem=recv_sem, device_id=(p, z), device_id_type=MESH
    )


def greet(p, z, pc, px, py):
    barrier = pltpu.get_barrier_semaphore()
    for peer in ((pc, z), (px, z), (py, z), (p, (z + 1) % 4), (p, (z + 2) % 4), (p, (z + 3) % 4)):
        pl.semaphore_signal(barrier, inc=1, device_id=peer, device_id_type=MESH)
    pl.semaphore_wait(barrier, 6)


def crossed(z, d):
    return (z // 2 + d // 2) % 2 * 2 + (z % 2 + d % 2) % 2


class Gather:
    steps = [(1, 1), (0, 1), (0, 2), (0, 3), (2, 1), (1, 2), (2, 2), (1, 3), (2, 3)]
    sems = [(3,)] + [(3, 3)] * 12 + [(3,)] * 2

    def __init__(self, mats, whole, bias, biases, sems):
        self.mats, self.whole, self.bias, self.biases = mats, whole, bias, biases
        (self.ls, self.zs, self.zr, self.xs, self.xr, self.ys, self.yr, self.as_, self.ar, self.bs, self.br, self.cs,
         self.cr, self.ss, self.sr) = sems
        self.where = place()

    def local(self, m):
        z = self.where[1]
        return pltpu.make_async_copy(self.mats[m - 1], self.whole.at[m, z], self.ls.at[m])

    def small(self, d):
        p, z = self.where[:2]
        return remote(self.bias, self.biases.at[z], self.ss.at[d - 1], self.sr.at[d - 1], p, crossed(z, d))

    def along_z(self, m, d):
        p, z, core, xy = self.where[:4]
        own = self.whole.at[m, z] if m == 0 else self.mats[m - 1]
        return remote(own.at[xy, core], self.whole.at[m, z, xy, core], self.zs.at[m, d - 1],
                      self.zr.at[m, d - 1], p, crossed(z, d))

    def plane(self, m, d, block, rows, send_sem, recv_sem, peer):
        z = self.where[1]
        part = self.whole.at[m, crossed(z, d), block, self.where[2], rows]
        return remote(part, part, send_sem.at[m, d - 1], recv_sem.at[m, d - 1], peer, z)

    def to_x(self, m, d):
        return self.plane(m, d, self.where[3], slice(None), self.xs, self.xr, self.where[5])

    def to_y(self, m, d):
        return self.plane(m, d, self.where[3], slice(None), self.ys, self.yr, self.where[6])

    def on_to_y(self, m, d):
        return self.plane(m, d, self.where[7], pl.ds(0, HALF), self.as_, self.ar, self.where[6])

    def on_to_x(self, m, d):
        return self.plane(m, d, self.where[8], pl.ds(HALF, HALF), self.bs, self.br, self.where[5])

    def to_core(self, m, d):
        z = self.where[1]
        part = self.whole.at[m, crossed(z, d), :, self.where[2]]
        return remote(part, part, self.cs.at[m, d - 1], self.cr.at[m, d - 1], self.where[4], z)

    def begin(self):
        p, z, _, _, pc, px, py = self.where[:7]
        greet(p, z, pc, px, py)
        self.along_z(1, 1).start()

    def begin_first(self):
        for d in (1, 2, 3):
            self.along_z(0, d).start()
            self.small(d).start()

    def run(self, kind, i):
        m, d = self.steps[i]
        if kind == 0:
            self.along_z(m, d).wait_recv()
            if m == 0:
                self.small(d).wait_recv()
            self.to_x(m, d).start()
            self.to_y(m, d).start()
            if m < 2 and (m, d) != (0, 1):
                self.along_z(m + 1, d).start()
        elif kind == 1:
            self.to_x(m, d).wait_recv()
            self.to_y(m, d).wait_recv()
            self.on_to_y(m, d).start()
            self.on_to_x(m, d).start()
        elif kind == 2:
            self.on_to_y(m, d).wait_recv()
            self.on_to_x(m, d).wait_recv()
            self.to_core(m, d).start()
        else:
            self.to_core(m, d).wait_recv()

    def finish(self):
        for d in (1, 2, 3):
            self.small(d).wait_send()
        for m, d in self.steps:
            for copy in (self.along_z, self.to_x, self.to_y, self.on_to_y, self.on_to_x, self.to_core):
                copy(m, d).wait_send()


class Scatter:
    steps = [(m, k) for k in (0, 3, 2, 1) for m in (2, 1)] + [(0, k) for k in (0, 3, 2, 1)]
    slots = [k + 4 * j for k in range(4) for j in (0, 1)] + list(range(4))
    buffers = [((12, 4, SLICE, D), BF)] + [((12, 2, HALF, D), BF)] * 2 + [((12, HALF, D), BF)] * 2 + [
        ((3, 3, SLICE, D), BF), ((3, 4, SLICE, D), BF), ((6, SMALL, D), F32), ((3, SMALL, D), F32)]
    sems = [(12,)] * 2 + [(12, 2)] * 4 + [(12,)] * 4 + [(3, 3)] * 2 + [(6,)] * 2

    def __init__(self, grads, buffers, sems):
        self.grads = grads
        self.sum, self.rx, self.ry, self.ra, self.rb, self.rz, self.plane, self.rv, self.sv = buffers
        (self.cs, self.cr, self.xs, self.xr, self.ys, self.yr, self.as_, self.ar, self.bs, self.br, self.zs, self.zr,
         self.ss, self.sr) = sems
        self.where = place()

    def to_core(self, i):
        _, z, core, _, pc = self.where[:5]
        return remote(self.grads.at[self.slots[i], :, 1 - core], self.sum.at[i], self.cs.at[i], self.cr.at[i], pc, z)

    def to_x(self, i, t):
        q = (self.where[7], 3 - self.where[3])[t]
        return remote(self.sum.at[i, q, pl.ds(0, HALF)], self.rx.at[i, t], self.xs.at[i, t], self.xr.at[i, t],
                      self.where[5], self.where[1])

    def to_y(self, i, t):
        q = (self.where[8], 3 - self.where[3])[t]
        return remote(self.sum.at[i, q, pl.ds(HALF, HALF)], self.ry.at[i, t], self.ys.at[i, t], self.yr.at[i, t],
                      self.where[6], self.where[1])

    def on_to_y(self, i):
        return remote(self.sum.at[i, self.where[8], pl.ds(0, HALF)], self.ra.at[i], self.as_.at[i], self.ar.at[i],
                      self.where[6], self.where[1])

    def on_to_x(self, i):
        return remote(self.sum.at[i, self.where[7], pl.ds(HALF, HALF)], self.rb.at[i], self.bs.at[i], self.br.at[i],
                      self.where[5], self.where[1])

    def to_owner(self, m, k, d):
        p = self.where[0]
        return remote(self.plane.at[m, k], self.rz.at[m, d - 1], self.zs.at[m, d - 1], self.zr.at[m, d - 1], p, k)

    def along_z(self, m, d):
        return self.to_owner(m, (self.where[1] + d) % 4, d)

    def begin(self):
        p, z, _, _, pc, px, py = self.where[:7]
        greet(p, z, pc, px, py)

    def run(self, kind, j):
        core, xy, xyx, xyy = self.where[2], self.where[3], self.where[7], self.where[8]
        low, high = slice(0, HALF), slice(HALF, SLICE)
        if kind == 0:
            self.to_core(j).start()
        elif kind == 1:
            self.to_core(j).wait_recv()

            @pl.loop(0, 4)
            def _(q):
                self.sum[j, q] = self.sum[j, q] + self.grads[self.slots[j], q, core]

            for t in (1, 0):
                self.to_x(j, t).start()
                self.to_y(j, t).start()
        elif kind == 2:
            for t in (0, 1):
                self.to_x(j, t).wait_recv()
                self.to_y(j, t).wait_recv()
            self.sum[j, xyy, low] = (self.sum[j, xyy, low].astype(F32) + self.rx[j, 1].astype(F32)).astype(BF)
            self.sum[j, xyx, high] = (self.sum[j, xyx, high].astype(F32) + self.ry[j, 1].astype(F32)).astype(BF)
            self.on_to_y(j).start()
            self.on_to_x(j).start()
        else:
            m, k = self.steps[j]
            self.on_to_y(j).wait_recv()
            self.on_to_x(j).wait_recv()
            self.plane[m, k, low] = (
                self.sum[j, xy, low].astype(F32) + self.rx[j, 0].astype(F32) + self.ra[j].astype(F32)
            ).astype(BF)
            self.plane[m, k, high] = (
                self.sum[j, xy, high].astype(F32) + self.ry[j, 0].astype(F32) + self.rb[j].astype(F32)
            ).astype(BF)
            z = self.where[1]
            pl.when(z != k)(lambda: self.to_owner(m, k, (k + 4 - z) % 4).start())

    def total(self, m):
        for d in (1, 2, 3):
            self.along_z(m, d).wait_recv()
        own = self.plane[m, self.where[1]].astype(F32)
        return own + self.rz[m, 0].astype(F32) + self.rz[m, 1].astype(F32) + self.rz[m, 2].astype(F32)

    def small_to(self, s, src, p, z):
        return remote(src, self.rv.at[s], self.ss.at[s], self.sr.at[s], p, z)

    def small_copy(self, part, c):
        p, z, _, _, pc, px, py = self.where[:7]
        if c == 0:
            return self.small_to(0, part, pc, z)
        if c == 1:
            return self.small_to(1, self.sv.at[0], px, z)
        if c == 2:
            return self.small_to(2, self.sv.at[1], py, z)
        return self.small_to(c, self.sv.at[2], p, (z + c - 2) % 4)

    def small_stage(self, part, i):
        if i == 0:
            self.small_copy(part, 0).start()
        elif i < 4:
            self.small_copy(part, i - 1).wait_recv()
            before = part[...] if i == 1 else self.sv[i - 2]
            self.sv[i - 1] = before + self.rv[i - 1]
            for c in (i,) if i < 3 else (3, 4, 5):
                self.small_copy(part, c).start()
        else:
            for c in (3, 4, 5):
                self.small_copy(part, c).wait_recv()
            return self.sv[2] + self.rv[3] + self.rv[4] + self.rv[5]

    def finish(self, part):
        for c in range(6):
            self.small_copy(part, c).wait_send()
        for i in range(len(self.steps)):
            if self.slots[i] not in self.slots[i + 1 :]:
                self.to_core(i).wait_send()
            self.on_to_y(i).wait_send()
            self.on_to_x(i).wait_send()
            for t in (0, 1):
                self.to_x(i, t).wait_send()
                self.to_y(i, t).wait_send()
        for m in range(3):
            for d in (1, 2, 3):
                self.along_z(m, d).wait_send()


def mm(a, b, dims):
    return lax.dot_general(a, b, (dims, ((), ())), preferred_element_type=jnp.float32)


def pack_weights(triple_weight, output_weight, expand_weight, shrink_weight):
    width = triple_weight.shape[2]
    mixing = jnp.concatenate([triple_weight.transpose(1, 0, 2).reshape(D, 3 * width), output_weight.T], axis=1)
    return mixing, expand_weight, shrink_weight


def pack_biases(query_value_bias, expand_bias):
    pair = query_value_bias.reshape(2, -1)
    none = jnp.zeros_like(pair[0])
    first = jnp.concatenate([pair[0], none, pair[1], none])
    return jnp.concatenate([first[None], expand_bias.reshape(1, -1), jnp.zeros((VECTORS - 2, D), BF)]).astype(F32)


TN = ((0,), (0,))
NT = ((1,), (1,))
NN = ((1,), (0,))
CHUNK = 384
STRIP = 128
VMEM_MOST = 60 << 20
EVENTS = {
    "block": {(1, 0): ((1, 0), (1, 1), (0, 2), (2, 0), (0, 3), (3, 0), (2, 1), (1, 2), (3, 1)), (2, 0): ((2, 3), (3, 2))},
    "project": {},
    "attend": {(0, 1): ((0, 0),), (1, 1): ((1, 3), (0, 5)), (1, 2): ((2, 2), (0, 4)), (2, 0): ((0, 7), (3, 3)), (2, 1): ((1, 5),), (3, 0): ((0, 6),), (3, 1): ((1, 7), (1, 4)), (3, 2): ((2, 5),)},
    "turn": {(0, 0): ((0, 1),)},
    "norm": {(0, 0): ((3, 5), (1, 6), (0, 8))},
    "feed": {},
    "middle": {},
    "expand": {(0, 0): ((2, 7),), (0, 1): ((2, 4),), (1, 0): ((3, 7),), (1, 1): ((3, 4), (1, 8), (2, 6)), (2, 1): ((3, 6), (2, 8)), (3, 1): ((3, 8),)},
    "shrink": {},
}


def half(n, tokens):
    return pl.ds(pl.multiple_of(n * (tokens // 2), 32), tokens // 2)


def square(whole, m, z):
    return whole[m, z].reshape(D, D)


def strip(s):
    return pl.ds(pl.multiple_of(s * STRIP, STRIP), STRIP)


def forward_kernel(fused, rows, length, *refs):
    n_sem = len(Gather.sems) if fused else 0
    x_in, cot_in, seg_ref, vec_in = refs[:4]
    n_in = 10 if fused else 6
    ins = refs[4:n_in]
    outs = refs[n_in : n_in + 13]
    (whole_out, qkv_out, ctx_out, prob_out, act_out, slope_out, normed_out, rstd_out, ds_out, turned_out, low_out,
     result_out, part_out) = outs
    rest = refs[n_in + 13 :]
    gather_sems, rest = rest[:n_sem], rest[n_sem:]
    (masks, whole, bias, biases, joint, vec, x, cot, qkv, ctx, prob, act, slope, mixed, normed, rstd, low, turned,
     result, part, in_sem, w_sem, qkv_sem, ctx_sem, prob_sem, act_sem, slope_sem, end_sem) = rest
    tokens = rows * length
    strips = tokens // STRIP
    heads = D // HEAD // 4
    width = heads * HEAD
    z_own = lax.axis_index("mp")
    x_copy = pltpu.make_async_copy(x_in, x, in_sem.at[0])
    cot_copy = pltpu.make_async_copy(cot_in, cot, in_sem.at[1])
    x_copy.start()
    if fused:
        triple_in, output_in, e_ref, s_ref, qv_ref, eb_ref = ins
        joint_copies = [
            pltpu.make_async_copy(triple_in.at[j], joint.at[pl.ds(j * width, width)], in_sem.at[2 + j]) for j in range(3)
        ] + [pltpu.make_async_copy(output_in, joint.at[pl.ds(3 * width, width)], in_sem.at[5])]
        for copy in joint_copies:
            copy.start()
        gather = Gather((e_ref, s_ref), whole, bias, biases, gather_sems)
        gather.begin()
        bias[...] = jnp.zeros_like(bias)
        for h in range(heads):
            for j in (0, 1):
                at = slice(2 * j * width + h * HEAD, 2 * j * width + (h + 1) * HEAD)
                bias[0:1, at] = qv_ref[h, j : j + 1, :].astype(F32)
        for b in range(D // HEAD):
            bias[1:2, b * HEAD : (b + 1) * HEAD] = eb_ref[b : b + 1, :].astype(F32)
        for copy in joint_copies:
            copy.wait()
        for j in (0, 1):
            columns = joint[:, j * CHUNK : (j + 1) * CHUNK].T
            whole[0, z_own, 2 * j : 2 * j + 2] = columns.reshape(2, 2, SLICE, D)
        gather.begin_first()
        gather.local(1).start()
        gather.local(2).start()
        own_bias = pltpu.make_async_copy(bias, biases.at[z_own], w_sem.at[0])
        own_bias.start()
        own_bias.wait()
    else:
        copy = pltpu.make_async_copy(ins[0], whole, w_sem.at[0])
        copy.start()
        small = pltpu.make_async_copy(ins[1], biases, w_sem.at[1])
        small.start()
        copy.wait()
        small.wait()
    cot_copy.start()
    vec[0:6, :] = vec_in[...].astype(F32)

    def block(i):
        return crossed(z_own, i)

    def turned_copy(slot):
        return pltpu.make_async_copy(turned.at[slot], turned_out.at[slot], end_sem.at[slot])

    def qkv_copy(i):
        return pltpu.make_async_copy(qkv.at[i % 2], qkv_out.at[block(i)], qkv_sem.at[i % 2])

    def ctx_copy(i):
        return pltpu.make_async_copy(ctx.at[i % 2], ctx_out.at[block(i)], ctx_sem.at[i % 2])

    def prob_copy(i, r):
        return pltpu.make_async_copy(prob.at[r], prob_out.at[block(i), r], prob_sem.at[r])

    def act_copy(i):
        return pltpu.make_async_copy(act.at[i % 2], act_out.at[block(i)], act_sem.at[i % 2])

    def slope_copy(i):
        return pltpu.make_async_copy(slope.at[i % 2], slope_out.at[block(i)], slope_sem.at[i % 2])

    def whole_copy(m):
        return pltpu.make_async_copy(whole.at[m], whole_out.at[m], w_sem.at[m])

    def events(place, i=0, n=0):
        for (a, b), due in EVENTS[place].items() if fused else ():

            @pl.when((i == a) & (n == b))
            def _(due=due):
                for kind, step in due:
                    gather.run(kind, step)

    @pl.loop(0, rows)
    def _(r):
        pair = seg_ref[pl.ds(z_own * rows + r, 1), :]
        number = lax.broadcasted_iota(jnp.int32, (8, length), 0)
        among = jnp.where(number == pair, 1.0, 0.0).astype(BF)
        masks[r] = (mm(among, among, TN) - 1.0) * -MASKED

    x_copy.wait()

    @pl.loop(0, 4)
    def _(i):
        events("block", i)
        z = block(i)
        slot = i % 2

        @pl.when(i >= 2)
        def _():
            qkv_copy(i - 2).wait()
            ctx_copy(i - 2).wait()

        @pl.loop(0, 2)
        def _(n):
            at = half(n, tokens)
            qkv[slot, at, :] = (mm(x[at, :], square(whole, 0, z), NN) + biases[z, 0:1, :]).astype(BF)
            events("project", i, n)

        qkv_copy(i).start()

        @pl.loop(0, rows)
        def _(r):
            at = pl.ds(pl.multiple_of(r * length, 32), length)
            pl.when(i >= 1)(lambda: prob_copy(i - 1, r).wait())
            mask = masks[r]

            def part_of(j, h):
                return qkv[slot, at, j * width + h * HEAD : j * width + (h + 1) * HEAD]

            scale = jnp.asarray(HEAD ** (-0.5), BF)
            scores = [mm(part_of(1, h), part_of(0, h) * scale, NT) + mask for h in range(heads)]
            probs = []
            for h in range(heads):
                weights = jnp.exp(scores[h] - jnp.max(scores[h], axis=0, keepdims=True))
                share = 1.0 / jnp.sum(weights, axis=0, keepdims=True)
                probs.append((weights * share).astype(BF))
            for h in range(heads):
                prob[r, h] = probs[h]
            done = [mm(part_of(2, h), probs[h], TN).astype(BF) for h in range(heads)]
            ctx[slot, at, :] = jnp.concatenate(done, axis=0).T
            prob_copy(i, r).start()
            events("attend", i, r)

        ctx_copy(i).start()

        @pl.when(i == 0)
        def _():
            @pl.loop(0, strips)
            def _(s):
                value = x[strip(s), :]
                mixed[strip(s), :] = value.astype(F32) + vec[2:3, :]
                turned[0, :, strip(s)] = value.T

            turned_copy(0).start()
            events("turn")

        @pl.loop(0, tokens // CHUNK)
        def _(c):
            at = pl.ds(pl.multiple_of(c * CHUNK, CHUNK), CHUNK)
            add = mm(ctx[slot, at, :], square(whole, 0, z)[:, 3 * width :], NT)
            mixed[at, :] = mixed[at, :] + add

    whole_copy(0).start()

    @pl.loop(0, strips)
    def _(s):
        at = strip(s)
        hidden, normal, scale = norm_forward(mixed[at, :], vec[0:1, :], vec[1:2, :])
        normed[at, :] = normal
        rstd[at, :] = jnp.broadcast_to(scale, (STRIP, 128))
        mixed[at, :] = hidden + vec[5:6, :]
        hidden = hidden.astype(BF)
        low[at, :] = hidden
        turned[1, :, at] = hidden.T

    events("norm")
    turned_copy(1).start()
    normed_copy = pltpu.make_async_copy(normed, normed_out, end_sem.at[3])
    normed_copy.start()
    rstd_copy = pltpu.make_async_copy(rstd, rstd_out, end_sem.at[4])
    rstd_copy.start()
    if fused:
        gather.local(1).wait()
        gather.local(2).wait()

    @pl.loop(0, 4)
    def _(i):
        events("feed", i)
        z = block(i)
        slot = i % 2

        @pl.when(i >= 2)
        def _():
            act_copy(i - 2).wait()
            slope_copy(i - 2).wait()

        @pl.loop(0, 2)
        def _(n):
            at = half(n, tokens)
            u = mm(low[at, :], square(whole, 1, z), NN) + biases[z, 1:2, :]
            cumulative = 0.5 + 0.5 * lax.erf(u * SQRT_HALF)
            act[slot, at, :] = (u * cumulative).astype(BF)
            slope[slot, at, :] = (cumulative + u * jnp.exp(-0.5 * u * u) * INV_ROOT_TAU).astype(BF)
            events("expand", i, n)

        act_copy(i).start()
        slope_copy(i).start()
        events("middle", i)
        for m in (1, 2):
            pltpu.make_async_copy(whole.at[m, z], whole_out.at[m, z], w_sem.at[m]).start()

        @pl.loop(0, 2)
        def _(n):
            at = half(n, tokens)
            mixed[at, :] = mixed[at, :] + mm(act[slot, at, :], square(whole, 2, z), NN)
            events("shrink", i, n)

    normed_copy.wait()
    cot_copy.wait()
    part[...] = jnp.zeros_like(part)

    @pl.loop(0, strips)
    def _(s):
        at = strip(s)
        block_result, normal, scale = norm_forward(mixed[at, :], vec[3:4, :], vec[4:5, :])
        result[at, :] = block_result.astype(BF)
        back = cot[at, :].astype(F32)
        dsummed = norm_backward(back, vec[3:4, :], normal, scale)
        normed[at, :] = dsummed
        dsummed_low = dsummed.astype(BF)
        low[at, :] = dsummed_low
        turned[2, :, at] = dsummed_low.T
        part[3:4, :] += jnp.sum(back * normal, axis=0, keepdims=True)
        part[4:5, :] += jnp.sum(back, axis=0, keepdims=True)
        part[5:6, :] += jnp.sum(dsummed, axis=0, keepdims=True)
        pltpu.make_async_copy(normed.at[at], ds_out.at[at], end_sem.at[5]).start()
        pltpu.make_async_copy(result.at[at], result_out.at[at], end_sem.at[6]).start()
        pltpu.make_async_copy(low.at[at], low_out.at[at], end_sem.at[8]).start()

    last = [
        turned_copy(2),
        pltpu.make_async_copy(part, part_out, end_sem.at[7]),
    ]
    for copy in last:
        copy.start()
    last = last + [
        pltpu.make_async_copy(normed, ds_out, end_sem.at[5]),
        pltpu.make_async_copy(result, result_out, end_sem.at[6]),
        pltpu.make_async_copy(low, low_out, end_sem.at[8]),
    ]
    for i in (2, 3):
        qkv_copy(i).wait()
        ctx_copy(i).wait()
        act_copy(i).wait()
        slope_copy(i).wait()
    for r in range(rows):
        prob_copy(3, r).wait()
    turned_copy(0).wait()
    turned_copy(1).wait()
    rstd_copy.wait()
    for m in range(3):
        whole_copy(m).wait()
    for copy in last:
        copy.wait()
    if fused:
        gather.finish()


def run_forward(x, cot, segments, vector_params, weights, biases):
    rows, length, _ = x.shape
    tokens = rows * length
    fused = lax.axis_size("dp") == 8 and lax.axis_size("mp") == 4
    hbm, vmem = pl.BlockSpec(memory_space=pl.ANY), pl.BlockSpec(memory_space=pltpu.VMEM)
    flat = (tokens, D)
    width = D // 4
    block = (4, 2, SLICE, D)
    dense = [x.reshape(flat), cot.reshape(flat), segments, vector_params]
    if fused:
        triple, output, expand, shrink = weights
        held = [triple.transpose(0, 2, 1), output, expand.reshape(block), shrink.reshape(block)]
        held = held + [biases[0].transpose(1, 0, 2), biases[1]]
        spaces = [hbm, hbm, hbm, hbm, vmem, vmem]
    else:
        mats = pack_weights(*weights)
        held = [jnp.stack([lax.all_gather(m, "mp", axis=0) for m in mats]).reshape((3, 4) + block)]
        held = held + [lax.all_gather(pack_biases(*biases), "mp", axis=0)]
        spaces = [hbm, hbm]
    probs = (rows, D // HEAD // 4, length, length)
    shape = jax.ShapeDtypeStruct
    dma = pltpu.SemaphoreType.DMA
    return pl.pallas_call(
        functools.partial(forward_kernel, fused, rows, length),
        out_shape=(
            shape((3, 4) + block, BF),
            shape((4,) + flat, BF),
            shape((4, tokens, width), BF),
            shape((4,) + probs, BF),
            shape((4,) + flat, BF),
            shape((4,) + flat, BF),
            shape(flat, F32),
            shape((tokens, 128), F32),
            shape(flat, F32),
            shape((3, D, tokens), BF),
            shape(flat, BF),
            shape(flat, BF),
            shape((VECTORS, D), F32),
        ),
        in_specs=[hbm, hbm, vmem, vmem] + spaces,
        out_specs=(hbm,) * 13,
        scratch_shapes=([dma(s) for s in Gather.sems] if fused else [])
        + [
            pltpu.VMEM((rows, length, length), F32),
            pltpu.VMEM((3, 4) + block, BF),
            pltpu.VMEM((VECTORS, D), F32),
            pltpu.VMEM((4, VECTORS, D), F32),
            pltpu.VMEM((D, D), BF),
            pltpu.VMEM((VECTORS, D), F32),
            pltpu.VMEM(flat, BF),
            pltpu.VMEM(flat, BF),
            pltpu.VMEM((2,) + flat, BF),
            pltpu.VMEM((2, tokens, width), BF),
            pltpu.VMEM(probs, BF),
            pltpu.VMEM((2,) + flat, BF),
            pltpu.VMEM((2,) + flat, BF),
            pltpu.VMEM(flat, F32),
            pltpu.VMEM(flat, F32),
            pltpu.VMEM((tokens, 128), F32),
            pltpu.VMEM(flat, BF),
            pltpu.VMEM((3, D, tokens), BF),
            pltpu.VMEM(flat, BF),
            pltpu.VMEM((VECTORS, D), F32),
            dma((6,)),
            dma((3,)),
            dma((2,)),
            dma((2,)),
            dma((rows,)),
            dma((2,)),
            dma((2,)),
            dma((9,)),
        ],
        compiler_params=pltpu.CompilerParams(
            collective_id=0 if fused else None, has_side_effects=True, vmem_limit_bytes=VMEM_MOST
        ),
        name="forward",
    )(*dense, *held)


BACK_EVENTS = {
    "shrink": {(0, 0): ((0, 0),), (1, 0): ((0, 2),), (2, 0): ((0, 4), (2, 1), (1, 3)), (3, 0): ((0, 6), (1, 5))},
    "slope": {(1, 0): ((1, 1),), (1, 1): ((2, 0),), (2, 0): ((3, 0),), (3, 0): ((2, 3),)},
    "expand": {(0, 0): ((0, 1), (1, 0)), (1, 0): ((0, 3), (1, 2)), (2, 0): ((0, 5), (1, 4), (2, 2)), (3, 0): ((0, 7), (1, 6), (2, 4))},
    "hidden": {(2, 0): ((3, 1),), (3, 1): ((3, 2),)},
    "norm": {(0, 0): ((1, 7), (2, 5))},
    "attend": {(0, 0): ((3, 3),), (0, 2): ((2, 6),), (0, 3): ((3, 4),), (1, 0): ((3, 5),), (1, 1): ((1, 8), (3, 6)), (1, 2): ((3, 7),), (2, 0): ((2, 8),), (2, 2): ((1, 9),), (2, 3): ((3, 8),), (3, 1): ((2, 9),), (3, 2): ((1, 10),)},
    "project": {(0, 0): ((0, 8),), (1, 0): ((0, 9),), (2, 0): ((0, 10),), (3, 0): ((0, 11), (3, 9))},
    "pull": {(0, 0): ((2, 7),), (2, 0): ((2, 10),), (3, 0): ((1, 11),)},
    "last": {(0, 0): ((3, 10), (2, 11), (3, 11))},
}


def turn_block(j):
    return 3 * j % 4


def backward_kernel(fused, rows, length, *refs):
    n_sem = len(Scatter.sems) if fused else 0
    n_buf = len(Scatter.buffers) if fused else 0
    (vec_in, part_in, whole, qkv_in, ctx_in, prob_in, act_in, slope_in, normed_in, rstd_in, ds_in, turned_in,
     low_in) = refs[:13]
    grad_out, small_out, input_out = refs[13:16]
    rest = refs[16:]
    buffers, sems, rest = rest[:n_buf], rest[n_buf : n_buf + n_sem], rest[n_buf + n_sem :]
    (grads, weights, wide, tall, stream, normed, rstd, low, turned, prob, ctx, dctx, part, vec,
     w_sem, wide_sem, tall_sem, prob_sem, ctx_sem, turned_sem, end_sem) = rest
    tokens = rows * length
    strips = tokens // STRIP
    heads = D // HEAD // 4
    width = heads * HEAD

    def weight_copy(m, j, slot):
        return pltpu.make_async_copy(whole.at[m, turn_block(j)], weights.at[slot], w_sem.at[slot])

    def wide_copy(source, j):
        return pltpu.make_async_copy(source.at[turn_block(j)], wide.at[j % 2], wide_sem.at[j % 2])

    def tall_copy(j):
        return pltpu.make_async_copy(slope_in.at[turn_block(j)], tall.at[j % 2], tall_sem.at[j % 2])

    def turned_copy(source, slot):
        return pltpu.make_async_copy(turned_in.at[source], turned.at[slot], turned_sem.at[slot])

    def prob_copy(g):
        return pltpu.make_async_copy(prob_in.at[turn_block(g // rows), g % rows], prob.at[g % 2], prob_sem.at[g % 2])

    def ctx_copy(j):
        return pltpu.make_async_copy(ctx_in.at[turn_block(j)], ctx.at[j % 2], ctx_sem.at[j % 2])

    stream_copy = pltpu.make_async_copy(ds_in, stream, end_sem.at[0])
    normed_copy = pltpu.make_async_copy(normed_in, normed, end_sem.at[1])
    rstd_copy = pltpu.make_async_copy(rstd_in, rstd, end_sem.at[2])
    low_copy = pltpu.make_async_copy(low_in, low, end_sem.at[4])
    for t in range(PIECES):
        for source, target, sem in ((turned_in.at[2], turned.at[0], turned_sem), (act_in.at[0], wide.at[0], wide_sem)):
            at = pl.ds(t * (source.shape[0] // PIECES), source.shape[0] // PIECES)
            pltpu.make_async_copy(source.at[at], target.at[at], sem.at[0]).start()
    weight_copy(2, 0, 0).start()
    low_copy.start()
    tall_copy(0).start()
    turned_copy(1, 1).start()
    weight_copy(1, 0, 1).start()
    stream_copy.start()
    wide_copy(act_in, 1).start()
    tall_copy(1).start()
    weight_copy(2, 1, 2).start()
    weight_copy(1, 1, 3).start()
    normed_copy.start()
    rstd_copy.start()
    if fused:
        scatter = Scatter(grads, buffers, sems)
        scatter.begin()

    def events(place, j=0, n=0):
        for (a, c), due in BACK_EVENTS[place].items() if fused else ():

            @pl.when((j == a) & (n == c))
            def _(due=due):
                for kind, step in due:
                    scatter.run(kind, step)

    vec[0:6, :] = vec_in[...].astype(F32)
    part[...] = jnp.zeros_like(part)
    part[0:VECTORS, :] = part_in[...]

    def outer(slot, turned_slot, right, offset=0):
        product = mm(turned[turned_slot], right, NN).astype(BF)
        count = product.shape[1]
        grads[slot, :, :, :, offset : offset + count] = product.reshape(4, 2, SLICE, count)

    def emit(slot, m, z):
        if not fused:
            copy = pltpu.make_async_copy(grads.at[slot], grad_out.at[m, z], end_sem.at[3])
            copy.start()
            copy.wait()

    turned_copy(2, 0).wait()

    @pl.loop(0, 4)
    def _(j):
        parity = j % 2
        slot = 2 * parity
        z = turn_block(j)
        wide_copy(act_in, j).wait()

        outer(j, 0, wide[parity])
        events("shrink", j)
        emit(j, 2, z)

        @pl.when(j == 0)
        def _():
            low_copy.wait()
            turned_copy(1, 1).wait()
            stream_copy.wait()

        weight_copy(2, j, slot).wait()
        tall_copy(j).wait()

        @pl.loop(0, 2)
        def _(n):
            at = half(n, tokens)
            dactive = mm(low[at, :], weights[slot], NT)
            value = (dactive * tall[parity, at, :].astype(F32)).astype(BF)
            tall[2, at, :] = value
            line = pl.ds(10 + z, 1)
            part[line, :] = part[line, :] + jnp.sum(value.astype(F32), axis=0, keepdims=True)
            events("slope", j, n)

        outer(4 + j, 1, tall[2])
        events("expand", j)
        emit(4 + j, 1, z)
        weight_copy(1, j, slot + 1).wait()

        @pl.loop(0, 2)
        def _(n):
            at = half(n, tokens)
            stream[at, :] = stream[at, :] + mm(tall[2, at, :], weights[slot + 1], NT)
            events("hidden", j, n)

        @pl.when(j < 2)
        def _():
            wide_copy(act_in, j + 2).start()
            tall_copy(j + 2).start()
            weight_copy(2, j + 2, slot).start()
            weight_copy(1, j + 2, slot + 1).start()

        @pl.when(j == 2)
        def _():
            wide_copy(qkv_in, 0).start()
            weight_copy(0, 0, 0).start()
            weight_copy(0, 1, 1).start()
            ctx_copy(0).start()
            ctx_copy(1).start()
            prob_copy(0).start()

        @pl.when(j == 3)
        def _():
            wide_copy(qkv_in, 1).start()
            weight_copy(0, 2, 2).start()
            weight_copy(0, 3, 3).start()
            turned_copy(0, 0).start()

    normed_copy.wait()
    rstd_copy.wait()

    @pl.loop(0, strips)
    def _(s):
        at = strip(s)
        dhidden, normal = stream[at, :], normed[at, :]
        dmixed = norm_backward(dhidden, vec[0:1, :], normal, rstd[at, 0:1])
        part[0:1, :] += jnp.sum(dhidden * normal, axis=0, keepdims=True)
        part[1:2, :] += jnp.sum(dhidden, axis=0, keepdims=True)
        part[2:3, :] += jnp.sum(dmixed, axis=0, keepdims=True)
        stream[at, :] = dmixed
        dmixed = dmixed.astype(BF)
        low[at, :] = dmixed
        turned[1, :, at] = dmixed.T

    events("norm")
    turned_copy(0, 0).wait()
    dproj = tall

    def pull(j):
        @pl.loop(0, 2)
        def _(n):
            at = half(n, tokens)
            stream[at, :] = stream[at, :] + mm(dproj[j % 3, at, 0 : 3 * width], weights[j, :, 0 : 3 * width], NT)
            events("pull", j, n)

    @pl.loop(0, 4)
    def _(j):
        parity = j % 2
        z = turn_block(j)
        weight_copy(0, j, j).wait()
        wide_copy(qkv_in, j).wait()
        ctx_copy(j).wait()
        dctx[...] = mm(low[...], weights[j, :, 3 * width :], NN).astype(BF)

        @pl.loop(0, rows)
        def _(r):
            at = pl.ds(pl.multiple_of(r * length, 32), length)
            g = j * rows + r
            prob_copy(g).wait()
            pl.when(g + 1 < 4 * rows)(lambda: prob_copy(g + 1).start())
            scale = jnp.asarray(HEAD ** (-0.5), BF)

            def part_of(i, h):
                return wide[parity, at, i * width + h * HEAD : i * width + (h + 1) * HEAD]

            def dc(h):
                return dctx[at, h * HEAD : (h + 1) * HEAD]

            dprobs = [mm(part_of(2, h), dc(h), NT) for h in range(heads)]
            dscores = []
            for h in range(heads):
                full = prob[g % 2, h].astype(F32)
                inner = jnp.sum(full * dprobs[h], axis=0, keepdims=True)
                dscores.append((full * (dprobs[h] - inner)).astype(BF))
            dv = [mm(prob[g % 2, h], dc(h), NN).astype(BF) for h in range(heads)]
            dk = [mm(dscores[h], part_of(0, h) * scale, NN).astype(BF) for h in range(heads)]
            dq = [(mm(part_of(1, h), dscores[h], TN) * HEAD ** (-0.5)).astype(BF) for h in range(heads)]
            dq = [jnp.concatenate(dq, axis=0).T]
            joined = jnp.concatenate(dq + dk + dv, axis=1)
            dproj[j % 3, at, 0 : 3 * width] = joined
            line = pl.ds(6 + z, 1)
            before = jnp.where(r == 0, 0.0, part[line, 0 : 3 * width])
            part[line, 0 : 3 * width] = before + jnp.sum(joined.astype(F32), axis=0, keepdims=True)
            events("attend", j, r)

        if fused:
            for k in range(4):
                pl.when(j == k)(lambda k=k: scatter.to_core(2 * k).wait_send())
            pl.when(j == 3)(lambda: scatter.small_stage(part, 0))

        outer(j, 0, dproj[j % 3, :, 0 : 3 * width])
        outer(j, 1, ctx[parity], 3 * width)
        emit(j, 0, z)
        events("project", j)

        @pl.when(j < 2)
        def _():
            wide_copy(qkv_in, j + 2).start()
            ctx_copy(j + 2).start()

        pl.when(j == 0)(lambda: pull(j))

    pull(1)
    if fused:
        scatter.small_stage(part, 1)
    pull(2)
    if fused:
        scatter.small_stage(part, 2)
    pull(3)
    input_copy = pltpu.make_async_copy(stream, input_out, end_sem.at[0])
    input_copy.start()
    if fused:
        events("last")
        scatter.small_stage(part, 3)
        grad_out[2] = scatter.total(2)
        grad_out[1] = scatter.total(1)
        small_out[...] = scatter.small_stage(part, 4)
        grad_out[0] = scatter.total(0)
        scatter.finish(part)
    else:
        small_out[...] = part[...]
    input_copy.wait()


def run_backward(vector_params, part, saved, rows, length):
    fused = lax.axis_size("dp") == 8 and lax.axis_size("mp") == 4
    hbm, vmem = pl.BlockSpec(memory_space=pl.ANY), pl.BlockSpec(memory_space=pltpu.VMEM)
    tokens = rows * length
    flat = (tokens, D)
    width = D // 4
    block = (4, 2, SLICE, D)
    shape = jax.ShapeDtypeStruct
    dma = pltpu.SemaphoreType.DMA
    whole_grad = shape((3, SLICE, D), F32) if fused else shape((3, 4) + block, BF)
    saved = [saved[0].reshape(3, 4, D, D)] + list(saved[1:])
    grads, sums, input_grad = pl.pallas_call(
        functools.partial(backward_kernel, fused, rows, length),
        out_shape=(whole_grad, shape((SMALL, D), F32), shape(flat, F32)),
        in_specs=[vmem] * 2 + [hbm] * 11,
        out_specs=(vmem if fused else hbm, vmem, hbm),
        scratch_shapes=([pltpu.VMEM(s, t) for s, t in Scatter.buffers] + [dma(s) for s in Scatter.sems] if fused else [])
        + [
            pltpu.VMEM((8,) + block, BF),
            pltpu.VMEM((4, D, D), BF),
            pltpu.VMEM((2,) + flat, BF),
            pltpu.VMEM((3,) + flat, BF),
            pltpu.VMEM(flat, F32),
            pltpu.VMEM(flat, F32),
            pltpu.VMEM((tokens, 128), F32),
            pltpu.VMEM(flat, BF),
            pltpu.VMEM((2, D, tokens), BF),
            pltpu.VMEM((2, D // HEAD // 4, length, length), BF),
            pltpu.VMEM((2, tokens, width), BF),
            pltpu.VMEM((tokens, width), BF),
            pltpu.VMEM((SMALL, D), F32),
            pltpu.VMEM((VECTORS, D), F32),
            dma((4,)),
            dma((2,)),
            dma((2,)),
            dma((2,)),
            dma((2,)),
            dma((2,)),
            dma((5,)),
        ],
        compiler_params=pltpu.CompilerParams(
            collective_id=1 if fused else None, has_side_effects=True, vmem_limit_bytes=VMEM_MOST
        ),
        name="backward",
    )(vector_params, part, *saved)
    if not fused:
        parts = lax.axis_size("dp")
        grads = lax.psum_scatter(grads.reshape(3, 4, D, D), "dp", scatter_dimension=2, tiled=True)
        grads = lax.psum_scatter(grads, "mp", scatter_dimension=1, tiled=True)
        grads = grads.reshape(3, D // parts, D).astype(F32)
        sums = lax.psum(sums, ("dp", "mp"))
    return input_grad, grads, sums


RATES = (D ** (-0.5), 0.5, (D // 16) ** (-0.5), D ** (-0.5), 0.5, FF ** (-0.5), 0.3)


LARGE = (3, 5, 0, 2)
PIECES = 4


def update_kernel(reduced, sums, result_in, input_in, *refs):
    state, outs = list(refs[:21]), list(refs[21:49])
    result_out, input_out, result, input_grad = refs[49:53]
    held, load_sem, store_sem, sems = refs[53:81], *refs[81:]
    piece = input_in.shape[0] // PIECES
    moves = []
    for t in range(PIECES):
        at = pl.ds(t * piece, piece)
        for j, (source, middle, target) in enumerate(((input_in, input_grad, input_out), (result_in, result, result_out))):
            moves.append((
                pltpu.make_async_copy(source.at[at], middle.at[at], sems.at[2 * j, t]),
                pltpu.make_async_copy(middle.at[at], target.at[at], sems.at[2 * j + 1, t]),
            ))
    loads, stores = {}, {}
    for t, i in enumerate(LARGE):
        mine = held[7 * t : 7 * t + 7]
        loads[i] = [pltpu.make_async_copy(state[3 * i + j], mine[j], load_sem.at[t, j]) for j in range(3)]
        stores[i] = [pltpu.make_async_copy(mine[3 + j], outs[4 * i + j], store_sem.at[t, j]) for j in range(4)]
        state[3 * i : 3 * i + 3] = mine[:3]
        outs[4 * i : 4 * i + 4] = mine[3:]
    for copy in loads[3]:
        copy.start()
    for load, _ in moves:
        load.start()
    for i in LARGE[1:]:
        for copy in loads[i]:
            copy.start()
    dp, mp = lax.axis_index("dp"), lax.axis_index("mp")
    groups = lax.axis_size("mp")
    width = D // groups
    own = width // HEAD

    def update(i, gradient, at=Ellipsis):
        new = adam_update(*(state[3 * i + j][at] for j in range(3)), gradient, RATES[i])
        for j in range(4):
            outs[4 * i + j][at] = new[j]

    def wait(copies):
        for copy in copies:
            copy.wait()

    def start(copies):
        for copy in copies:
            copy.start()

    wait(loads[3])
    update(3, reduced[1])
    start(stores[3])
    for load, store in moves:
        load.wait()
        store.start()
    wait(loads[5])
    update(5, reduced[2])
    start(stores[5])
    wait(loads[0])
    mixing = reduced[0]
    for j in range(3):
        update(0, mixing[:, j * width : (j + 1) * width], j)
    start(stores[0])
    wait(loads[2])
    update(2, mixing[:, 3 * width :].T)
    start(stores[2])

    def lanes(row, count, first):
        return pltpu.roll(sums[pl.ds(row, count), :], lax.rem(D - first, D), 1)

    piece = state[3].shape[2]
    moved = lanes(6 + mp, 1, dp * piece)
    for j in (0, 1):
        for h in range(own):
            at = 2 * j * width + h * HEAD
            update(1, moved[:, at : at + piece], (h, slice(j, j + 1)))
    piece = state[12].shape[0]
    moved = lanes(10 + mp, 1, dp * piece)
    blocks = [moved[:, b * HEAD : b * HEAD + piece] for b in range(D // HEAD)]
    update(4, jnp.concatenate(blocks, axis=0).T)
    piece = state[18].shape[1]
    update(6, lanes(0, 8, (dp * groups + mp) * piece)[0:6, 0:piece])
    for i in LARGE:
        wait(stores[i])
    for _, store in moves:
        store.wait()


AXES = ((0, 1, 2), (1, 0, 2), (0, 1), (0, 1), (1, 0), (1, 0), (0, 1))


def update_all(state, reduced, sums, result, input_grad):
    hbm, vmem = pl.BlockSpec(memory_space=pl.ANY), pl.BlockSpec(memory_space=pltpu.VMEM)
    state = [s.transpose(AXES[i // 3]) for i, s in enumerate(state)]
    shapes = []
    for i in range(7):
        shapes = shapes + [jax.ShapeDtypeStruct(state[3 * i].shape, t) for t in (F32, F32, F32, BF)]
    kept = [jax.ShapeDtypeStruct(a.shape, a.dtype) for a in (result, input_grad)]
    held = []
    for i in LARGE:
        held = held + [pltpu.VMEM(state[3 * i].shape, t) for t in (F32,) * 6 + (BF,)]
    dma = pltpu.SemaphoreType.DMA
    state_specs = [hbm if i // 3 in LARGE else vmem for i in range(21)]
    new_specs = [hbm if i // 4 in LARGE else vmem for i in range(28)]
    *new, result, input_grad = pl.pallas_call(
        update_kernel,
        out_shape=tuple(shapes + kept),
        in_specs=[vmem] * 2 + [hbm] * 2 + state_specs,
        out_specs=tuple(new_specs) + (hbm,) * 2,
        scratch_shapes=[pltpu.VMEM(a.shape, a.dtype) for a in kept] + held + [dma((4, 3)), dma((4, 4)), dma((4, PIECES))],
        name="update",
    )(reduced, sums, result, input_grad, *state)
    return result, input_grad, tuple(s.transpose(AXES[i // 4]) for i, s in enumerate(new))


def per_device(
    activations,
    cotangent,
    segments,
    triple_weight,
    query_value_bias,
    output_weight,
    expand_weight,
    expand_bias,
    shrink_weight,
    vector_params,
    *state,
):
    rows, length, _ = activations.shape
    weights = (triple_weight, output_weight, expand_weight, shrink_weight)
    *saved, result, part = run_forward(
        activations, cotangent, segments, vector_params, weights, (query_value_bias, expand_bias)
    )
    input_grad, reduced, sums = run_backward(vector_params, part, saved, rows, length)
    result, input_grad, new = update_all(state, reduced, sums, result, input_grad)
    return (result.reshape(activations.shape), input_grad.reshape(activations.shape)) + new


STATE_SPECS = (
    P(None, "dp", "mp"),
    P(None, "mp", "dp"),
    P("mp", "dp"),
    P("dp", "mp"),
    P("mp", "dp"),
    P("mp", "dp"),
    P(None, ("dp", "mp")),
)


def solution(mesh):
    rows = P(("dp", "mp"), None, None)
    placed = (
        rows,
        rows,
        P("dp", None),
        P(None, None, "mp"),
        P(None, "mp", None),
        P("mp", None),
        P(None, "mp"),
        P("mp", None),
        P("mp", None),
        P(),
    )
    for spec in STATE_SPECS:
        placed = placed + (spec,) * 3
    out_specs = (rows, rows)
    for spec in STATE_SPECS:
        out_specs = out_specs + (spec,) * 4
    return jax.shard_map(per_device, mesh=mesh, in_specs=placed, out_specs=out_specs, check_vma=False)
```
